128 devices in a mesh: dom: 8 (over z, core), wide: 16 (over x, y).
Axes of the slice: x: 4, y: 4, z: 4, core: 2. Of those that a mesh axis runs over, the one named last changes fastest.
Arguments:
- embeddings: float32 [16384, 1024], P(('dom', 'wide')), may hold values from -1 to 3
- domain_ids: int32 [16384, 1], P(('dom', 'wide')), may hold values from 0 to 7; in each aligned block of 128 rows (0 to 127, 128 to 255, ...) at most 32 rows name the same one
- order: int32 [128, 128], P(('dom', 'wide')), may hold values from 0 to 127, each once within a row
Outputs:
- whitened_rows: float32 [16384, 1024], P(('dom', 'wide'))
The draws below stay inside these ranges and needn't reach their ends.
Inputs may be any that keep to these rules, and one draw needn't show every extreme that they name: `domain_ids`: among the rows of one device at most 32 name one domain; every domain is named by some row. Each row of order is a permutation.
All inputs are finite; a program needn't handle non-finite values.
Results may differ from the reference program's by a relative error of at most 0.0003.
Values sent between devices are 32-bit elements; how exact they have to be, the bound alone decides.
No kernel may reach another device: no remote copies, remote signals or barrier semaphores. Data moves between devices by JAX's collectives and lax.ppermute only.
A program may use at most 64 MiB of HBM per device.

```python
import math
import jax
import jax.numpy as jnp
import numpy as np
from jax import lax

F = 1024
ROW_DEV = 128
DOMAINS = 8
MOST = 32
SHARDS = 128
ROWS = 16384


def block_scale(key, extent, pieces, smallest, top_value):
    def one(position, blocks):
        draws = jax.random.uniform(jax.random.fold_in(jax.random.fold_in(key, 6), position), (blocks,), jnp.float32, smallest / len(pieces), top_value / len(pieces))
        return jnp.repeat(jnp.exp(draws), extent[position] // blocks).reshape((-1,) + (1,) * (len(extent) - position - 1))

    gain = one(*pieces[0])
    for cut in pieces[1:]:
        gain = gain * one(*cut)
    return gain


def shared_out(stream_key, own, number, rows, number_of, top, limit, skew):
    sequence = jax.random.permutation(stream_key, number_of)
    crowded, common = load_shares(number_of, rows * top, limit, skew, True), load_shares(number_of, rows * top, limit, skew, False)
    places = jnp.arange(number_of)

    def named(sizes, turn):
        used = int((sizes > 0).sum())
        fixed = max(1, used // 4)
        shifted = fixed + (places - fixed + turn * (used - fixed)) % max(1, number_of - fixed)
        return jnp.zeros((number_of,), jnp.int32).at[sequence[jnp.where(places < fixed, places, shifted)]].set(jnp.asarray(sizes, jnp.int32))

    sizes = jnp.where(number % 4 == 0, named(crowded, number // 4), named(common, number - number // 4 - 1))
    mixed = jax.random.permutation(jax.random.fold_in(own, 3), number_of)
    giver, sink = mixed[0:number_of // 2 * 2:2], mixed[1:number_of // 2 * 2:2]
    margin = jnp.minimum(sizes[giver] - 1, limit - sizes[sink]) // 2
    margin = jnp.where((giver == sequence[0]) | (sink == sequence[0]) | (sizes[sink] == 0), 0, jnp.maximum(margin, 0))
    shifted = jax.random.randint(jax.random.fold_in(own, 4), (number_of // 2,), 0, 1 << 20) % (margin + 1)
    sizes = sizes.at[giver].add(-shifted).at[sink].add(shifted)
    members = jnp.searchsorted(jnp.cumsum(sizes), jnp.arange(rows * top), side="right").astype(jnp.int32)
    listing = members.reshape(top, rows).T
    listing = listing[jax.random.permutation(jax.random.fold_in(own, 1), rows)]
    turn = jax.random.randint(jax.random.fold_in(own, 2), (rows, 1), 0, top)
    return jnp.take_along_axis(listing, (jnp.arange(top)[None, :] + turn) % top, axis=1)


def load_shares(number_of, total, bound, slope, full):
    loads = [(1 << 20) // math.isqrt(grade ** slope) + 1 for grade in range(1, number_of + 1)]
    largest = bound if full else min(bound, max(-(-total // number_of), total * loads[0] // sum(loads)))
    least = 1 if total - largest >= number_of - 1 else 0
    counts, surplus = [largest] + [least] * (number_of - 1), total - largest - least * (number_of - 1)
    while surplus > 0:
        free = [i for i in range(1, number_of) if counts[i] < largest] or [i for i in range(1, number_of) if counts[i] < bound]
        whole, left = sum([loads[i] for i in free]), surplus
        for i in free:
            extra = min(bound - counts[i], max(1, left * loads[i] // whole), surplus)
            counts[i] = counts[i] + extra
            surplus = surplus - extra
    return np.array(counts)


def setup_inputs(seed: int = 0) -> dict:
    keys = jax.random.split(jax.random.key(seed), 4)
    embeddings = jnp.clip(-1.0 + 4.0 * jax.random.uniform(keys[0], (ROWS, F), jnp.float32) ** block_scale(keys[0], (ROWS, F), ((0, 128),), -0.2, 0.2), -1.0, 3.0)
    domain_ids_keys = jax.random.split(jax.random.fold_in(keys[1], 1), ROWS // ROW_DEV)
    domain_ids_turns = jax.random.permutation(jax.random.fold_in(keys[1], 3), ROWS // ROW_DEV)
    domain_ids = jax.vmap(lambda own, number: shared_out(jax.random.fold_in(keys[1], 2), own, number, ROW_DEV, DOMAINS, 1, MOST, 1))(domain_ids_keys, domain_ids_turns).reshape((ROWS, 1))
    order = jax.vmap(lambda own: jax.random.permutation(own, ROW_DEV))(jax.random.split(keys[2], SHARDS)).reshape((SHARDS, ROW_DEV)).astype(jnp.int32)
    return {"embeddings": embeddings, "domain_ids": domain_ids, "order": order}


ridge_term = 0.1

def reference(embeddings, domain_ids, order):
    domain_of = domain_ids[:, 0]
    total = domain_of.shape[0]
    sorted_pos = jnp.argsort(domain_of, stable=True).astype(jnp.int32)
    onehot = (domain_of[:, None] == jnp.arange(DOMAINS, dtype=jnp.int32)[None, :]).astype(jnp.int32)
    counts_int = jnp.sum(onehot, axis=0).astype(jnp.int32)
    starts = (jnp.cumsum(counts_int) - counts_int).astype(jnp.int32)
    capacity = MOST * SHARDS

    def per_domain(output, domain):
        slots = jnp.arange(capacity, dtype=jnp.int32)
        live_mask = (slots < counts_int[domain]).astype(jnp.float32)
        index = sorted_pos[jnp.minimum(starts[domain] + slots, total - 1).astype(jnp.int32)]
        rows = embeddings[index] * live_mask[:, None]
        count = counts_int[domain].astype(jnp.float32)
        center = jnp.sum(rows, axis=0) / count
        centered = (rows - center[None, :]) * live_mask[:, None]
        gram = jnp.dot(centered.T.astype(jnp.float32), centered.astype(jnp.float32), precision=lax.Precision.HIGHEST, preferred_element_type=jnp.float32)
        covariance = gram / count + ridge_term * jnp.eye(F, dtype=jnp.float32)
        factor = jnp.linalg.cholesky(covariance)
        whitened = jax.scipy.linalg.solve_triangular(factor, (rows - center[None, :]).T, lower=True).T
        output = output.at[index].add(whitened * live_mask[:, None])
        return (output, None)
    whitened_all, _ = lax.scan(per_domain, jnp.zeros((total, F), jnp.float32), jnp.arange(DOMAINS, dtype=jnp.int32))
    shaped = whitened_all.reshape(SHARDS, ROW_DEV, F)
    return jnp.take_along_axis(shaped, order[:, :, None], axis=1).reshape(ROWS, F)
```

```python
import functools

import jax
import jax.numpy as jnp
from jax import lax
from jax.experimental import pallas as pl
from jax.experimental.pallas import tpu as pltpu
from jax.sharding import PartitionSpec as P

RIDGE = 0.1
SHIFT = 1.0
EMPTY = 1e30
B = 128
HIGHEST = lax.Precision.HIGHEST
AXES = ("dom", "wide")


PLACE = (0, 1, 1, 0)


def coords(n):
    d, w = divmod(n, 16)
    return [w // 4, w % 4, d // 2, d % 2]


def number(c):
    x, y, z, core = c
    return (z * 2 + core) * 16 + x * 4 + y


def domain_of_device(n):
    x, y, z, _ = coords(n)
    return (x // 2) * 4 + (y // 2) * 2 + z // 2


def toward(n, mask):
    c = coords(n)
    for axis, bit in ((0, 4), (1, 2), (2, 1)):
        if mask & bit:
            c[axis] = 3 - c[axis]
    return number(c)


def partner(n, axis):
    c = coords(n)
    c[axis] ^= 1
    return number(c)


def permute(x, to):
    return lax.ppermute(x, AXES, [(n, to(n)) for n in range(128)])


def dot(a, b, dims):
    return lax.dot_general(a, b, (dims, ((), ())), precision=HIGHEST, preferred_element_type=jnp.float32)


def nn(a, b):
    return dot(a, b, ((1,), (0,)))


def nt(a, b):
    return dot(a, b, ((1,), (1,)))


def iota(shape, axis):
    return lax.broadcasted_iota(jnp.int32, shape, axis)


def pack_kernel(home_ref, x_ref, ids_ref, order_ref, out_ref, sel_ref):
    rows = x_ref.shape[0]
    home = home_ref[0]
    ids = ids_ref[...] ^ home
    ids_rows = jnp.broadcast_to(ids.astype(jnp.float32), (rows, rows)).T
    ids8 = ids_rows[0:8, :]
    onehot = jnp.where(ids8 == iota((8, rows), 0).astype(jnp.float32), 1.0, 0.0)
    earlier = jnp.where(iota((rows, rows), 0) < iota((rows, rows), 1), 1.0, 0.0)
    rank = jnp.sum(nn(onehot, earlier) * onehot, axis=0, keepdims=True)
    slot = ids8[0:1, :] * 32.0 + rank
    place = jnp.where(slot == iota((256, rows), 0).astype(jnp.float32), 1.0, 0.0)
    used = jnp.sum(place, axis=1, keepdims=True)
    packed = jnp.where(used > 0.5, nn(place, x_ref[...]), EMPTY)
    for g in range(8):
        out_ref[g] = packed[g * 32 : (g + 1) * 32]
    want = jnp.broadcast_to(order_ref[...].astype(jnp.float32), (rows, rows)).T
    picked = jnp.where(want == iota((rows, rows), 1).astype(jnp.float32), jnp.broadcast_to(slot, (rows, rows)), 0.0)
    sel_ref[...] = jnp.broadcast_to(jnp.sum(picked, axis=1, keepdims=True), (rows, rows))


PAIRS = [(i, k) for k in range(8) for i in range(k, 8)]
AT = {p: n for n, p in enumerate(PAIRS)}
HALF = len(PAIRS) // 2
STAT = HALF * B


def gram_kernel(core_ref, *refs):
    rows_refs, (mine_ref, other_ref), (xt, xs) = refs[:8], refs[8:10], refs[10:]
    total = jnp.zeros((1, 1024), jnp.float32)
    count = jnp.zeros((1, 1), jnp.float32)
    for g in range(8):
        x = rows_refs[g][...]
        live = x[:, 0:1] < 1e29
        x = jnp.where(live, x - SHIFT, 0.0)
        xs[g * 32 : (g + 1) * 32, :] = x
        total = total + jnp.sum(x, axis=0, keepdims=True)
        count = count + jnp.sum(live.astype(jnp.float32), axis=0, keepdims=True)
    xt[...] = xs[...].T
    sums = jnp.concatenate([total[:, j * B : (j + 1) * B] for j in range(8)], axis=0)

    def fill(first, refs_of):
        for k in range(8):
            block = nn(xt[k * B :, :], xs[:, k * B : (k + 1) * B])
            for i in range(k, 8):
                n = AT[i, k]
                ref = refs_of[n // HALF]
                ref[n % HALF * B : (n % HALF + 1) * B, :] = block[(i - k) * B : (i - k + 1) * B, :]
        for ref in refs_of:
            ref[STAT : STAT + 8, :] = sums
            ref[STAT + 8 : STAT + 16, :] = jnp.broadcast_to(count, (8, B))

    @pl.when(core_ref[0] == 0)
    def _():
        fill(0, (mine_ref, other_ref))

    @pl.when(core_ref[0] == 1)
    def _():
        fill(1, (other_ref, mine_ref))


def row_of(x, j):
    return jnp.broadcast_to(x[j : j + 1, :], x.shape)


def col_of(x, j):
    return jnp.broadcast_to(x[:, j : j + 1], x.shape)


def inverse_factor(block, out_ref):
    sub = iota((8, B), 0)
    lane = iota((8, B), 1)
    groups = B // 8
    s = [block(g) for g in range(groups)]
    t = [jnp.where(lane == sub + 8 * g, 1.0, 0.0) for g in range(groups)]
    for g in range(groups):
        base = 8 * g
        e0, e1 = s[g], t[g]
        c = [col_of(e0, base + j) for j in range(8)]
        a = {(i, j): row_of(c[j], i) for j in range(8) for i in range(j + 1)}
        v = jnp.zeros((8, B), jnp.float32)
        for j in range(8):
            pivot = a[j, j]
            root = lax.rsqrt(pivot)
            inv = 1.0 / pivot
            here = sub == j
            b0, b1 = row_of(e0, j), row_of(e1, j)
            m = c[j] * inv
            v = jnp.where(here, b1 * root, v)
            e0 = jnp.where(here, b0 * inv, e0 - m * b0)
            e1 = jnp.where(here, b1 * inv, e1 - m * b1)
            for k in range(j + 1, 8):
                c[k] = jnp.where(here, a[j, k] * inv, c[k] - m * a[j, k])
            for i in range(j + 1, 8):
                q = a[j, i] * inv
                for k in range(i, 8):
                    a[i, k] = a[i, k] - q * a[j, k]
        out_ref[base : base + 8, :] = v
        if g + 1 < groups:
            w0 = [row_of(e0, r) for r in range(8)]
            w1 = [row_of(e1, r) for r in range(8)]
            for h in range(g + 1, groups):
                cols = [col_of(s[h], base + r) for r in range(8)]
                for r in range(8):
                    s[h] = s[h] - cols[r] * w0[r]
                    t[h] = t[h] - cols[r] * w1[r]


def factor_kernel(core_ref, mine_ref, other_ref, *refs):
    rows_refs, out_refs, (a, x, inv) = refs[:8], refs[8:16], refs[16:]
    core = core_ref[0]
    stats = mine_ref[STAT : STAT + 16, :]
    scale = 1.0 / stats[8:16, :]
    mean = stats[0:8, :] * scale
    mean_t = jnp.concatenate([mean, jnp.zeros((B - 8, B), jnp.float32)], axis=0).T
    eye = jnp.where(iota((B, B), 0) == iota((B, B), 1), RIDGE, 0.0)
    scale_b = jnp.broadcast_to(scale[0:1, :], (B, B))

    def prepare(refs_of):
        for n, (i, k) in enumerate(PAIRS):
            r = n % HALF * B
            block = refs_of[n // HALF][r : r + B, :] * scale_b
            block = block - jnp.broadcast_to(mean_t[:, i : i + 1], (B, B)) * mean[k : k + 1, :]
            a[n] = block + eye if i == k else block

    @pl.when(core == 0)
    def _():
        prepare((mine_ref, other_ref))

    @pl.when(core == 1)
    def _():
        prepare((other_ref, mine_ref))

    for g in range(8):
        row = rows_refs[g][...]
        live = row[:, 0:1] < 1e29
        for k in range(8):
            y = row[:, k * B : (k + 1) * B]
            x[k, g * 32 : (g + 1) * 32, :] = jnp.where(live, y - SHIFT - mean[k : k + 1, :], 0.0)

    @pl.loop(0, 8)
    def _(k):
        start = k * 8 - (k * (k - 1)) // 2
        inverse_factor(lambda g: a[start, 8 * g : 8 * g + 8, :], inv)
        for kk in range(8):

            @pl.when(k == kk)
            def _():
                n0 = AT[kk, kk]
                z = nt(x[kk], inv[...])
                for g in range(8):
                    out_refs[g][:, kk * B : (kk + 1) * B] = z[g * 32 : (g + 1) * 32, :]
                rest = 7 - kk
                if rest:
                    panel = nt(a[n0 + 1 : n0 + 1 + rest].reshape(rest * B, B), inv[...])
                    down = nt(z, panel)
                    for j in range(rest):
                        x[kk + 1 + j] = x[kk + 1 + j] - down[:, j * B : (j + 1) * B]
                        n = AT[kk + 1 + j, kk + 1 + j]
                        update = nt(panel[j * B :, :], panel[j * B : (j + 1) * B, :])
                        a[n : n + rest - j] = a[n : n + rest - j] - update.reshape(rest - j, B, B)


def unpack_kernel(sel_ref, *refs):
    rows_refs, out_ref = refs[:8], refs[8]
    sel = sel_ref[...]
    total = None
    lane = iota((B, 256), 1).astype(jnp.float32)
    place = jnp.where(jnp.concatenate([sel, sel], axis=1) == lane, 1.0, 0.0)
    rows = jnp.concatenate([r[...] for r in rows_refs], axis=0)
    out_ref[...] = nn(place, rows)


VMEM = pl.BlockSpec(memory_space=pltpu.VMEM)
SMEM = pl.BlockSpec(memory_space=pltpu.SMEM)


def f32(*shape):
    return jax.ShapeDtypeStruct(shape, jnp.float32)


def call(kernel, name, outs, n_in, scratch=(), cost=1000000):
    return pl.pallas_call(
        kernel,
        name=name,
        out_shape=outs,
        in_specs=[SMEM] * 1 + [VMEM] * (n_in - 1),
        out_specs=jax.tree.map(lambda _: VMEM, outs),
        scratch_shapes=scratch,
        cost_estimate=pl.CostEstimate(flops=cost, bytes_accessed=4000000, transcendentals=0),
        compiler_params=pltpu.CompilerParams(vmem_limit_bytes=60 << 20),
    )


def factor(core, mine, other, rows):
    return call(
        factor_kernel,
        "factor",
        [f32(32, 1024)] * 8,
        11,
        [pltpu.VMEM((36, B, B), jnp.float32), pltpu.VMEM((8, 256, B), jnp.float32), pltpu.VMEM((B, B), jnp.float32)],
    )(core, mine, other, *rows)


def gram(core, rows):
    return call(
        gram_kernel,
        "gram",
        [f32(STAT + 16, B)] * 2,
        9,
        [pltpu.VMEM((1024, 256), jnp.float32), pltpu.VMEM((256, 1024), jnp.float32)],
    )(core, *rows)


def local(embeddings, domain_ids, order):
    d, w = lax.axis_index("dom"), lax.axis_index("wide")
    core = (d % 2).reshape(1).astype(jnp.int32)
    home = ((w // 8) * 4 + (w % 4) // 2 * 2 + d // 4).reshape(1).astype(jnp.int32)
    packed, sel = call(pack_kernel, "pack", [f32(8, 32, 1024), f32(B, B)], 4)(home, embeddings, domain_ids, order)

    def exchange(blocks):
        return [blocks[0]] + [permute(blocks[m], lambda n, m=m: toward(n, m)) for m in range(1, 8)]

    rows = exchange([packed[m] for m in range(8)])
    mine, other = gram(core, rows)
    mine = mine + permute(other, lambda n: partner(n, 3))
    cuts = (0, 6 * B, 12 * B, STAT + 16)
    parts = [mine[lo:hi] for lo, hi in zip(cuts, cuts[1:])]
    for step in range(3):
        parts = [p + permute(p, lambda n, axis=(i + step) % 3: partner(n, axis)) for i, p in enumerate(parts)]
    mine = jnp.concatenate(parts)
    other = permute(mine, lambda n: partner(n, 3))
    white = exchange(factor(core, mine, other, rows))
    return pl.pallas_call(
        unpack_kernel,
        name="unpack",
        out_shape=f32(B, 1024),
        in_specs=[VMEM] * 9,
        out_specs=VMEM,
        compiler_params=pltpu.CompilerParams(vmem_limit_bytes=60 << 20),
    )(sel, *white)


def solution(mesh):
    placed = (P(AXES, None), P(AXES, None), P(AXES, None))
    return jax.shard_map(local, mesh=mesh, in_specs=placed, out_specs=P(AXES, None), check_vma=False)
```

```python
import functools

import jax
import jax.numpy as jnp
from jax import lax
from jax.experimental import pallas as pl
from jax.experimental.pallas import tpu as pltpu
from jax.sharding import PartitionSpec as P

RIDGE = 0.1
SHIFT = 1.0
EMPTY = 1e30
B = 128
HIGHEST = lax.Precision.HIGHEST
AXES = ("dom", "wide")


PLACE = (0, 1, 1, 0)


def coords(n):
    d, w = divmod(n, 16)
    return [w // 4, w % 4, d // 2, d % 2]


def number(c):
    x, y, z, core = c
    return (z * 2 + core) * 16 + x * 4 + y


def domain_of_device(n):
    x, y, z, _ = coords(n)
    return (x // 2) * 4 + (y // 2) * 2 + z // 2


def toward(n, mask):
    c = coords(n)
    for axis, bit in ((0, 4), (1, 2), (2, 1)):
        if mask & bit:
            c[axis] = 3 - c[axis]
    return number(c)


def partner(n, axis):
    c = coords(n)
    c[axis] ^= 1
    return number(c)


def permute(x, to):
    return lax.ppermute(x, AXES, [(n, to(n)) for n in range(128)])


def dot(a, b, dims):
    return lax.dot_general(a, b, (dims, ((), ())), precision=HIGHEST, preferred_element_type=jnp.float32)


def nn(a, b):
    return dot(a, b, ((1,), (0,)))


def nt(a, b):
    return dot(a, b, ((1,), (1,)))


def iota(shape, axis):
    return lax.broadcasted_iota(jnp.int32, shape, axis)


def split(x):
    high = x.astype(jnp.bfloat16)
    rest = x - high.astype(jnp.float32)
    middle = rest.astype(jnp.bfloat16)
    low = (rest - middle.astype(jnp.float32)).astype(jnp.bfloat16)
    return high, middle, low


def left(x):
    h, m, l = split(x)
    return jnp.concatenate([l, m, h, m, h, h], axis=1)


def right(x):
    h, m, l = split(x)
    return jnp.concatenate([h, m, l, h, m, h], axis=1)


def product(a, b):
    return lax.dot_general(a, b, (((1,), (1,)), ((), ())), preferred_element_type=jnp.float32)


def plain(a, b):
    return lax.dot_general(a, b, (((1,), (0,)), ((), ())), preferred_element_type=jnp.float32)


def pick(place, x):
    h, m, l = split(x)
    p = place.astype(jnp.bfloat16)
    return plain(jnp.concatenate([p, p, p], axis=1), jnp.concatenate([l, m, h], axis=0))


def pack_kernel(home_ref, x_ref, ids_ref, order_ref, *refs):
    out_refs, sel_ref = refs[:8], refs[8]
    rows = x_ref.shape[0]
    home = home_ref[0]
    ids = ids_ref[...] ^ home
    ids_rows = jnp.broadcast_to(ids.astype(jnp.float32), (rows, rows)).T
    ids8 = ids_rows[0:8, :]
    onehot = jnp.where(ids8 == iota((8, rows), 0).astype(jnp.float32), 1.0, 0.0)
    earlier = jnp.where(iota((rows, rows), 0) < iota((rows, rows), 1), 1.0, 0.0)
    rank = jnp.sum(nn(onehot, earlier) * onehot, axis=0, keepdims=True)
    slot = ids8[0:1, :] * 32.0 + rank
    place = jnp.where(slot == iota((256, rows), 0).astype(jnp.float32), 1.0, 0.0)
    used = jnp.sum(place, axis=1, keepdims=True)
    packed = jnp.where(used > 0.5, pick(place, x_ref[...]), EMPTY)
    for g in range(8):
        out_refs[g][...] = packed[g * 32 : (g + 1) * 32]
    want = jnp.broadcast_to(order_ref[...].astype(jnp.float32), (rows, rows)).T
    picked = jnp.where(want == iota((rows, rows), 1).astype(jnp.float32), jnp.broadcast_to(slot, (rows, rows)), 0.0)
    sel_ref[...] = jnp.broadcast_to(jnp.sum(picked, axis=1, keepdims=True), (rows, rows))


PAIRS = [(i, k) for k in range(8) for i in range(k, 8)]
AT = {p: n for n, p in enumerate(PAIRS)}
HALF = len(PAIRS) // 2
STAT = HALF * B


def gram_kernel(core_ref, *refs):
    rows_refs, (mine_ref, other_ref), (xs, xl, xr, block) = refs[:8], refs[8:10], refs[10:]
    total = jnp.zeros((1, 1024), jnp.float32)
    count = jnp.zeros((1, 1), jnp.float32)
    for g in range(8):
        x = rows_refs[g][...]
        live = x[:, 0:1] < 1e29
        x = jnp.where(live, x - SHIFT, 0.0)
        xs[g * 32 : (g + 1) * 32, :] = x
        total = total + jnp.sum(x, axis=0, keepdims=True)
        count = count + jnp.sum(live.astype(jnp.float32), axis=0, keepdims=True)
    sums = jnp.concatenate([total[:, j * B : (j + 1) * B] for j in range(8)], axis=0)
    xl[...] = left(xs[...].T)
    h, m, l = split(xs[...])
    xr[...] = jnp.concatenate([h, m, l, h, m, h], axis=0)
    for k in range(0, 8, 2):
        two = plain(xl[k * B :, :], xr[:, k * B : (k + 2) * B])
        for c in range(2):
            n = AT[k + c, k + c]
            block[n : n + 8 - k - c] = two[c * B :, c * B : (c + 1) * B].reshape(8 - k - c, B, B)
    for ref, half in ((mine_ref, core_ref[0]), (other_ref, 1 - core_ref[0])):
        for n in range(HALF):
            ref[n * B : (n + 1) * B, :] = block[half * HALF + n]
        ref[STAT : STAT + 8, :] = sums
        ref[STAT + 8 : STAT + 16, :] = jnp.broadcast_to(count, (8, B))


def row_of(x, j):
    return jnp.broadcast_to(x[j : j + 1, :], x.shape)


def col_of(x, j):
    return jnp.broadcast_to(x[:, j : j + 1], x.shape)


def inverse_factor(block, one, out_ref):
    sub = iota((8, B), 0)
    lane = iota((8, B), 1)
    groups = B // 8
    s = [block(g) for g in range(groups)]
    t = [jnp.where(lane == sub + 8 * g, 1.0, 0.0) for g in range(groups)]

    def eliminate(e0, e1, c, ahead, rows):
        v = jnp.zeros((8, B), jnp.float32)
        invs = []
        for j in range(8):
            top = {k: row_of(c[k], j) for k in range(j, 8)}
            inv = 1.0 / top[j]
            invs.append(inv)
            here = sub == j
            b0, b1 = row_of(e0, j), row_of(e1, j)
            m = jnp.where(here, 0.0, c[j] * inv)
            for k in range(j + 1, 8):
                c[k] = c[k] - m * top[k]
            v = jnp.where(here, b1 * lax.rsqrt(top[j]), v)
            e0 = e0 - m * b0
            e1 = e1 - m * b1
            if rows is not None:
                f0, f1, d = rows
                n = d[j] * inv
                f0, f1 = f0 - n * b0, f1 - n * b1
                for k in range(j + 1, 8):
                    d[k] = d[k] - n * top[k]
                for k in range(8):
                    r = row_of(ahead[k], j)
                    ahead[k] = ahead[k] - m * r
                    d[8 + k] = d[8 + k] - n * r
                rows = f0, f1, d
        scale = invs[7]
        for j in range(7):
            scale = jnp.where(sub == j, invs[j], scale)
        return v, e0 * scale, e1 * scale, rows

    def spread(x, first, count):
        return [col_of(x, first + j) * one for j in range(count)]

    def update(h, base, w0, w1):
        cols = [col_of(s[h], base + r) for r in range(8)]
        for r in range(8):
            s[h] = s[h] - cols[r] * w0[r]
            t[h] = t[h] - cols[r] * w1[r]

    for g in range(0, groups, 2):
        base = 8 * g
        near = range(g + 2, min(g + 4, groups))
        far = range(g + 4, groups)
        c = spread(s[g], base, 16)
        d = spread(s[g + 1], base, 16)
        v, p0, p1, (f0, f1, d) = eliminate(s[g], t[g], c[:8], c[8:], (s[g + 1], t[g + 1], d))
        out_ref[base : base + 8, :] = v
        if near:
            w0 = [row_of(p0, r) for r in range(8)]
            w1 = [row_of(p1, r) for r in range(8)]
        if far:
            below = jnp.concatenate([s[h] for h in far], axis=0)
            below = jnp.where(iota(below.shape, 1) >= base, below, 0.0)
            below = jnp.where(iota(below.shape, 1) < base + 16, below, 0.0)
        for h in near:
            update(h, base, w0, w1)
        v, q0, q1, _ = eliminate(f0, f1, d[8:], None, None)
        out_ref[base + 8 : base + 16, :] = v
        if near:
            w0 = [row_of(q0, r) for r in range(8)]
            w1 = [row_of(q1, r) for r in range(8)]
            for h in near:
                update(h, base + 8, w0, w1)
        if far:
            fix = [col_of(p0, base + 8 + r) for r in range(8)]
            for r in range(8):
                p0 = p0 - fix[r] * w0[r]
                p1 = p1 - fix[r] * w1[r]
            parts = [jnp.concatenate([p0, p1], axis=1), jnp.concatenate([q0, q1], axis=1)]
            zero = jnp.zeros((8, 2 * B), jnp.float32)
            w = jnp.concatenate([parts[i - g] if g <= i < g + 2 else zero for i in range(groups)], axis=0)
            h, m, l = split(w)
            change = lax.dot_general(
                left(below), jnp.concatenate([h, m, l, h, m, h], axis=0), (((1,), (0,)), ((), ())), preferred_element_type=jnp.float32
            )
            for i, n in enumerate(far):
                s[n] = s[n] - change[8 * i : 8 * i + 8, :B]
                t[n] = t[n] - change[8 * i : 8 * i + 8, B:]


def factor_kernel(core_ref, mine_ref, other_ref, *refs):
    rows_refs, out_refs, (a, x, inv, ones) = refs[:8], refs[8:16], refs[16:]
    core = core_ref[0]
    ones[...] = jnp.ones((8, B), jnp.float32)
    stats = mine_ref[STAT : STAT + 16, :]
    scale = 1.0 / stats[8:16, :]
    mean = stats[0:8, :] * scale
    mean_t = jnp.concatenate([mean, jnp.zeros((B - 8, B), jnp.float32)], axis=0).T
    eye = jnp.where(iota((B, B), 0) == iota((B, B), 1), RIDGE, 0.0)
    scale_b = jnp.broadcast_to(scale[0:1, :], (B, B))

    for ref, half in ((mine_ref, core), (other_ref, 1 - core)):

        @pl.loop(0, HALF)
        def _(n):
            a[half * HALF + n] = ref[pl.ds(pl.multiple_of(n * B, B), B), :] * scale_b

    for n, (i, k) in enumerate(PAIRS):
        block = a[n] - jnp.broadcast_to(mean_t[:, i : i + 1], (B, B)) * mean[k : k + 1, :]
        a[n] = block + eye if i == k else block

    for g in range(8):
        row = rows_refs[g][...]
        live = row[:, 0:1] < 1e29
        for k in range(8):
            y = row[:, k * B : (k + 1) * B]
            x[k, g * 32 : (g + 1) * 32, :] = jnp.where(live, y - SHIFT - mean[k : k + 1, :], 0.0)

    @pl.loop(0, 8)
    def _(k):
        start = k * 8 - (k * (k - 1)) // 2
        inverse_factor(lambda g: a[start, 8 * g : 8 * g + 8, :], ones[...], inv)
        for kk in range(8):

            @pl.when(k == kk)
            def _():
                n0 = AT[kk, kk]
                inv_r = right(inv[...])
                z = product(left(x[kk]), inv_r)
                for g in range(8):
                    out_refs[g][:, kk * B : (kk + 1) * B] = z[g * 32 : (g + 1) * 32, :]
                rest = 7 - kk
                if rest:
                    panel = product(left(a[n0 + 1 : n0 + 1 + rest].reshape(rest * B, B)), inv_r)
                    panel_l, panel_r = left(panel), right(panel)
                    down = product(left(z), panel_r)
                    for j in range(rest):
                        x[kk + 1 + j] = x[kk + 1 + j] - down[:, j * B : (j + 1) * B]
                    for j in range(0, rest, 2):
                        two = j + 1 < rest
                        change = product(panel_l[j * B :, :], panel_r[j * B : (j + 1 + two) * B, :])
                        n = AT[kk + 1 + j, kk + 1 + j]
                        a[n : n + rest - j] = a[n : n + rest - j] - change[:, :B].reshape(rest - j, B, B)
                        if two:
                            n += rest - j
                            a[n : n + rest - j - 1] = a[n : n + rest - j - 1] - change[B:, B:].reshape(rest - j - 1, B, B)


def unpack_kernel(sel_ref, *refs):
    rows_refs, out_ref = refs[:8], refs[8]
    sel = sel_ref[...]
    total = None
    lane = iota((B, 256), 1).astype(jnp.float32)
    place = jnp.where(jnp.concatenate([sel, sel], axis=1) == lane, 1.0, 0.0)
    rows = jnp.concatenate([r[...] for r in rows_refs], axis=0)
    out_ref[...] = pick(place, rows)


VMEM = pl.BlockSpec(memory_space=pltpu.VMEM)
SMEM = pl.BlockSpec(memory_space=pltpu.SMEM)


def f32(*shape):
    return jax.ShapeDtypeStruct(shape, jnp.float32)


def call(kernel, name, outs, n_in, scratch=(), cost=1000000):
    return pl.pallas_call(
        kernel,
        name=name,
        out_shape=outs,
        in_specs=[SMEM] * 1 + [VMEM] * (n_in - 1),
        out_specs=jax.tree.map(lambda _: VMEM, outs),
        scratch_shapes=scratch,
        cost_estimate=pl.CostEstimate(flops=cost, bytes_accessed=4000000, transcendentals=0),
        compiler_params=pltpu.CompilerParams(vmem_limit_bytes=60 << 20),
    )


def factor(core, mine, other, rows):
    return call(
        factor_kernel,
        "factor",
        [f32(32, 1024)] * 8,
        11,
        [pltpu.VMEM((36, B, B), jnp.float32), pltpu.VMEM((8, 256, B), jnp.float32), pltpu.VMEM((B, B), jnp.float32), pltpu.VMEM((8, B), jnp.float32)],
    )(core, mine, other, *rows)


def gram(core, rows):
    return call(
        gram_kernel,
        "gram",
        [f32(STAT + 16, B)] * 2,
        9,
        [
            pltpu.VMEM((256, 1024), jnp.float32),
            pltpu.VMEM((1024, 1536), jnp.bfloat16),
            pltpu.VMEM((1536, 1024), jnp.bfloat16),
            pltpu.VMEM((36, B, B), jnp.float32),
        ],
    )(core, *rows)


def local(embeddings, domain_ids, order):
    d, w = lax.axis_index("dom"), lax.axis_index("wide")
    core = (d % 2).reshape(1).astype(jnp.int32)
    home = ((w // 8) * 4 + (w % 4) // 2 * 2 + d // 4).reshape(1).astype(jnp.int32)
    *packed, sel = call(pack_kernel, "pack", [f32(32, 1024)] * 8 + [f32(B, B)], 4)(home, embeddings, domain_ids, order)

    def exchange(blocks):
        return [blocks[0]] + [permute(blocks[m], lambda n, m=m: toward(n, m)) for m in range(1, 8)]

    rows = exchange(packed)
    mine, other = gram(core, rows)
    mine = mine + permute(other, lambda n: partner(n, 3))
    cuts = (0, 6 * B, 12 * B, STAT + 16)
    parts = [mine[lo:hi] for lo, hi in zip(cuts, cuts[1:])]
    for step in range(3):
        parts = [p + permute(p, lambda n, axis=(i + step) % 3: partner(n, axis)) for i, p in enumerate(parts)]
    mine = jnp.concatenate(parts)
    other = permute(mine, lambda n: partner(n, 3))
    white = exchange(factor(core, mine, other, rows))
    return pl.pallas_call(
        unpack_kernel,
        name="unpack",
        out_shape=f32(B, 1024),
        in_specs=[VMEM] * 9,
        out_specs=VMEM,
        compiler_params=pltpu.CompilerParams(vmem_limit_bytes=60 << 20),
    )(sel, *white)


def solution(mesh):
    placed = (P(AXES, None), P(AXES, None), P(AXES, None))
    return jax.shard_map(local, mesh=mesh, in_specs=placed, out_specs=P(AXES, None), check_vma=False)
```

```python
import functools

import jax
import jax.numpy as jnp
from jax import lax
from jax.experimental import pallas as pl
from jax.experimental.pallas import tpu as pltpu
from jax.sharding import PartitionSpec as P

RIDGE = 0.1
SHIFT = 1.0
EMPTY = 1e30
B = 128
HIGHEST = lax.Precision.HIGHEST
AXES = ("dom", "wide")


PLACE = (0, 1, 1, 0)


def coords(n):
    d, w = divmod(n, 16)
    return [w // 4, w % 4, d // 2, d % 2]


def number(c):
    x, y, z, core = c
    return (z * 2 + core) * 16 + x * 4 + y


def domain_of_device(n):
    x, y, z, _ = coords(n)
    return (x // 2) * 4 + (y // 2) * 2 + z // 2


CARRIED = ((7, 3, 4, 0), (5, 6, 1, 2))


def toward(n, turn):
    c = coords(n)
    mask = CARRIED[c[3]][turn]
    for axis, bit in ((0, 4), (1, 2), (2, 1)):
        if mask & bit:
            c[axis] = 3 - c[axis]
    return number(c)


def partner(n, axis):
    c = coords(n)
    c[axis] ^= 1
    return number(c)


def permute(x, to):
    return lax.ppermute(x, AXES, [(n, to(n)) for n in range(128)])


def dot(a, b, dims):
    return lax.dot_general(a, b, (dims, ((), ())), precision=HIGHEST, preferred_element_type=jnp.float32)


def nn(a, b):
    return dot(a, b, ((1,), (0,)))


def nt(a, b):
    return dot(a, b, ((1,), (1,)))


def iota(shape, axis):
    return lax.broadcasted_iota(jnp.int32, shape, axis)


def split(x):
    high = x.astype(jnp.bfloat16)
    rest = x - high.astype(jnp.float32)
    middle = rest.astype(jnp.bfloat16)
    low = (rest - middle.astype(jnp.float32)).astype(jnp.bfloat16)
    return high, middle, low


def left(x):
    h, m, l = split(x)
    return jnp.concatenate([l, m, h, m, h, h], axis=1)


def right(x):
    h, m, l = split(x)
    return jnp.concatenate([h, m, l, h, m, h], axis=1)


def product(a, b):
    return lax.dot_general(a, b, (((1,), (1,)), ((), ())), preferred_element_type=jnp.float32)


def plain(a, b):
    return lax.dot_general(a, b, (((1,), (0,)), ((), ())), preferred_element_type=jnp.float32)


def pick(place, x):
    h, m, l = split(x)
    p = place.astype(jnp.bfloat16)
    return plain(jnp.concatenate([p, p, p], axis=1), jnp.concatenate([l, m, h], axis=0))


def pack_kernel(where_ref, ids_ref, order_ref, ids2_ref, x_ref, x2_ref, *refs):
    out_refs, sel_ref = refs[:4], refs[4]
    rows = x_ref.shape[0]
    core, home = where_ref[0], where_ref[1]
    earlier = jnp.where(iota((rows, rows), 0) < iota((rows, rows), 1), 1.0, 0.0).astype(jnp.bfloat16)

    def group_and_rank(ids):
        turned = ids ^ home
        group = jnp.zeros_like(turned)
        for place, mask in enumerate(CARRIED[0] + CARRIED[1]):
            group = jnp.where(turned == mask, place, group)
        group = group ^ (4 * core)
        group = jnp.broadcast_to(group.astype(jnp.float32), (8, rows))
        onehot = jnp.where(group == iota((8, rows), 0).astype(jnp.float32), 1.0, 0.0)
        counted = plain(onehot.astype(jnp.bfloat16), earlier)
        return group[0:1, :], jnp.sum(counted * onehot, axis=0, keepdims=True)

    group, rank = group_and_rank(ids_ref[...])
    group2, rank2 = group_and_rank(ids2_ref[...])
    slot = jnp.concatenate([group * 64.0 + rank, group2 * 64.0 + 32.0 + rank2], axis=1)
    place = jnp.where(slot == iota((256, 2 * rows), 0).astype(jnp.float32), 1.0, 0.0)
    used = jnp.sum(place, axis=1, keepdims=True)
    packed = jnp.where(used > 0.5, pick(place, jnp.concatenate([x_ref[...], x2_ref[...]], axis=0)), EMPTY)
    for g in range(4):
        out_refs[g][...] = packed[g * 64 : (g + 1) * 64]
    home_slot = jnp.broadcast_to(group * 32.0 + rank, (rows, rows))
    want = jnp.broadcast_to(order_ref[...].astype(jnp.float32), (rows, rows)).T
    picked = jnp.where(want == iota((rows, rows), 1).astype(jnp.float32), home_slot, 0.0)
    sel_ref[...] = jnp.broadcast_to(jnp.sum(picked, axis=1, keepdims=True), (rows, rows))


HALVES = ((0, 6), (2, 4))
PAIRS = [(i, c) for half in HALVES for k in half for c in (k, k + 1) for i in range(c, 8)]
AT = {p: n for n, p in enumerate(PAIRS)}
HALF = len(PAIRS) // 2
THIRD = HALF // 3
STAT = HALF * B


def gram_kernel(half_ref, *refs):
    rows_refs, out_ref, (xs, xl, xr) = refs[:4], refs[4], refs[5:]
    total = jnp.zeros((1, 1024), jnp.float32)
    count = jnp.zeros((1, 1), jnp.float32)
    for g in range(4):
        x = rows_refs[g][...]
        live = x[:, 0:1] < 1e29
        x = jnp.where(live, x - SHIFT, 0.0)
        xs[g * 64 : (g + 1) * 64, :] = x
        total = total + jnp.sum(x, axis=0, keepdims=True)
        count = count + jnp.sum(live.astype(jnp.float32), axis=0, keepdims=True)
    out_ref[STAT : STAT + 8, :] = jnp.concatenate([total[:, j * B : (j + 1) * B] for j in range(8)], axis=0)
    out_ref[STAT + 8 : STAT + 16, :] = jnp.broadcast_to(count, (8, B))

    def fill(half):
        first = min(HALVES[half])
        xl[first * B :, :] = left(xs[:, first * B :].T)
        for k in HALVES[half]:
            h, m, l = split(xs[:, k * B : (k + 2) * B])
            two = plain(xl[k * B :, :], jnp.concatenate([h, m, l, h, m, h], axis=0))
            for c in range(2):
                n = AT[k + c, k + c] % HALF * B
                out_ref[n : n + (8 - k - c) * B, :] = two[c * B :, c * B : (c + 1) * B]

    for half in range(2):
        pl.when(half_ref[0] == half)(functools.partial(fill, half))


def row_of(x, j):
    return jnp.broadcast_to(x[j : j + 1, :], x.shape)


def col_of(x, j):
    return jnp.broadcast_to(x[:, j : j + 1], x.shape)


def inverse_factor(block, one, out_ref):
    sub = iota((8, B), 0)
    lane = iota((8, B), 1)
    groups = B // 8
    s = [block(g) for g in range(groups)]
    t = [jnp.where(lane == sub + 8 * g, 1.0, 0.0) for g in range(groups)]

    def eliminate(e0, e1, c, ahead, rows):
        v = jnp.zeros((8, B), jnp.float32)
        invs = []
        for j in range(8):
            top = {k: row_of(c[k], j) for k in range(j, 8)}
            inv = 1.0 / top[j]
            invs.append(inv)
            here = sub == j
            b0, b1 = row_of(e0, j), row_of(e1, j)
            m = jnp.where(here, 0.0, c[j] * inv)
            for k in range(j + 1, 8):
                c[k] = c[k] - m * top[k]
            v = jnp.where(here, b1 * lax.rsqrt(top[j]), v)
            e0 = e0 - m * b0
            e1 = e1 - m * b1
            if rows is not None:
                f0, f1, d = rows
                n = d[j] * inv
                f0, f1 = f0 - n * b0, f1 - n * b1
                for k in range(j + 1, 8):
                    d[k] = d[k] - n * top[k]
                for k in range(8):
                    r = row_of(ahead[k], j)
                    ahead[k] = ahead[k] - m * r
                    d[8 + k] = d[8 + k] - n * r
                rows = f0, f1, d
        scale = invs[7]
        for j in range(7):
            scale = jnp.where(sub == j, invs[j], scale)
        return v, e0 * scale, e1 * scale, rows

    def spread(x, first, count):
        return [col_of(x, first + j) * one for j in range(count)]

    def update(h, base, w0, w1):
        cols = [col_of(s[h], base + r) for r in range(8)]
        for r in range(8):
            s[h] = s[h] - cols[r] * w0[r]
            t[h] = t[h] - cols[r] * w1[r]

    for g in range(0, groups, 2):
        base = 8 * g
        near = range(g + 2, min(g + 4, groups))
        far = range(g + 4, groups)
        c = spread(s[g], base, 16)
        d = spread(s[g + 1], base, 16)
        v, p0, p1, (f0, f1, d) = eliminate(s[g], t[g], c[:8], c[8:], (s[g + 1], t[g + 1], d))
        out_ref[base : base + 8, :] = v
        if near:
            w0 = [row_of(p0, r) for r in range(8)]
            w1 = [row_of(p1, r) for r in range(8)]
        if far:
            below = jnp.concatenate([s[h] for h in far], axis=0)
            below = jnp.where(iota(below.shape, 1) >= base, below, 0.0)
            below = jnp.where(iota(below.shape, 1) < base + 16, below, 0.0)
        for h in near:
            update(h, base, w0, w1)
        v, q0, q1, _ = eliminate(f0, f1, d[8:], None, None)
        out_ref[base + 8 : base + 16, :] = v
        if near:
            w0 = [row_of(q0, r) for r in range(8)]
            w1 = [row_of(q1, r) for r in range(8)]
            for h in near:
                update(h, base + 8, w0, w1)
        if far:
            fix = [col_of(p0, base + 8 + r) for r in range(8)]
            for r in range(8):
                p0 = p0 - fix[r] * w0[r]
                p1 = p1 - fix[r] * w1[r]
            parts = [jnp.concatenate([p0, p1], axis=1), jnp.concatenate([q0, q1], axis=1)]
            zero = jnp.zeros((8, 2 * B), jnp.float32)
            w = jnp.concatenate([parts[i - g] if g <= i < g + 2 else zero for i in range(groups)], axis=0)
            h, m, l = split(w)
            change = lax.dot_general(
                left(below), jnp.concatenate([h, m, l, h, m, h], axis=0), (((1,), (0,)), ((), ())), preferred_element_type=jnp.float32
            )
            for i, n in enumerate(far):
                s[n] = s[n] - change[8 * i : 8 * i + 8, :B]
                t[n] = t[n] - change[8 * i : 8 * i + 8, B:]


def factor_kernel(core_ref, *refs):
    mine_refs, other_refs, rows_refs, out_refs, (a, x, inv, ones) = refs[:3], refs[3:6], refs[6:10], refs[10:14], refs[14:]
    core = core_ref[0]
    ones[...] = jnp.ones((8, B), jnp.float32)
    stats = mine_refs[2][THIRD * B : THIRD * B + 16, :]
    scale = 1.0 / stats[8:16, :]
    mean = stats[0:8, :] * scale
    mean_t = jnp.concatenate([mean, jnp.zeros((B - 8, B), jnp.float32)], axis=0).T
    eye = jnp.where(iota((B, B), 0) == iota((B, B), 1), RIDGE, 0.0)
    scale_b = jnp.broadcast_to(scale[0:1, :], (B, B))

    for third in range(3):
        for ref, half in ((mine_refs[third], core), (other_refs[third], 1 - core)):

            @pl.loop(0, THIRD)
            def _(n, ref=ref, first=half * HALF + third * THIRD):
                a[first + n] = ref[pl.ds(pl.multiple_of(n * B, B), B), :] * scale_b

    for n, (i, k) in enumerate(PAIRS):
        block = a[n] - jnp.broadcast_to(mean_t[:, i : i + 1], (B, B)) * mean[k : k + 1, :]
        a[n] = block + eye if i == k else block

    for g in range(4):
        row = rows_refs[g][...]
        live = row[:, 0:1] < 1e29
        for k in range(8):
            y = row[:, k * B : (k + 1) * B]
            x[k, g * 64 : (g + 1) * 64, :] = jnp.where(live, y - SHIFT - mean[k : k + 1, :], 0.0)

    @pl.loop(0, 8)
    def _(k):
        start = jnp.int32(AT[0, 0])
        for kk in range(1, 8):
            start = jnp.where(k == kk, AT[kk, kk], start)
        inverse_factor(lambda g: a[start, 8 * g : 8 * g + 8, :], ones[...], inv)
        for kk in range(8):

            @pl.when(k == kk)
            def _():
                n0 = AT[kk, kk]
                inv_r = right(inv[...])
                z = product(left(x[kk]), inv_r)
                for g in range(4):
                    out_refs[g][:, kk * B : (kk + 1) * B] = z[g * 64 : (g + 1) * 64, :]
                rest = 7 - kk
                if rest:
                    panel = product(left(a[n0 + 1 : n0 + 1 + rest].reshape(rest * B, B)), inv_r)
                    panel_l, panel_r = left(panel), right(panel)
                    down = product(left(z), panel_r)
                    for j in range(rest):
                        x[kk + 1 + j] = x[kk + 1 + j] - down[:, j * B : (j + 1) * B]
                    for j in range(0, rest, 2):
                        two = j + 1 < rest
                        change = product(panel_l[j * B :, :], panel_r[j * B : (j + 1 + two) * B, :])
                        for c in range(1 + two):
                            n, size = AT[kk + 1 + j + c, kk + 1 + j + c], rest - j - c
                            a[n : n + size] = a[n : n + size] - change[c * B :, c * B : (c + 1) * B].reshape(size, B, B)


def unpack_kernel(sel_ref, *refs):
    own_refs, other_refs, out_ref = refs[:4], refs[4:8], refs[8]
    sel = sel_ref[...]
    lane = iota((B, 256), 1).astype(jnp.float32)
    place = jnp.where(jnp.concatenate([sel, sel], axis=1) == lane, 1.0, 0.0)
    out_ref[...] = pick(place, jnp.concatenate([r[:32, :] for r in own_refs] + [r[32:, :] for r in other_refs], axis=0))


VMEM = pl.BlockSpec(memory_space=pltpu.VMEM)
SMEM = pl.BlockSpec(memory_space=pltpu.SMEM)


def f32(*shape):
    return jax.ShapeDtypeStruct(shape, jnp.float32)


def call(kernel, name, outs, args, scratch=(), mib=24, scalars=1):
    return pl.pallas_call(
        kernel,
        name=name,
        out_shape=outs,
        in_specs=[SMEM] * scalars + [VMEM] * (len(args) - scalars),
        out_specs=jax.tree.map(lambda _: VMEM, outs),
        scratch_shapes=scratch,
        cost_estimate=pl.CostEstimate(flops=1000000, bytes_accessed=4000000, transcendentals=0),
        compiler_params=pltpu.CompilerParams(vmem_limit_bytes=mib << 20),
    )(*args)


def local(embeddings, domain_ids, order):
    d, w = lax.axis_index("dom"), lax.axis_index("wide")
    core = (d % 2).reshape(1).astype(jnp.int32)
    home = ((w // 8) * 4 + (w % 4) // 2 * 2 + d // 4).reshape(1).astype(jnp.int32)

    def swap(x):
        return permute(x, lambda n: partner(n, 3))

    def exchange(arrays):
        return [permute(x, lambda n, turn=turn: toward(n, turn)) for turn, x in enumerate(arrays)]

    ids = domain_ids.reshape(1, B)
    where = jnp.concatenate([core, home])
    *packed, sel = call(
        pack_kernel,
        "pack",
        [f32(64, 1024)] * 4 + [f32(B, B)],
        (where, ids, order, swap(ids), embeddings, swap(embeddings)),
        mib=12,
    )
    rows = exchange(packed)
    scratch = [pltpu.VMEM((256, 1024), jnp.float32), pltpu.VMEM((1024, 1536), jnp.bfloat16), pltpu.VMEM((8, B), jnp.float32)]
    other = call(gram_kernel, "gram", f32(STAT + 16, B), (1 - core, *rows), scratch)
    other = swap(other)
    mine = call(gram_kernel, "gram", f32(STAT + 16, B), (core, *rows), scratch)
    cuts = (0, THIRD * B, 2 * THIRD * B, STAT + 16)
    parts = [mine[lo:hi] + other[lo:hi] for lo, hi in zip(cuts, cuts[1:])]
    for step in range(3):
        parts = [p + permute(p, lambda n, axis=(i + step) % 3: partner(n, axis)) for i, p in enumerate(parts)]
    white = call(
        factor_kernel,
        "factor",
        [f32(64, 1024)] * 4,
        (core, *parts, *[swap(p) for p in parts], *rows),
        [
            pltpu.VMEM((36, B, B), jnp.float32),
            pltpu.VMEM((8, 256, B), jnp.float32),
            pltpu.VMEM((B, B), jnp.float32),
            pltpu.VMEM((8, B), jnp.float32),
        ],
    )
    white = exchange(white)
    return call(unpack_kernel, "unpack", f32(B, 1024), (sel, *white, *[swap(x) for x in white]), mib=12, scalars=0)


def solution(mesh):
    placed = (P(AXES, None), P(AXES, None), P(AXES, None))
    return jax.shard_map(local, mesh=mesh, in_specs=placed, out_specs=P(AXES, None), check_vma=False)
```

```python
import functools

import jax
import jax.numpy as jnp
from jax import lax
from jax.experimental import pallas as pl
from jax.experimental.pallas import tpu as pltpu
from jax.sharding import PartitionSpec as P

RIDGE = 0.1
SHIFT = 1.0
EMPTY = 1e30
B = 128
HIGHEST = lax.Precision.HIGHEST
AXES = ("dom", "wide")


PLACE = (0, 1, 1, 0)


def coords(n):
    d, w = divmod(n, 16)
    return [w // 4, w % 4, d // 2, d % 2]


def number(c):
    x, y, z, core = c
    return (z * 2 + core) * 16 + x * 4 + y


def domain_of_device(n):
    x, y, z, _ = coords(n)
    return (x // 2) * 4 + (y // 2) * 2 + z // 2


CARRIED = ((4, 3, 7, 0), (1, 2, 5, 6))


def toward(n, turn):
    c = coords(n)
    mask = CARRIED[c[3]][turn]
    for axis, bit in ((0, 4), (1, 2), (2, 1)):
        if mask & bit:
            c[axis] = 3 - c[axis]
    return number(c)


def partner(n, axis):
    c = coords(n)
    c[axis] ^= 1
    return number(c)


def permute(x, to):
    return lax.ppermute(x, AXES, [(n, to(n)) for n in range(128)])


def dot(a, b, dims):
    return lax.dot_general(a, b, (dims, ((), ())), precision=HIGHEST, preferred_element_type=jnp.float32)


def nn(a, b):
    return dot(a, b, ((1,), (0,)))


def nt(a, b):
    return dot(a, b, ((1,), (1,)))


def iota(shape, axis):
    return lax.broadcasted_iota(jnp.int32, shape, axis)


def split(x):
    high = x.astype(jnp.bfloat16)
    rest = x - high.astype(jnp.float32)
    middle = rest.astype(jnp.bfloat16)
    low = (rest - middle.astype(jnp.float32)).astype(jnp.bfloat16)
    return high, middle, low


def left(x):
    h, m, l = split(x)
    return jnp.concatenate([l, m, h, m, h, h], axis=1)


def right(x):
    h, m, l = split(x)
    return jnp.concatenate([h, m, l, h, m, h], axis=1)


def product(a, b):
    return lax.dot_general(a, b, (((1,), (1,)), ((), ())), preferred_element_type=jnp.float32)


def plain(a, b):
    return lax.dot_general(a, b, (((1,), (0,)), ((), ())), preferred_element_type=jnp.float32)


def pick(place, x):
    h, m, l = split(x)
    p = place.astype(jnp.bfloat16)
    return plain(jnp.concatenate([p, p, p], axis=1), jnp.concatenate([l, m, h], axis=0))


def pack_kernel(where_ref, ids_ref, order_ref, ids2_ref, x_ref, x2_ref, *refs):
    out_refs, sel_ref, copied, sems = refs[:4], refs[4], refs[5:8], refs[8]
    copies = [
        pltpu.make_async_copy(hbm, vmem, sems.at[i]) for i, (hbm, vmem) in enumerate(zip((ids_ref, order_ref, x_ref), copied))
    ]
    for copy in copies:
        copy.start()
    for copy in copies:
        copy.wait()
    ids_ref, order_ref, x_ref = copied
    rows = x_ref.shape[0]
    core, home = where_ref[0], where_ref[1]
    earlier = jnp.where(iota((rows, rows), 0) < iota((rows, rows), 1), 1.0, 0.0).astype(jnp.bfloat16)

    def group_and_rank(ids):
        turned = ids ^ home
        group = jnp.zeros_like(turned)
        for place, mask in enumerate(CARRIED[0] + CARRIED[1]):
            group = jnp.where(turned == mask, place, group)
        group = group ^ (4 * core)
        group = jnp.broadcast_to(group.astype(jnp.float32), (8, rows))
        onehot = jnp.where(group == iota((8, rows), 0).astype(jnp.float32), 1.0, 0.0)
        counted = plain(onehot.astype(jnp.bfloat16), earlier)
        return group[0:1, :], jnp.sum(counted * onehot, axis=0, keepdims=True)

    group, rank = group_and_rank(ids_ref[...])
    group2, rank2 = group_and_rank(ids2_ref[...])
    slot = jnp.concatenate([group * 64.0 + rank, group2 * 64.0 + 32.0 + rank2], axis=1)
    place = jnp.where(slot == iota((256, 2 * rows), 0).astype(jnp.float32), 1.0, 0.0)
    used = jnp.sum(place, axis=1, keepdims=True)
    packed = jnp.where(used > 0.5, pick(place, jnp.concatenate([x_ref[...], x2_ref[...]], axis=0)), EMPTY)
    for g in range(4):
        out_refs[g][...] = packed[g * 64 : (g + 1) * 64]
    home_slot = jnp.broadcast_to(group * 32.0 + rank, (rows, rows))
    want = jnp.broadcast_to(order_ref[...].astype(jnp.float32), (rows, rows)).T
    picked = jnp.where(want == iota((rows, rows), 1).astype(jnp.float32), home_slot, 0.0)
    sel_ref[...] = jnp.broadcast_to(jnp.sum(picked, axis=1, keepdims=True), (rows, rows))


HALVES = ((0, 6), (2, 4))
PAIRS = [(i, c) for half in HALVES for k in half for c in (k, k + 1) for i in range(c, 8)]
AT = {p: n for n, p in enumerate(PAIRS)}
HALF = len(PAIRS) // 2
SIXTH = HALF // 6
SIZES = (SIXTH * B, SIXTH * B, SIXTH * B + 8)
STARTS = (0, 2 * SIZES[0], 4 * SIZES[0], 4 * SIZES[0] + 2 * SIZES[2])


def row_in_half(n, bit_ref):
    part, second, inside = (2, n - HALF, SIXTH) if n >= HALF else (n // SIXTH // 2, n // SIXTH % 2, n % SIXTH)
    sent = second ^ bit_ref[1 + part]
    return pl.multiple_of(STARTS[part] + sent * SIZES[part] + inside * B, 8)


def gram_kernel(half_ref, *refs):
    rows_refs, out_ref, (xs, xl, xr) = refs[:4], refs[4], refs[5:]
    total = jnp.zeros((1, 1024), jnp.float32)
    count = jnp.zeros((1, 1), jnp.float32)
    for g in range(4):
        x = rows_refs[g][...]
        live = x[:, 0:1] < 1e29
        x = jnp.where(live, x - SHIFT, 0.0)
        xs[g * 64 : (g + 1) * 64, :] = x
        total = total + jnp.sum(x, axis=0, keepdims=True)
        count = count + jnp.sum(live.astype(jnp.float32), axis=0, keepdims=True)
    sums = jnp.concatenate([total[:, j * B : (j + 1) * B] for j in range(8)], axis=0)
    out_ref[pl.ds(row_in_half(HALF, half_ref), 8), :] = sums
    out_ref[pl.ds(row_in_half(HALF + 1, half_ref), 8), :] = jnp.broadcast_to(count, (8, B))

    def fill(half):
        first = min(HALVES[half])
        xl[first * B :, :] = left(xs[:, first * B :].T)
        for k in HALVES[half]:
            h, m, l = split(xs[:, k * B : (k + 2) * B])
            two = plain(xl[k * B :, :], jnp.concatenate([h, m, l, h, m, h], axis=0))
            for c in range(2):
                for i in range(k + c, 8):
                    row = row_in_half(AT[i, k + c] % HALF, half_ref)
                    out_ref[pl.ds(row, B), :] = two[(i - k) * B : (i - k + 1) * B, c * B : (c + 1) * B]

    for half in range(2):
        pl.when(half_ref[0] == half)(functools.partial(fill, half))


def row_of(x, j):
    return jnp.broadcast_to(x[j : j + 1, :], x.shape)


def col_of(x, j):
    return jnp.broadcast_to(x[:, j : j + 1], x.shape)


def inverse_factor(block, one, out_ref):
    sub = iota((8, B), 0)
    lane = iota((8, B), 1)
    groups = B // 8
    s = [block(g) for g in range(groups)]
    t = [jnp.where(lane == sub + 8 * g, 1.0, 0.0) for g in range(groups)]

    def eliminate(e0, e1, c, ahead, rows):
        v = jnp.zeros((8, B), jnp.float32)
        invs = []
        for j in range(8):
            top = {k: row_of(c[k], j) for k in range(j, 8)}
            inv = 1.0 / top[j]
            invs.append(inv)
            here = sub == j
            b0, b1 = row_of(e0, j), row_of(e1, j)
            m = jnp.where(here, 0.0, c[j] * inv)
            for k in range(j + 1, 8):
                c[k] = c[k] - m * top[k]
            v = jnp.where(here, b1 * lax.rsqrt(top[j]), v)
            e0 = e0 - m * b0
            e1 = e1 - m * b1
            if rows is not None:
                f0, f1, d = rows
                n = d[j] * inv
                f0, f1 = f0 - n * b0, f1 - n * b1
                for k in range(j + 1, 8):
                    d[k] = d[k] - n * top[k]
                for k in range(8):
                    r = row_of(ahead[k], j)
                    ahead[k] = ahead[k] - m * r
                    d[8 + k] = d[8 + k] - n * r
                rows = f0, f1, d
        scale = invs[7]
        for j in range(7):
            scale = jnp.where(sub == j, invs[j], scale)
        return v, e0 * scale, e1 * scale, rows

    def spread(x, first, count):
        return [col_of(x, first + j) * one for j in range(count)]

    def update(h, base, w0, w1):
        cols = [col_of(s[h], base + r) for r in range(8)]
        for r in range(8):
            s[h] = s[h] - cols[r] * w0[r]
            t[h] = t[h] - cols[r] * w1[r]

    for g in range(0, groups, 2):
        base = 8 * g
        near = range(g + 2, min(g + 4, groups))
        far = range(g + 4, groups)
        c = spread(s[g], base, 16)
        d = spread(s[g + 1], base, 16)
        v, p0, p1, (f0, f1, d) = eliminate(s[g], t[g], c[:8], c[8:], (s[g + 1], t[g + 1], d))
        out_ref[base : base + 8, :] = v
        if near:
            w0 = [row_of(p0, r) for r in range(8)]
            w1 = [row_of(p1, r) for r in range(8)]
        if far:
            below = jnp.concatenate([s[h] for h in far], axis=0)
            below = jnp.where(iota(below.shape, 1) >= base, below, 0.0)
            below = jnp.where(iota(below.shape, 1) < base + 16, below, 0.0)
        for h in near:
            update(h, base, w0, w1)
        v, q0, q1, _ = eliminate(f0, f1, d[8:], None, None)
        out_ref[base + 8 : base + 16, :] = v
        if near:
            w0 = [row_of(q0, r) for r in range(8)]
            w1 = [row_of(q1, r) for r in range(8)]
            for h in near:
                update(h, base + 8, w0, w1)
        if far:
            fix = [col_of(p0, base + 8 + r) for r in range(8)]
            for r in range(8):
                p0 = p0 - fix[r] * w0[r]
                p1 = p1 - fix[r] * w1[r]
            parts = [jnp.concatenate([p0, p1], axis=1), jnp.concatenate([q0, q1], axis=1)]
            zero = jnp.zeros((8, 2 * B), jnp.float32)
            w = jnp.concatenate([parts[i - g] if g <= i < g + 2 else zero for i in range(groups)], axis=0)
            h, m, l = split(w)
            change = lax.dot_general(
                left(below), jnp.concatenate([h, m, l, h, m, h], axis=0), (((1,), (0,)), ((), ())), preferred_element_type=jnp.float32
            )
            for i, n in enumerate(far):
                s[n] = s[n] - change[8 * i : 8 * i + 8, :B]
                t[n] = t[n] - change[8 * i : 8 * i + 8, B:]


def factor_kernel(core_ref, *refs):
    sixths_refs, rows_refs, out_refs, (a, x, inv, ones, stat) = refs[:12], refs[12:16], refs[16:20], refs[20:]
    core = core_ref[0]
    ones[...] = jnp.ones((8, B), jnp.float32)
    for second in range(2):
        stat[pl.ds(pl.multiple_of((second ^ core_ref[3]) * 8, 8), 8), :] = sixths_refs[2 + 3 * second][SIXTH * B :, :]
    stats = stat[...]
    scale = 1.0 / stats[8:16, :]
    mean = stats[0:8, :] * scale
    mean_t = jnp.concatenate([mean, jnp.zeros((B - 8, B), jnp.float32)], axis=0).T
    eye = jnp.where(iota((B, B), 0) == iota((B, B), 1), RIDGE, 0.0)
    scale_b = jnp.broadcast_to(scale[0:1, :], (B, B))

    for which, ref in enumerate(sixths_refs):
        half, second, part = which // 6, which // 3 % 2, which % 3
        first = (half ^ core) * HALF + (2 * part + (second ^ core_ref[1 + part])) * SIXTH

        @pl.loop(0, SIXTH)
        def _(n, ref=ref, first=first):
            a[first + n] = ref[pl.ds(pl.multiple_of(n * B, B), B), :] * scale_b

    for n, (i, k) in enumerate(PAIRS):
        block = a[n] - jnp.broadcast_to(mean_t[:, i : i + 1], (B, B)) * mean[k : k + 1, :]
        a[n] = block + eye if i == k else block

    for g in range(4):
        row = rows_refs[g][...]
        live = row[:, 0:1] < 1e29
        for k in range(8):
            y = row[:, k * B : (k + 1) * B]
            x[k, g * 64 : (g + 1) * 64, :] = jnp.where(live, y - SHIFT - mean[k : k + 1, :], 0.0)

    @pl.loop(0, 8)
    def _(k):
        start = jnp.int32(AT[0, 0])
        for kk in range(1, 8):
            start = jnp.where(k == kk, AT[kk, kk], start)
        inverse_factor(lambda g: a[start, 8 * g : 8 * g + 8, :], ones[...], inv)
        for kk in range(8):

            @pl.when(k == kk)
            def _():
                n0 = AT[kk, kk]
                inv_r = right(inv[...])
                z = product(left(x[kk]), inv_r)
                for g in range(4):
                    out_refs[g][:, kk * B : (kk + 1) * B] = z[g * 64 : (g + 1) * 64, :]
                rest = 7 - kk
                if rest:
                    panel = product(left(a[n0 + 1 : n0 + 1 + rest].reshape(rest * B, B)), inv_r)
                    panel_l, panel_r = left(panel), right(panel)
                    down = product(left(z), panel_r)
                    for j in range(rest):
                        x[kk + 1 + j] = x[kk + 1 + j] - down[:, j * B : (j + 1) * B]
                    for j in range(0, rest, 2):
                        two = j + 1 < rest
                        change = product(panel_l[j * B :, :], panel_r[j * B : (j + 1 + two) * B, :])
                        for c in range(1 + two):
                            n, size = AT[kk + 1 + j + c, kk + 1 + j + c], rest - j - c
                            a[n : n + size] = a[n : n + size] - change[c * B :, c * B : (c + 1) * B].reshape(size, B, B)


def unpack_kernel(sel_ref, *refs):
    own_refs, other_refs, out_ref = refs[:4], refs[4:8], refs[8]
    sel = sel_ref[...]
    lane = iota((B, 256), 1).astype(jnp.float32)
    place = jnp.where(jnp.concatenate([sel, sel], axis=1) == lane, 1.0, 0.0)
    out_ref[...] = pick(place, jnp.concatenate([r[:32, :] for r in own_refs] + [r[32:, :] for r in other_refs], axis=0))


VMEM = pl.BlockSpec(memory_space=pltpu.VMEM)
SMEM = pl.BlockSpec(memory_space=pltpu.SMEM)
OUTSIDE = pl.BlockSpec(memory_space=pltpu.HBM)


def f32(*shape):
    return jax.ShapeDtypeStruct(shape, jnp.float32)


def call(kernel, name, outs, args, scratch=(), mib=24, scalars=1, outside=()):
    return pl.pallas_call(
        kernel,
        name=name,
        out_shape=outs,
        in_specs=[SMEM if i < scalars else OUTSIDE if i in outside else VMEM for i in range(len(args))],
        out_specs=jax.tree.map(lambda _: VMEM, outs),
        scratch_shapes=scratch,
        cost_estimate=pl.CostEstimate(flops=1000000, bytes_accessed=4000000, transcendentals=0),
        compiler_params=pltpu.CompilerParams(vmem_limit_bytes=mib << 20),
    )(*args)


def local(embeddings, domain_ids, order):
    d, w = lax.axis_index("dom"), lax.axis_index("wide")
    core = (d % 2).reshape(1).astype(jnp.int32)
    home = ((w // 8) * 4 + (w % 4) // 2 * 2 + d // 4).reshape(1).astype(jnp.int32)

    def swap(x):
        return permute(x, lambda n: partner(n, 3))

    def exchange(arrays):
        return [permute(x, lambda n, turn=turn: toward(n, turn)) for turn, x in enumerate(arrays)]

    ids = domain_ids.reshape(1, B)
    where = jnp.concatenate([core, home])
    *packed, sel = call(
        pack_kernel,
        "pack",
        [f32(64, 1024)] * 4 + [f32(B, B)],
        (where, ids, order, swap(ids), embeddings, swap(embeddings)),
        [pltpu.VMEM((1, B), jnp.int32), pltpu.VMEM((1, B), jnp.int32), pltpu.VMEM((B, 1024), jnp.float32), pltpu.SemaphoreType.DMA((3,))],
        mib=12,
        outside=(1, 2, 4),
    )
    rows = exchange(packed)
    scratch = [pltpu.VMEM((256, 1024), jnp.float32), pltpu.VMEM((1024, 1536), jnp.bfloat16), pltpu.VMEM((8, B), jnp.float32)]
    bits = jnp.stack([w // 4 % 2, w % 2, d // 2 % 2]).astype(jnp.int32)
    other = call(gram_kernel, "gram", f32(STARTS[3], B), (jnp.concatenate([1 - core, bits]), *rows), scratch)
    other = swap(other)
    mine = call(gram_kernel, "gram", f32(STARTS[3], B), (jnp.concatenate([core, bits]), *rows), scratch)

    def across(x, axis):
        return permute(x, lambda n: partner(n, axis % 3))

    def both(start, size):
        return mine[start : start + size] + other[start : start + size]

    sums = [both(start, size) for start, size in zip(STARTS, SIZES)]
    sums = [x + across(both(STARTS[i] + SIZES[i], SIZES[i]), i) for i, x in enumerate(sums)]
    sums = [x + across(x, i + 1) for i, x in enumerate(sums)]
    sums = [x + across(x, i + 2) for i, x in enumerate(sums)]
    sums = sums + [across(x, i) for i, x in enumerate(sums)]
    white = call(
        factor_kernel,
        "factor",
        [f32(64, 1024)] * 4,
        (jnp.concatenate([core, bits]), *sums, *[swap(x) for x in sums], *rows),
        [
            pltpu.VMEM((36, B, B), jnp.float32),
            pltpu.VMEM((8, 256, B), jnp.float32),
            pltpu.VMEM((B, B), jnp.float32),
            pltpu.VMEM((8, B), jnp.float32),
            pltpu.VMEM((16, B), jnp.float32),
        ],
    )
    white = exchange(white)
    return call(unpack_kernel, "unpack", f32(B, 1024), (sel, *white, *[swap(x) for x in white]), mib=12, scalars=0)


def solution(mesh):
    placed = (P(AXES, None), P(AXES, None), P(AXES, None))
    return jax.shard_map(local, mesh=mesh, in_specs=placed, out_specs=P(AXES, None), check_vma=False)
```

```python
import functools

import jax
import jax.numpy as jnp
from jax import lax
from jax.experimental import pallas as pl
from jax.experimental.pallas import tpu as pltpu
from jax.sharding import PartitionSpec as P

RIDGE = 0.1
SHIFT = 1.0
EMPTY = 1e30
B = 128
HIGHEST = lax.Precision.HIGHEST
AXES = ("dom", "wide")


PLACE = (0, 1, 1, 0)


def coords(n):
    d, w = divmod(n, 16)
    return [w // 4, w % 4, d // 2, d % 2]


def number(c):
    x, y, z, core = c
    return (z * 2 + core) * 16 + x * 4 + y


def domain_of_device(n):
    x, y, z, _ = coords(n)
    return (x // 2) * 4 + (y // 2) * 2 + z // 2


CARRIED = ((4, 2, 1, 7), (3, 5, 6, 0))


def toward(n, turn):
    c = coords(n)
    mask = CARRIED[c[3]][turn]
    for axis, bit in ((0, 4), (1, 2), (2, 1)):
        if mask & bit:
            c[axis] = 3 - c[axis]
    return number(c)


def partner(n, axis):
    c = coords(n)
    c[axis] ^= 1
    return number(c)


def permute(x, to):
    return lax.ppermute(x, AXES, [(n, to(n)) for n in range(128)])


def dot(a, b, dims):
    return lax.dot_general(a, b, (dims, ((), ())), precision=HIGHEST, preferred_element_type=jnp.float32)


def nn(a, b):
    return dot(a, b, ((1,), (0,)))


def nt(a, b):
    return dot(a, b, ((1,), (1,)))


def iota(shape, axis):
    return lax.broadcasted_iota(jnp.int32, shape, axis)


def split(x):
    high = x.astype(jnp.bfloat16)
    rest = x - high.astype(jnp.float32)
    middle = rest.astype(jnp.bfloat16)
    low = (rest - middle.astype(jnp.float32)).astype(jnp.bfloat16)
    return high, middle, low


def left(x):
    h, m, l = split(x)
    return jnp.concatenate([l, m, h, m, h, h], axis=1)


def right(x):
    h, m, l = split(x)
    return jnp.concatenate([h, m, l, h, m, h], axis=1)


def product(a, b):
    return lax.dot_general(a, b, (((1,), (1,)), ((), ())), preferred_element_type=jnp.float32)


def plain(a, b):
    return lax.dot_general(a, b, (((1,), (0,)), ((), ())), preferred_element_type=jnp.float32)


def pick(place, x):
    h, m, l = split(x)
    p = place.astype(jnp.bfloat16)
    return plain(jnp.concatenate([p, p, p], axis=1), jnp.concatenate([l, m, h], axis=0))


def pack_kernel(where_ref, small_ref, ids2_ref, x_ref, x2_ref, *refs):
    out_refs, sel_ref = refs[:4], refs[4]
    rows = x_ref.shape[0]
    core, home = where_ref[0], where_ref[1]
    earlier = jnp.where(iota((rows, rows), 0) < iota((rows, rows), 1), 1.0, 0.0).astype(jnp.bfloat16)

    def group_and_rank(ids):
        turned = ids ^ home
        group = jnp.zeros_like(turned)
        for place, mask in enumerate(CARRIED[0] + CARRIED[1]):
            group = jnp.where(turned == mask, place, group)
        group = group ^ (4 * core)
        group = jnp.broadcast_to(group.astype(jnp.float32), (8, rows))
        onehot = jnp.where(group == iota((8, rows), 0).astype(jnp.float32), 1.0, 0.0)
        counted = plain(onehot.astype(jnp.bfloat16), earlier)
        return group[0:1, :], jnp.sum(counted * onehot, axis=0, keepdims=True)

    group, rank = group_and_rank(small_ref[0:1, :])
    group2, rank2 = group_and_rank(ids2_ref[...])
    slot = jnp.concatenate([group * 64.0 + rank, group2 * 64.0 + 32.0 + rank2], axis=1)
    place = jnp.where(slot == iota((256, 2 * rows), 0).astype(jnp.float32), 1.0, 0.0)
    used = jnp.sum(place, axis=1, keepdims=True)
    packed = jnp.where(used > 0.5, pick(place, jnp.concatenate([x_ref[...], x2_ref[...]], axis=0)), EMPTY)
    for g in range(4):
        out_refs[g][...] = packed[g * 64 : (g + 1) * 64]
    home_slot = jnp.broadcast_to(group * 32.0 + rank, (rows, rows))
    want = jnp.broadcast_to(small_ref[1:2, :].astype(jnp.float32), (rows, rows)).T
    picked = jnp.where(want == iota((rows, rows), 1).astype(jnp.float32), home_slot, 0.0)
    sel_ref[...] = jnp.broadcast_to(jnp.sum(picked, axis=1, keepdims=True), (rows, rows))


CHUNKS = ((0, 2), (2, 8))
PLACE_IN = [{p: n for n, p in enumerate((i, k) for k in range(*cols) for i in range(k, 8))} for cols in CHUNKS]
STAT = len(PLACE_IN[0]) * B
HALVES = ((STAT + 16) // 2, len(PLACE_IN[1]) * B // 2)
CUTS = ((0, 328, 648, 968), (0, 448, 896, 1344))


def gram_kernel(chunk, core_ref, *refs):
    rows_refs, (mine_ref, other_ref), (xs, xl, flat) = refs[:4], refs[4:6], refs[6:]
    for g in range(4):
        x = rows_refs[g][...]
        live = x[:, 0:1] < 1e29
        xs[g * 64 : (g + 1) * 64, :] = jnp.where(live, x - SHIFT, 0.0)
    first, end = CHUNKS[chunk]
    if chunk == 0:
        total = jnp.sum(xs[...], axis=0, keepdims=True)
        flat[STAT : STAT + 8, :] = jnp.concatenate([total[:, j * B : (j + 1) * B] for j in range(8)], axis=0)
        live = [jnp.where(ref[:, 0:B] < 1e29, 1.0, 0.0) for ref in rows_refs]
        count = jnp.sum(jnp.concatenate(live, axis=0), axis=0, keepdims=True)
        flat[STAT + 8 : STAT + 16, :] = jnp.broadcast_to(count, (8, B))
    xl[first * B :, :] = left(xs[:, first * B :].T)
    for k in range(first, end, 2):
        h, m, l = split(xs[:, k * B : (k + 2) * B])
        two = plain(xl[k * B :, :], jnp.concatenate([h, m, l, h, m, h], axis=0))
        for c in range(2):
            n = PLACE_IN[chunk][k + c, k + c] * B
            flat[n : n + (8 - k - c) * B, :] = two[c * B :, c * B : (c + 1) * B]
    half = HALVES[chunk]
    for ref, which in ((mine_ref, core_ref[0]), (other_ref, 1 - core_ref[0])):
        ref[...] = flat[pl.ds(pl.multiple_of(which * half, 8), half), :]


def row_of(x, j):
    return jnp.broadcast_to(x[j : j + 1, :], x.shape)


def col_of(x, j):
    return jnp.broadcast_to(x[:, j : j + 1], x.shape)


def inverse_factor(block, one, out_ref, between):
    sub = iota((8, B), 0)
    lane = iota((8, B), 1)
    groups = B // 8
    s = [block(g) for g in range(groups)]
    t = [jnp.where(lane == sub + 8 * g, 1.0, 0.0) for g in range(groups)]

    def eliminate(e0, e1, c, ahead, rows):
        v = jnp.zeros((8, B), jnp.float32)
        invs = []
        for j in range(8):
            top = {k: row_of(c[k], j) for k in range(j, 8)}
            inv = 1.0 / top[j]
            invs.append(inv)
            here = sub == j
            b0, b1 = row_of(e0, j), row_of(e1, j)
            m = jnp.where(here, 0.0, c[j] * inv)
            for k in range(j + 1, 8):
                c[k] = c[k] - m * top[k]
            v = jnp.where(here, b1 * lax.rsqrt(top[j]), v)
            e0 = e0 - m * b0
            e1 = e1 - m * b1
            if rows is not None:
                f0, f1, d = rows
                n = d[j] * inv
                f0, f1 = f0 - n * b0, f1 - n * b1
                for k in range(j + 1, 8):
                    d[k] = d[k] - n * top[k]
                for k in range(8):
                    r = row_of(ahead[k], j)
                    ahead[k] = ahead[k] - m * r
                    d[8 + k] = d[8 + k] - n * r
                rows = f0, f1, d
        scale = invs[7]
        for j in range(7):
            scale = jnp.where(sub == j, invs[j], scale)
        return v, e0 * scale, e1 * scale, rows

    def spread(x, first, count):
        return [col_of(x, first + j) * one for j in range(count)]

    def update(h, base, w0, w1):
        cols = [col_of(s[h], base + r) for r in range(8)]
        for r in range(8):
            s[h] = s[h] - cols[r] * w0[r]
            t[h] = t[h] - cols[r] * w1[r]

    for g in range(0, groups, 2):
        base = 8 * g
        near = range(g + 2, min(g + 4, groups))
        far = range(g + 4, groups)
        c = spread(s[g], base, 16)
        d = spread(s[g + 1], base, 16)
        v, p0, p1, (f0, f1, d) = eliminate(s[g], t[g], c[:8], c[8:], (s[g + 1], t[g + 1], d))
        out_ref[base : base + 8, :] = v
        if near:
            w0 = [row_of(p0, r) for r in range(8)]
            w1 = [row_of(p1, r) for r in range(8)]
        if far:
            below = jnp.concatenate([s[h] for h in far], axis=0)
            below = jnp.where(iota(below.shape, 1) >= base, below, 0.0)
            below = jnp.where(iota(below.shape, 1) < base + 16, below, 0.0)
        for h in near:
            update(h, base, w0, w1)
        between[g]()
        v, q0, q1, _ = eliminate(f0, f1, d[8:], None, None)
        out_ref[base + 8 : base + 16, :] = v
        if near:
            w0 = [row_of(q0, r) for r in range(8)]
            w1 = [row_of(q1, r) for r in range(8)]
            for h in near:
                update(h, base + 8, w0, w1)
        if far:
            fix = [col_of(p0, base + 8 + r) for r in range(8)]
            for r in range(8):
                p0 = p0 - fix[r] * w0[r]
                p1 = p1 - fix[r] * w1[r]
            parts = [jnp.concatenate([p0, p1], axis=1), jnp.concatenate([q0, q1], axis=1)]
            zero = jnp.zeros((8, 2 * B), jnp.float32)
            w = jnp.concatenate([parts[i - g] if g <= i < g + 2 else zero for i in range(groups)], axis=0)
            h, m, l = split(w)
            change = lax.dot_general(
                left(below), jnp.concatenate([h, m, l, h, m, h], axis=0), (((1,), (0,)), ((), ())), preferred_element_type=jnp.float32
            )
            for i, n in enumerate(far):
                s[n] = s[n] - change[8 * i : 8 * i + 8, :B]
                t[n] = t[n] - change[8 * i : 8 * i + 8, B:]
        between[g + 1]()


def gather_chunk(chunk, core, refs, flat):
    for which, ref in enumerate(refs):
        start = (which // 3 ^ core) * HALVES[chunk] + CUTS[chunk][which % 3]
        flat[pl.ds(pl.multiple_of(start, 8), ref.shape[0]), :] = ref[...]


def make_covariance(chunk, flat, mean, scale):
    mean_t = jnp.concatenate([mean, jnp.zeros((B - 8, B), jnp.float32)], axis=0).T
    eye = jnp.where(iota((B, B), 0) == iota((B, B), 1), RIDGE, 0.0)
    scale = jnp.broadcast_to(scale[0:1, :], (B, B))
    for (i, k), n in PLACE_IN[chunk].items():
        block = flat[n * B : (n + 1) * B, :] * scale
        block = block - jnp.broadcast_to(mean_t[:, i : i + 1], (B, B)) * mean[k : k + 1, :]
        flat[n * B : (n + 1) * B, :] = block + eye if i == k else block


def center_rows(rows_refs, mean, k):
    out = []
    for ref in rows_refs:
        live = ref[:, 0:1] < 1e29
        out.append(jnp.where(live, ref[:, k * B : (k + 1) * B] - SHIFT - mean[k : k + 1, :], 0.0))
    return jnp.concatenate(out, axis=0)


def leaf(block, ones, inv, work):
    slots = [[] for _ in range(16)]
    for i, piece in enumerate(work):
        slots[i * 16 // len(work)].append(piece)

    def run(pieces):
        for piece in pieces:
            piece()

    inverse_factor(lambda g: block[8 * g : 8 * g + 8, :], ones[...], inv, [functools.partial(run, p) for p in slots])


def in_a_region(scalar):
    return pl.when(scalar >= 0)


def first_kernel(core_ref, *refs):
    parts_refs, rows_refs, (stat_ref, col0_ref, col1_ref, inv_ref, z_ref, x_ref) = refs[:6], refs[6:10], refs[10:16]
    flat, ones, inv, inv_r, diagonal, first, first_r, x0, z_l = refs[16:]
    core = core_ref[0]
    gather_chunk(0, core, parts_refs, flat)
    scale = 1.0 / flat[STAT + 8 : STAT + 16, :]
    mean = flat[STAT : STAT + 8, :] * scale
    stat_ref[0:8, :] = mean
    stat_ref[8:16, :] = scale
    make_covariance(0, flat, mean, scale)
    ones[...] = jnp.ones((8, B), jnp.float32)

    @in_a_region(core)
    def _():
        def center(k, ref):
            ref[...] = center_rows(rows_refs, stat_ref[...], k)

        leaf(flat[0:B], ones, inv, [lambda: center(0, x0), lambda: center(1, x_ref)])
        inv_r[...] = right(inv[...])
        below = product(left(flat[B : 2 * B, :]), inv_r[...])
        first_r[...] = right(below)
        diagonal[...] = flat[8 * B : 9 * B, :] - product(left(below), first_r[...])

    @in_a_region(core)
    def _():
        def solve(j):
            p = product(left(flat[(2 + j) * B : (5 + j) * B, :]), inv_r[...])
            col0_ref[j * B : (j + 3) * B, :] = p

        def apply(j):
            change = product(left(col0_ref[j * B : (j + 3) * B, :]), first_r[...])
            col1_ref[j * B : (j + 3) * B, :] = flat[(9 + j) * B : (12 + j) * B, :] - change

        def whiten():
            z = product(left(x0[...]), inv_r[...])
            z_ref[...] = z
            z_l[...] = left(z)

        def down():
            x_ref[...] = x_ref[...] - product(z_l[...], first_r[...])

        work = [lambda: solve(0), lambda: solve(3), whiten, lambda: apply(0), lambda: apply(3), down]
        leaf(diagonal[...], ones, inv_ref, work)


def second_kernel(core_ref, *refs):
    parts_refs, (stat_ref, col0_ref, col1_ref, inv1_ref, z0_ref, x1_ref), rows_refs, out_refs = refs[:6], refs[6:12], refs[12:16], refs[16:20]
    flat, ones, inv, inv_r, diagonal, panel, x, z_l, rows_l, rows_r = refs[20:]
    core = core_ref[0]
    at = PLACE_IN[1]
    mean = stat_ref[0:8, :]
    gather_chunk(1, core, parts_refs, flat)
    make_covariance(1, flat, mean, stat_ref[8:16, :])
    ones[...] = jnp.ones((8, B), jnp.float32)
    inv_r[...] = right(inv1_ref[...])
    second = product(left(col1_ref[0:B, :]), inv_r[...])
    panel[2 * B : 3 * B, :] = second
    both_l = jnp.concatenate([left(col0_ref[0:B, :]), left(second)], axis=1)
    both_r = jnp.concatenate([right(col0_ref[0:B, :]), right(second)], axis=1)
    diagonal[...] = flat[0:B, :] - product(both_l, both_r)

    def put(k, z):
        for g in range(4):
            out_refs[g][:, k * B : (k + 1) * B] = z[g * 64 : (g + 1) * 64, :]

    def step(k):
        width = 12 * B if k == 2 else 6 * B

        def solve(lo, hi):
            n = at[lo, k - 1] * B if k > 2 else 0
            column = flat[n : n + (hi - lo) * B, :] if k > 2 else col1_ref[(lo - 2) * B : (hi - 2) * B, :]
            panel[lo * B : hi * B, :] = product(left(column), inv_r[...])

        def whiten():
            z = product(left(x1_ref[...] if k == 2 else x[k - 1]), inv_r[...])
            put(k - 1, z)
            if k == 2:
                put(0, z0_ref[...])
                z_l[:, : 6 * B] = left(z0_ref[...])
                z_l[:, 6 * B :] = left(z)
            else:
                z_l[:, : 6 * B] = left(z)

        def center(j):
            x[j] = center_rows(rows_refs, stat_ref[...], j)

        def parts(lo, hi):
            if k == 2:
                old = col0_ref[(lo - 2) * B : (hi - 2) * B, :]
                rows_l[lo * B : hi * B, : 6 * B] = left(old)
                rows_r[lo * B : hi * B, : 6 * B] = right(old)
            new = panel[lo * B : hi * B, :]
            rows_l[lo * B : hi * B, width - 6 * B : width] = left(new)
            rows_r[lo * B : hi * B, width - 6 * B : width] = right(new)

        def down(j):
            hi = min(j + 2, 8)
            change = product(z_l[:, :width], rows_r[j * B : hi * B, :width])
            for i in range(j, hi):
                x[i] = x[i] - change[:, (i - j) * B : (i - j + 1) * B]

        def update(j, lo, hi):
            top = min(j + 2, 8)
            change = product(rows_l[lo * B : hi * B, :width], rows_r[j * B : top * B, :width])
            for c in range(j, top):
                low = max(lo, c)
                n, size = at[low, c] * B, (hi - low) * B
                flat[n : n + size, :] = flat[n : n + size, :] - change[(low - lo) * B :, (c - j) * B : (c - j + 1) * B]

        def spans(lo, hi):
            return [(i, min(i + 3, hi)) for i in range(lo, hi, 3)]

        work = [functools.partial(solve, *span) for span in spans(k + 1, 8)]
        work += [whiten]
        work += [functools.partial(parts, *span) for span in spans(k, 8)]
        if k == 2:
            work += [functools.partial(center, j) for j in range(2, 8)]
        columns = range(k, 8, 2)
        work += [functools.partial(update, j, *span) for j in columns for span in spans(j, 8)]
        work += [functools.partial(down, j) for j in columns]
        leaf(diagonal[...], ones, inv, work)
        inv_r[...] = right(inv[...])
        if k < 7:
            n = at[k, k] * B
            below = product(left(flat[n + B : n + 2 * B, :]), inv_r[...])
            panel[(k + 1) * B : (k + 2) * B, :] = below
            n = at[k + 1, k + 1] * B
            diagonal[...] = flat[n : n + B, :] - product(left(below), right(below))
        else:
            put(7, product(left(x[7]), inv_r[...]))

    for k in range(2, 8):
        in_a_region(core)(functools.partial(step, k))


def unpack_kernel(sel_ref, *refs):
    own_refs, other_refs, out_ref = refs[:4], refs[4:8], refs[8]
    sel = sel_ref[...]
    lane = iota((B, 256), 1).astype(jnp.float32)
    place = jnp.where(jnp.concatenate([sel, sel], axis=1) == lane, 1.0, 0.0)
    out_ref[...] = pick(place, jnp.concatenate([r[:32, :] for r in own_refs] + [r[32:, :] for r in other_refs], axis=0))


VMEM = pl.BlockSpec(memory_space=pltpu.VMEM)
SMEM = pl.BlockSpec(memory_space=pltpu.SMEM)


def f32(*shape):
    return jax.ShapeDtypeStruct(shape, jnp.float32)


def call(kernel, name, outs, args, scratch=(), mib=24, scalars=1):
    return pl.pallas_call(
        kernel,
        name=name,
        out_shape=outs,
        in_specs=[SMEM] * scalars + [VMEM] * (len(args) - scalars),
        out_specs=jax.tree.map(lambda _: VMEM, outs),
        scratch_shapes=scratch,
        cost_estimate=pl.CostEstimate(flops=1000000, bytes_accessed=4000000, transcendentals=0),
        compiler_params=pltpu.CompilerParams(vmem_limit_bytes=mib << 20),
    )(*args)


def local(embeddings, domain_ids, order):
    d, w = lax.axis_index("dom"), lax.axis_index("wide")
    core = (d % 2).reshape(1).astype(jnp.int32)
    home = ((w // 8) * 4 + (w % 4) // 2 * 2 + d // 4).reshape(1).astype(jnp.int32)

    def swap(x):
        return permute(x, lambda n: partner(n, 3))

    def exchange(arrays):
        return [permute(x, lambda n, turn=turn: toward(n, turn)) for turn, x in enumerate(arrays)]

    ids = domain_ids.reshape(1, B)
    where = jnp.concatenate([core, home])
    *packed, sel = call(
        pack_kernel,
        "pack",
        [f32(64, 1024)] * 4 + [f32(B, B)],
        (where, jnp.concatenate([ids, order]), swap(ids), embeddings, swap(embeddings)),
        mib=12,
    )
    rows = exchange(packed)
    def scratch(*shapes, dtype=jnp.float32):
        return [pltpu.VMEM(shape, dtype) for shape in shapes]

    def wide(*shapes):
        return scratch(*shapes, dtype=jnp.bfloat16)

    def gram(chunk):
        half = HALVES[chunk]
        return call(
            functools.partial(gram_kernel, chunk),
            "gram",
            [f32(half, B)] * 2,
            (core, *rows),
            scratch((256, 1024)) + wide((1024, 1536)) + scratch((2 * half, B)),
        )

    def across(x, axis):
        return permute(x, lambda n: partner(n, axis % 3))

    grams = [gram(chunk) for chunk in range(2)]
    sums = []
    for chunk, (mine, other) in enumerate(grams):
        other = swap(other)
        sums.append([mine[lo:hi] + other[lo:hi] for lo, hi in zip(CUTS[chunk], CUTS[chunk][1:])])
    for turn in range(3):
        sums = [[x + across(x, i + turn) for i, x in enumerate(parts)] for parts in sums]
    sums = [parts + [swap(x) for x in parts] for parts in sums]
    tile, tall = (B, B), (6 * B, B)
    state = call(
        first_kernel,
        "first",
        [f32(16, B), f32(*tall), f32(*tall), f32(*tile), f32(256, B), f32(256, B)],
        (core, *sums[0], *rows),
        scratch((STAT + 16, B), (8, B), tile) + wide((B, 6 * B)) + scratch(tile, tile) + wide((B, 6 * B)) + scratch((256, B)) + wide((256, 6 * B)),
    )
    white = call(
        second_kernel,
        "second",
        [f32(64, 1024)] * 4,
        (core, *sums[1], *state, *rows),
        scratch((2 * HALVES[1], B), (8, B), tile)
        + wide((B, 6 * B))
        + scratch(tile, (8 * B, B), (8, 256, B))
        + wide((256, 12 * B), (8 * B, 12 * B), (8 * B, 12 * B)),
    )
    white = exchange(white)
    return call(unpack_kernel, "unpack", f32(B, 1024), (sel, *white, *[swap(x) for x in white]), mib=12, scalars=0)


def solution(mesh):
    placed = (P(AXES, None), P(AXES, None), P(AXES, None))
    return jax.shard_map(local, mesh=mesh, in_specs=placed, out_specs=P(AXES, None), check_vma=False)
```

```python
import functools

import jax
import jax.numpy as jnp
from jax import lax
from jax.experimental import pallas as pl
from jax.experimental.pallas import tpu as pltpu
from jax.sharding import PartitionSpec as P


RIDGE = 0.1
SHIFT = 1.0
EMPTY = 1e30
B = 128
AXES = ("dom", "wide")


def coords(n):
    d, w = divmod(n, 16)
    return [w // 4, w % 4, d // 2, d % 2]


def number(c):
    x, y, z, core = c
    return (z * 2 + core) * 16 + x * 4 + y


CARRIED = ((4, 2, 1, 7), (3, 5, 6, 0))


def toward(n, turn):
    c = coords(n)
    mask = CARRIED[c[3]][turn]
    for axis, bit in ((0, 4), (1, 2), (2, 1)):
        if mask & bit:
            c[axis] = 3 - c[axis]
    return number(c)


def partner(n, axis):
    c = coords(n)
    c[axis] ^= 1
    return number(c)


def permute(x, to):
    return lax.ppermute(x, AXES, [(n, to(n)) for n in range(128)])


def iota(shape, axis):
    return lax.broadcasted_iota(jnp.int32, shape, axis)


def split(x):
    high = x.astype(jnp.bfloat16)
    rest = x - high.astype(jnp.float32)
    middle = rest.astype(jnp.bfloat16)
    low = (rest - middle.astype(jnp.float32)).astype(jnp.bfloat16)
    return high, middle, low


def left(x):
    h, m, l = split(x)
    return jnp.concatenate([l, m, h, m, h, h], axis=1)


def right(x):
    h, m, l = split(x)
    return jnp.concatenate([h, m, l, h, m, h], axis=1)


def product(a, b):
    return lax.dot_general(a, b, (((1,), (1,)), ((), ())), preferred_element_type=jnp.float32)


def plain(a, b):
    return lax.dot_general(a, b, (((1,), (0,)), ((), ())), preferred_element_type=jnp.float32)


def pick(place, x):
    h, m, l = split(x)
    p = place.astype(jnp.bfloat16)
    return plain(jnp.concatenate([p, p, p], axis=1), jnp.concatenate([l, m, h], axis=0))


def pack_kernel(where_ref, small_ref, ids2_ref, x_ref, x2_ref, *refs):
    out_refs, sel_ref = refs[:4], refs[4]
    rows = x_ref.shape[0]
    core, home = where_ref[0], where_ref[1]
    earlier = jnp.where(iota((rows, rows), 0) < iota((rows, rows), 1), 1.0, 0.0).astype(jnp.bfloat16)

    def group_and_rank(ids):
        turned = ids ^ home
        group = jnp.zeros_like(turned)
        for place, mask in enumerate(CARRIED[0] + CARRIED[1]):
            group = jnp.where(turned == mask, place, group)
        group = group ^ (4 * core)
        group = jnp.broadcast_to(group.astype(jnp.float32), (8, rows))
        onehot = jnp.where(group == iota((8, rows), 0).astype(jnp.float32), 1.0, 0.0)
        counted = plain(onehot.astype(jnp.bfloat16), earlier)
        return group[0:1, :], jnp.sum(counted * onehot, axis=0, keepdims=True)

    group, rank = group_and_rank(small_ref[0:1, :])
    group2, rank2 = group_and_rank(ids2_ref[...])
    slot = jnp.concatenate([group * 64.0 + rank, group2 * 64.0 + 32.0 + rank2], axis=1)
    place = jnp.where(slot == iota((256, 2 * rows), 0).astype(jnp.float32), 1.0, 0.0)
    used = jnp.sum(place, axis=1, keepdims=True)
    packed = jnp.where(used > 0.5, pick(place, jnp.concatenate([x_ref[...], x2_ref[...]], axis=0)), EMPTY)
    for g in range(4):
        out_refs[g][...] = packed[g * 64 : (g + 1) * 64]
    home_slot = jnp.broadcast_to(group * 32.0 + rank, (rows, rows))
    want = jnp.broadcast_to(small_ref[1:2, :].astype(jnp.float32), (rows, rows)).T
    picked = jnp.where(want == iota((rows, rows), 1).astype(jnp.float32), home_slot, 0.0)
    sel_ref[...] = jnp.broadcast_to(jnp.sum(picked, axis=1, keepdims=True), (rows, rows))


CHUNKS = ((0, 2), (2, 8))
PLACE_IN = [{p: n for n, p in enumerate((i, k) for k in range(*cols) for i in range(k, 8))} for cols in CHUNKS]
STAT = len(PLACE_IN[0]) * B
HALVES = ((STAT + 16) // 2, len(PLACE_IN[1]) * B // 2)
CUTS = ((0, 648, 968), (0, 896, 1344))


def gram_kernel(chunk, core_ref, *refs):
    rows_refs, (mine_ref, other_ref), (xs, xl, flat) = refs[:4], refs[4:6], refs[6:]
    for g in range(4):
        x = rows_refs[g][...]
        live = x[:, 0:1] < 1e29
        xs[g * 64 : (g + 1) * 64, :] = jnp.where(live, x - SHIFT, 0.0)
    first, end = CHUNKS[chunk]
    if chunk == 0:
        total = jnp.sum(xs[...], axis=0, keepdims=True)
        flat[STAT : STAT + 8, :] = jnp.concatenate([total[:, j * B : (j + 1) * B] for j in range(8)], axis=0)
        live = [jnp.where(ref[:, 0:B] < 1e29, 1.0, 0.0) for ref in rows_refs]
        count = jnp.sum(jnp.concatenate(live, axis=0), axis=0, keepdims=True)
        flat[STAT + 8 : STAT + 16, :] = jnp.broadcast_to(count, (8, B))
    xl[first * B :, :] = left(xs[:, first * B :].T)
    for k in range(first, end, 2):
        h, m, l = split(xs[:, k * B : (k + 2) * B])
        two = plain(xl[k * B :, :], jnp.concatenate([h, m, l, h, m, h], axis=0))
        for c in range(2):
            n = PLACE_IN[chunk][k + c, k + c] * B
            flat[n : n + (8 - k - c) * B, :] = two[c * B :, c * B : (c + 1) * B]
    half = HALVES[chunk]
    for ref, which in ((mine_ref, core_ref[0]), (other_ref, 1 - core_ref[0])):
        ref[...] = flat[pl.ds(pl.multiple_of(which * half, 8), half), :]


def row_of(x, j):
    return jnp.broadcast_to(x[j : j + 1, :], x.shape)


def col_of(x, j):
    return jnp.broadcast_to(x[:, j : j + 1], x.shape)


def inverse_factor(block, one, out_ref, between):
    sub = iota((8, B), 0)
    lane = iota((8, B), 1)
    groups = B // 8
    s = [block(g) for g in range(groups)]
    t = [jnp.where(lane == sub + 8 * g, 1.0, 0.0) for g in range(groups)]

    def eliminate(e0, e1, c, ahead, rows):
        v = jnp.zeros((8, B), jnp.float32)
        invs = []
        for j in range(8):
            top = {k: row_of(c[k], j) for k in range(j, 8)}
            inv = 1.0 / top[j]
            invs.append(inv)
            here = sub == j
            b0, b1 = row_of(e0, j), row_of(e1, j)
            m = jnp.where(here, 0.0, c[j] * inv)
            for k in range(j + 1, 8):
                c[k] = c[k] - m * top[k]
            v = jnp.where(here, b1 * lax.rsqrt(top[j]), v)
            e0 = e0 - m * b0
            e1 = e1 - m * b1
            if rows is not None:
                f0, f1, d = rows
                n = d[j] * inv
                f0, f1 = f0 - n * b0, f1 - n * b1
                for k in range(j + 1, 8):
                    d[k] = d[k] - n * top[k]
                for k in range(8):
                    r = row_of(ahead[k], j)
                    ahead[k] = ahead[k] - m * r
                    d[8 + k] = d[8 + k] - n * r
                rows = f0, f1, d
        scale = invs[7]
        for j in range(7):
            scale = jnp.where(sub == j, invs[j], scale)
        return v, e0 * scale, e1 * scale, rows

    def spread(x, first, count):
        return [col_of(x, first + j) * one for j in range(count)]

    def update(h, base, w0, w1):
        cols = [col_of(s[h], base + r) for r in range(8)]
        for r in range(8):
            s[h] = s[h] - cols[r] * w0[r]
            t[h] = t[h] - cols[r] * w1[r]

    for g in range(0, groups, 2):
        base = 8 * g
        near = range(g + 2, min(g + 4, groups))
        far = range(g + 4, groups)
        c = spread(s[g], base, 16)
        d = spread(s[g + 1], base, 16)
        v, p0, p1, (f0, f1, d) = eliminate(s[g], t[g], c[:8], c[8:], (s[g + 1], t[g + 1], d))
        out_ref[base : base + 8, :] = v
        if near:
            w0 = [row_of(p0, r) for r in range(8)]
            w1 = [row_of(p1, r) for r in range(8)]
        if far:
            below = jnp.concatenate([s[h] for h in far], axis=0)
            below = jnp.where(iota(below.shape, 1) >= base, below, 0.0)
            below = jnp.where(iota(below.shape, 1) < base + 16, below, 0.0)
        for h in near:
            update(h, base, w0, w1)
        between[g]()
        v, q0, q1, _ = eliminate(f0, f1, d[8:], None, None)
        out_ref[base + 8 : base + 16, :] = v
        if near:
            w0 = [row_of(q0, r) for r in range(8)]
            w1 = [row_of(q1, r) for r in range(8)]
            for h in near:
                update(h, base + 8, w0, w1)
        if far:
            fix = [col_of(p0, base + 8 + r) for r in range(8)]
            for r in range(8):
                p0 = p0 - fix[r] * w0[r]
                p1 = p1 - fix[r] * w1[r]
            parts = [jnp.concatenate([p0, p1], axis=1), jnp.concatenate([q0, q1], axis=1)]
            zero = jnp.zeros((8, 2 * B), jnp.float32)
            w = jnp.concatenate([parts[i - g] if g <= i < g + 2 else zero for i in range(groups)], axis=0)
            h, m, l = split(w)
            change = lax.dot_general(
                left(below), jnp.concatenate([h, m, l, h, m, h], axis=0), (((1,), (0,)), ((), ())), preferred_element_type=jnp.float32
            )
            for i, n in enumerate(far):
                s[n] = s[n] - change[8 * i : 8 * i + 8, :B]
                t[n] = t[n] - change[8 * i : 8 * i + 8, B:]
        between[g + 1]()


def gather_chunk(chunk, core, refs, flat):
    for which, ref in enumerate(refs):
        start = (which // 2 ^ core) * HALVES[chunk] + CUTS[chunk][which % 2]
        flat[pl.ds(pl.multiple_of(start, 8), ref.shape[0]), :] = ref[...]


def make_covariance(chunk, flat, mean, scale):
    mean_t = jnp.concatenate([mean, jnp.zeros((B - 8, B), jnp.float32)], axis=0).T
    eye = jnp.where(iota((B, B), 0) == iota((B, B), 1), RIDGE, 0.0)
    scale = jnp.broadcast_to(scale[0:1, :], (B, B))
    for (i, k), n in PLACE_IN[chunk].items():
        block = flat[n * B : (n + 1) * B, :] * scale
        block = block - jnp.broadcast_to(mean_t[:, i : i + 1], (B, B)) * mean[k : k + 1, :]
        flat[n * B : (n + 1) * B, :] = block + eye if i == k else block


def center_rows(rows_refs, mean, k):
    out = []
    for ref in rows_refs:
        live = ref[:, 0:1] < 1e29
        out.append(jnp.where(live, ref[:, k * B : (k + 1) * B] - SHIFT - mean[k : k + 1, :], 0.0))
    return jnp.concatenate(out, axis=0)


def leaf(block, ones, inv, work):
    slots = [[] for _ in range(16)]
    for i, piece in enumerate(work):
        slots[i * 16 // len(work)].append(piece)

    def run(pieces):
        for piece in pieces:
            piece()

    inverse_factor(lambda g: block[8 * g : 8 * g + 8, :], ones[...], inv, [functools.partial(run, p) for p in slots])


def in_a_region(scalar):
    return pl.when(scalar >= 0)


def first_kernel(core_ref, *refs):
    parts_refs, rows_refs, (stat_ref, col0_ref, col1_ref, inv_ref, z_ref, x_ref) = refs[:4], refs[4:8], refs[8:14]
    flat, ones, inv, inv_r, diagonal, first_r, x0, z_l = refs[14:]
    core = core_ref[0]
    gather_chunk(0, core, parts_refs, flat)
    scale = 1.0 / flat[STAT + 8 : STAT + 16, :]
    mean = flat[STAT : STAT + 8, :] * scale
    stat_ref[0:8, :] = mean
    stat_ref[8:16, :] = scale
    make_covariance(0, flat, mean, scale)
    ones[...] = jnp.ones((8, B), jnp.float32)

    @in_a_region(core)
    def _():
        def center(k, ref):
            ref[...] = center_rows(rows_refs, stat_ref[...], k)

        leaf(flat[0:B], ones, inv, [lambda: center(0, x0), lambda: center(1, x_ref)])
        inv_r[...] = right(inv[...])
        below = product(left(flat[B : 2 * B, :]), inv_r[...])
        first_r[...] = right(below)
        diagonal[...] = flat[8 * B : 9 * B, :] - product(left(below), first_r[...])

    @in_a_region(core)
    def _():
        def solve(j):
            p = product(left(flat[(2 + j) * B : (5 + j) * B, :]), inv_r[...])
            col0_ref[j * B : (j + 3) * B, :] = p

        def apply(j):
            change = product(left(col0_ref[j * B : (j + 3) * B, :]), first_r[...])
            col1_ref[j * B : (j + 3) * B, :] = flat[(9 + j) * B : (12 + j) * B, :] - change

        def whiten():
            z = product(left(x0[...]), inv_r[...])
            z_ref[...] = z
            z_l[...] = left(z)

        def down():
            x_ref[...] = x_ref[...] - product(z_l[...], first_r[...])

        work = [lambda: solve(0), lambda: solve(3), whiten, lambda: apply(0), lambda: apply(3), down]
        leaf(diagonal[...], ones, inv_ref, work)


def second_kernel(core_ref, *refs):
    parts_refs, (stat_ref, col0_ref, col1_ref, inv1_ref, z0_ref, x1_ref), rows_refs, out_refs = refs[:4], refs[4:10], refs[10:14], refs[14:18]
    flat, ones, inv, inv_r, diagonal, panel, x, z_l, rows_l, rows_r, white = refs[18:]
    core = core_ref[0]
    at = PLACE_IN[1]
    mean = stat_ref[0:8, :]
    gather_chunk(1, core, parts_refs, flat)
    make_covariance(1, flat, mean, stat_ref[8:16, :])
    ones[...] = jnp.ones((8, B), jnp.float32)
    inv_r[...] = right(inv1_ref[...])
    second = product(left(col1_ref[0:B, :]), inv_r[...])
    panel[2 * B : 3 * B, :] = second
    both_l = jnp.concatenate([left(col0_ref[0:B, :]), left(second)], axis=1)
    both_r = jnp.concatenate([right(col0_ref[0:B, :]), right(second)], axis=1)
    diagonal[...] = flat[0:B, :] - product(both_l, both_r)

    def start_of(k):
        row = jnp.int32(0)
        for j in range(3, 8):
            row = jnp.where(k == j, at[j, j] * B, row)
        return pl.multiple_of(row, B)

    def step(k, low):
        both = low == 2
        width = 12 * B if both else 6 * B

        def solve(lo, hi):
            if both:
                column = col1_ref[(1 + lo) * B : (1 + hi) * B, :]
                panel[(3 + lo) * B : (3 + hi) * B, :] = product(left(column), inv_r[...])
            else:
                size = (hi - lo) * B
                column = flat[pl.ds(start_of(k - 1) + (2 + lo) * B, size), :]
                panel[pl.ds(pl.multiple_of((k + 1 + lo) * B, B), size), :] = product(left(column), inv_r[...])

        def whiten():
            z = product(left(x1_ref[...] if both else x[k - 1]), inv_r[...])
            white[k - 1] = z
            if both:
                white[0] = z0_ref[...]
                z_l[:, : 6 * B] = left(z0_ref[...])
            z_l[:, width - 6 * B : width] = left(z)

        def center(j):
            x[j] = center_rows(rows_refs, stat_ref[...], j)

        def parts(lo, hi):
            if both:
                old = col0_ref[(lo - 2) * B : (hi - 2) * B, :]
                rows_l[lo * B : hi * B, : 6 * B] = left(old)
                rows_r[lo * B : hi * B, : 6 * B] = right(old)
            new = panel[lo * B : hi * B, :]
            rows_l[lo * B : hi * B, width - 6 * B : width] = left(new)
            rows_r[lo * B : hi * B, width - 6 * B : width] = right(new)

        def down(j):
            hi = min(j + 2, 8)
            change = product(z_l[:, :width], rows_r[j * B : hi * B, :width])
            for i in range(j, hi):
                x[i] = x[i] - change[:, (i - j) * B : (i - j + 1) * B]

        def update(j, lo, hi):
            top = min(j + 2, 8)
            change = product(rows_l[lo * B : hi * B, :width], rows_r[j * B : top * B, :width])
            for c in range(j, top):
                first = max(lo, c)
                n, size = at[first, c] * B, (hi - first) * B
                flat[n : n + size, :] = flat[n : n + size, :] - change[(first - lo) * B :, (c - j) * B : (c - j + 1) * B]

        def spans(lo, hi):
            return [(i, min(i + 3, hi)) for i in range(lo, hi, 3)]

        work = [functools.partial(solve, *span) for span in spans(0, 7 - low)]
        work += [whiten]
        work += [functools.partial(parts, *span) for span in spans(low, 8)]
        if both:
            work += [functools.partial(center, j) for j in range(2, 8)]
        columns = range(low, 8, 2)
        work += [functools.partial(update, j, *span) for j in columns for span in spans(j, 8)]
        work += [functools.partial(down, j) for j in columns]
        leaf(diagonal[...], ones, inv, work)
        inv_r[...] = right(inv[...])
        below = product(left(flat[pl.ds(start_of(k) + B, B), :]), inv_r[...])
        panel[pl.ds(pl.multiple_of((k + 1) * B, B), B), :] = below
        diagonal[...] = flat[pl.ds(start_of(jnp.minimum(k + 1, 7)), B), :] - product(left(below), right(below))

    in_a_region(core)(lambda: step(2, 2))
    pl.loop(3, 8)(lambda k: step(k, 3))
    white[7] = product(left(x[7]), inv_r[...])
    for k in range(8):
        for g in range(4):
            out_refs[g][:, k * B : (k + 1) * B] = white[k, g * 64 : (g + 1) * 64, :]


def unpack_kernel(sel_ref, *refs):
    own_refs, other_refs, out_ref = refs[:4], refs[4:8], refs[8]
    sel = sel_ref[...]
    lane = iota((B, 256), 1).astype(jnp.float32)
    place = jnp.where(jnp.concatenate([sel, sel], axis=1) == lane, 1.0, 0.0)
    out_ref[...] = pick(place, jnp.concatenate([r[:32, :] for r in own_refs] + [r[32:, :] for r in other_refs], axis=0))


VMEM = pl.BlockSpec(memory_space=pltpu.VMEM)
SMEM = pl.BlockSpec(memory_space=pltpu.SMEM)


def f32(*shape):
    return jax.ShapeDtypeStruct(shape, jnp.float32)


def call(kernel, outs, args, scratch=(), mib=24, scalars=1, flops=1000000):
    return pl.pallas_call(
        kernel,
        out_shape=outs,
        in_specs=[SMEM] * scalars + [VMEM] * (len(args) - scalars),
        out_specs=jax.tree.map(lambda _: VMEM, outs),
        scratch_shapes=scratch,
        cost_estimate=pl.CostEstimate(flops=flops, bytes_accessed=4000000, transcendentals=0),
        compiler_params=pltpu.CompilerParams(vmem_limit_bytes=mib << 20),
    )(*args)


def whiten(embeddings, domain_ids, order):
    d, w = lax.axis_index("dom"), lax.axis_index("wide")
    core = (d % 2).reshape(1).astype(jnp.int32)
    home = ((w // 8) * 4 + (w % 4) // 2 * 2 + d // 4).reshape(1).astype(jnp.int32)

    def swap(x):
        return permute(x, lambda n: partner(n, 3))

    def exchange(arrays):
        return [permute(x, lambda n, turn=turn: toward(n, turn)) for turn, x in enumerate(arrays)]

    ids = domain_ids.reshape(1, B)
    where = jnp.concatenate([core, home])
    *packed, sel = call(
        pack_kernel,
        [f32(64, 1024)] * 4 + [f32(B, B)],
        (where, jnp.concatenate([ids, order]), swap(ids), embeddings, swap(embeddings)),
        mib=12,
    )
    rows = exchange(packed)

    def scratch(*shapes, dtype=jnp.float32):
        return [pltpu.VMEM(shape, dtype) for shape in shapes]

    def wide(*shapes):
        return scratch(*shapes, dtype=jnp.bfloat16)

    def gram(chunk):
        half = HALVES[chunk]
        return call(
            functools.partial(gram_kernel, chunk),
            [f32(half, B)] * 2,
            (core, *rows),
            scratch((256, 1024)) + wide((1024, 1536)) + scratch((2 * half, B)),
        )

    def across(x, turn, i):
        return permute(x, lambda n: partner(n, (turn + (2 if i else coords(n)[3])) % 3))

    grams = [gram(chunk) for chunk in range(2)]
    sums = []
    for chunk, (mine, other) in enumerate(grams):
        other = swap(other)
        sums.append([mine[lo:hi] + other[lo:hi] for lo, hi in zip(CUTS[chunk], CUTS[chunk][1:])])

    def doubled(x, turn, i):
        partners = across(x, turn, i)
        return x + partners

    for turn in range(3):
        sums = [[doubled(x, turn, i) for i, x in enumerate(parts)] for parts in sums]
    sums = [parts + [swap(x) for x in parts] for parts in sums]
    tile, tall = (B, B), (6 * B, B)
    state = call(
        first_kernel,
        [f32(16, B), f32(*tall), f32(*tall), f32(*tile), f32(256, B), f32(256, B)],
        (core, *sums[0], *rows),
        scratch((STAT + 16, B), (8, B), tile) + wide((B, 6 * B)) + scratch(tile) + wide((B, 6 * B)) + scratch((256, B)) + wide((256, 6 * B)),
        flops=6000000000,
    )
    white = call(
        second_kernel,
        [f32(64, 1024)] * 4,
        (core, *sums[1], *state, *rows),
        scratch((2 * HALVES[1] + 8 * B, B), (8, B), tile)
        + wide((B, 6 * B))
        + scratch(tile, (14 * B, B), (8, 256, B))
        + wide((256, 12 * B), (8 * B, 12 * B), (8 * B, 12 * B))
        + scratch((8, 256, B)),
        flops=20000000000,
    )
    white = exchange(white)
    return call(unpack_kernel, f32(B, 1024), (sel, *white, *[swap(x) for x in white]), mib=12, scalars=0)


def solution(mesh):
    placed = (P(AXES, None), P(AXES, None), P(AXES, None))
    return jax.shard_map(whiten, mesh=mesh, in_specs=placed, out_specs=P(AXES, None), check_vma=False)
```

```python
import functools

import jax
import jax.numpy as jnp
from jax import lax
from jax.experimental import pallas as pl
from jax.experimental.pallas import tpu as pltpu
from jax.sharding import PartitionSpec as P


RIDGE = 0.1
SHIFT = 1.0
EMPTY = 1e30
B = 128
AXES = ("dom", "wide")


def coords(n):
    d, w = divmod(n, 16)
    return [w // 4, w % 4, d // 2, d % 2]


def number(c):
    x, y, z, core = c
    return (z * 2 + core) * 16 + x * 4 + y


CARRIED = ((7, 0, 4, 2), (3, 5, 6, 1))


def toward(n, turn):
    c = coords(n)
    mask = CARRIED[c[3]][turn]
    for axis, bit in ((0, 4), (1, 2), (2, 1)):
        if mask & bit:
            c[axis] = 3 - c[axis]
    return number(c)


def partner(n, axis):
    c = coords(n)
    c[axis] ^= 1
    return number(c)


def permute(x, to):
    return lax.ppermute(x, AXES, [(n, to(n)) for n in range(128)])


def iota(shape, axis):
    return lax.broadcasted_iota(jnp.int32, shape, axis)


def split(x):
    high = x.astype(jnp.bfloat16)
    rest = x - high.astype(jnp.float32)
    middle = rest.astype(jnp.bfloat16)
    low = (rest - middle.astype(jnp.float32)).astype(jnp.bfloat16)
    return high, middle, low


def left(x):
    h, m, l = split(x)
    return jnp.concatenate([l, m, h, m, h, h], axis=1)


def right(x):
    h, m, l = split(x)
    return jnp.concatenate([h, m, l, h, m, h], axis=1)


def product(a, b):
    return lax.dot_general(a, b, (((1,), (1,)), ((), ())), preferred_element_type=jnp.float32)


def plain(a, b):
    return lax.dot_general(a, b, (((1,), (0,)), ((), ())), preferred_element_type=jnp.float32)


def pick(place, x):
    h, m, l = split(x)
    p = place.astype(jnp.bfloat16)
    return plain(jnp.concatenate([p, p, p], axis=1), jnp.concatenate([l, m, h], axis=0))


def pack_kernel(where_ref, small_ref, ids2_ref, x_ref, x2_ref, *refs):
    out_refs, sel_ref = refs[:4], refs[4]
    rows = x_ref.shape[0]
    core, home = where_ref[0], where_ref[1]
    earlier = jnp.where(iota((rows, rows), 0) < iota((rows, rows), 1), 1.0, 0.0).astype(jnp.bfloat16)

    def group_and_rank(ids):
        turned = ids ^ home
        group = jnp.zeros_like(turned)
        for place, mask in enumerate(CARRIED[0] + CARRIED[1]):
            group = jnp.where(turned == mask, place, group)
        group = group ^ (4 * core)
        group = jnp.broadcast_to(group.astype(jnp.float32), (8, rows))
        onehot = jnp.where(group == iota((8, rows), 0).astype(jnp.float32), 1.0, 0.0)
        counted = plain(onehot.astype(jnp.bfloat16), earlier)
        return group[0:1, :], jnp.sum(counted * onehot, axis=0, keepdims=True)

    group, rank = group_and_rank(small_ref[0:1, :])
    group2, rank2 = group_and_rank(ids2_ref[...])
    slot = jnp.concatenate([group * 64.0 + rank, group2 * 64.0 + 32.0 + rank2], axis=1)
    place = jnp.where(slot == iota((256, 2 * rows), 0).astype(jnp.float32), 1.0, 0.0)
    used = jnp.sum(place, axis=1, keepdims=True)
    packed = jnp.where(used > 0.5, pick(place, jnp.concatenate([x_ref[...], x2_ref[...]], axis=0)), EMPTY)
    for g in range(4):
        out_refs[g][...] = packed[g * 64 : (g + 1) * 64]
    home_slot = jnp.broadcast_to(group * 32.0 + rank, (rows, rows))
    want = jnp.broadcast_to(small_ref[1:2, :].astype(jnp.float32), (rows, rows)).T
    picked = jnp.where(want == iota((rows, rows), 1).astype(jnp.float32), home_slot, 0.0)
    sel_ref[...] = jnp.broadcast_to(jnp.sum(picked, axis=1, keepdims=True), (rows, rows))


CHUNKS = ((0, 2), (2, 8))
PLACE_IN = [{p: n for n, p in enumerate((i, k) for k in range(*cols) for i in range(k, 8))} for cols in CHUNKS]
STAT = len(PLACE_IN[0]) * B
HALVES = ((STAT + 16) // 2, len(PLACE_IN[1]) * B // 2)
CUTS = ((0, 648, 968), (0, 896, 1344))


def gram_kernel(chunk, core_ref, *refs):
    rows_refs, (mine_ref, other_ref), (xs, xl, flat) = refs[:4], refs[4:6], refs[6:]
    for g in range(4):
        x = rows_refs[g][...]
        live = x[:, 0:1] < 1e29
        xs[g * 64 : (g + 1) * 64, :] = jnp.where(live, x - SHIFT, 0.0)
    first, end = CHUNKS[chunk]
    if chunk == 0:
        total = jnp.sum(xs[...], axis=0, keepdims=True)
        flat[STAT : STAT + 8, :] = jnp.concatenate([total[:, j * B : (j + 1) * B] for j in range(8)], axis=0)
        live = [jnp.where(ref[:, 0:B] < 1e29, 1.0, 0.0) for ref in rows_refs]
        count = jnp.sum(jnp.concatenate(live, axis=0), axis=0, keepdims=True)
        flat[STAT + 8 : STAT + 16, :] = jnp.broadcast_to(count, (8, B))
    xl[first * B :, :] = left(xs[:, first * B :].T)
    for k in range(first, end, 2):
        h, m, l = split(xs[:, k * B : (k + 2) * B])
        two = plain(xl[k * B :, :], jnp.concatenate([h, m, l, h, m, h], axis=0))
        for c in range(2):
            n = PLACE_IN[chunk][k + c, k + c] * B
            flat[n : n + (8 - k - c) * B, :] = two[c * B :, c * B : (c + 1) * B]
    half = HALVES[chunk]
    for ref, which in ((mine_ref, core_ref[0]), (other_ref, 1 - core_ref[0])):
        ref[...] = flat[pl.ds(pl.multiple_of(which * half, 8), half), :]


def row_of(x, j):
    return jnp.broadcast_to(x[j : j + 1, :], x.shape)


def col_of(x, j):
    return jnp.broadcast_to(x[:, j : j + 1], x.shape)


def inverse_factor(block, one, out_ref, between):
    sub = iota((8, B), 0)
    lane = iota((8, B), 1)
    groups = B // 8
    s = [block(g) for g in range(groups)]
    t = [jnp.where(lane == sub + 8 * g, 1.0, 0.0) for g in range(groups)]

    even = sub % 2 == 0

    def eliminate(e0, e1, c, rows):
        v = jnp.zeros((8, B), jnp.float32)
        straight = crossed = jnp.zeros((8, B), jnp.float32)
        for j in range(0, 8, 2):
            top = {k: row_of(c[k], j) for k in range(j, 8)}
            low = {k: row_of(c[k], j + 1) for k in range(j + 1, 8)}
            p, q, r = top[j], top[j + 1], low[j + 1]
            inv = 1.0 / (p * r - q * q)
            pair = (sub == j) | (sub == j + 1)

            def multipliers(x, y):
                return (r * x - q * y) * inv, (p * y - q * x) * inv

            def sides(x):
                return row_of(x, j), row_of(x, j + 1)

            x, y = jnp.where(pair, 0.0, c[j]), jnp.where(pair, 0.0, c[j + 1])
            for k in range(j + 2, min(j + 4, 8)):
                both = x * (r * top[k] - q * low[k]) + y * (p * low[k] - q * top[k])
                c[k] = c[k] - both * inv
            m, n = multipliers(x, y)
            for k in range(j + 4, 8):
                c[k] = c[k] - m * top[k] - n * low[k]
            (b0, d0), (b1, d1) = sides(e0), sides(e1)
            e0 = e0 - m * b0 - n * d0
            e1 = e1 - m * b1 - n * d1
            over = q * (1.0 / p)
            v = jnp.where(sub == j, b1 * lax.rsqrt(p), v)
            v = jnp.where(sub == j + 1, (d1 - over * b1) * lax.rsqrt(r - over * q), v)
            straight = jnp.where(pair, jnp.where(even, r, p) * inv, straight)
            crossed = jnp.where(pair, q * inv, crossed)
            if rows is not None:
                f0, f1, d = rows
                m, n = multipliers(d[j], d[j + 1])
                f0 = f0 - m * b0 - n * d0
                f1 = f1 - m * b1 - n * d1
                for k in range(j + 2, 8):
                    d[k] = d[k] - m * top[k] - n * low[k]
                for k in range(8):
                    d[8 + k] = d[8 + k] - m * row_of(d[j], k) - n * row_of(d[j + 1], k)
                rows = f0, f1, d

        def scaled(e):
            other = jnp.where(even, pltpu.roll(e, 7, 0), pltpu.roll(e, 1, 0))
            return e * straight - other * crossed

        return v, scaled(e0), scaled(e1), rows

    def spread(x, first, count):
        return [col_of(x, first + j) * one for j in range(count)]

    def update(h, base, w0, w1):
        cols = [col_of(s[h], base + r) for r in range(8)]
        for r in range(8):
            s[h] = s[h] - cols[r] * w0[r]
            t[h] = t[h] - cols[r] * w1[r]

    for g in range(0, groups, 2):
        base = 8 * g
        near = range(g + 2, min(g + 4, groups))
        far = range(g + 4, groups)
        c = spread(s[g], base, 8)
        d = spread(s[g + 1], base, 16)
        v, p0, p1, (f0, f1, d) = eliminate(s[g], t[g], c, (s[g + 1], t[g + 1], d))
        out_ref[base : base + 8, :] = v
        if near:
            w0 = [row_of(p0, r) for r in range(8)]
            w1 = [row_of(p1, r) for r in range(8)]
        if far:
            below = jnp.concatenate([s[h] for h in far], axis=0)
            below = jnp.where(iota(below.shape, 1) >= base, below, 0.0)
            below = jnp.where(iota(below.shape, 1) < base + 16, below, 0.0)
        for h in near:
            update(h, base, w0, w1)
        between[g]()
        v, q0, q1, _ = eliminate(f0, f1, d[8:], None)
        out_ref[base + 8 : base + 16, :] = v
        if near:
            w0 = [row_of(q0, r) for r in range(8)]
            w1 = [row_of(q1, r) for r in range(8)]
            for h in near:
                update(h, base + 8, w0, w1)
        if far:
            fix = [col_of(p0, base + 8 + r) for r in range(8)]
            for r in range(8):
                p0 = p0 - fix[r] * w0[r]
                p1 = p1 - fix[r] * w1[r]
            parts = [jnp.concatenate([p0, p1], axis=1), jnp.concatenate([q0, q1], axis=1)]
            zero = jnp.zeros((8, 2 * B), jnp.float32)
            w = jnp.concatenate([parts[i - g] if g <= i < g + 2 else zero for i in range(groups)], axis=0)
            h, m, l = split(w)
            change = lax.dot_general(
                left(below), jnp.concatenate([h, m, l, h, m, h], axis=0), (((1,), (0,)), ((), ())), preferred_element_type=jnp.float32
            )
            for i, n in enumerate(far):
                s[n] = s[n] - change[8 * i : 8 * i + 8, :B]
                t[n] = t[n] - change[8 * i : 8 * i + 8, B:]
        between[g + 1]()


def gather_chunk(chunk, core, refs, flat):
    for which, ref in enumerate(refs):
        start = (which // 2 ^ core) * HALVES[chunk] + CUTS[chunk][which % 2]
        flat[pl.ds(pl.multiple_of(start, 8), ref.shape[0]), :] = ref[...]


def make_covariance(chunk, flat, mean, scale):
    mean_t = jnp.concatenate([mean, jnp.zeros((B - 8, B), jnp.float32)], axis=0).T
    eye = jnp.where(iota((B, B), 0) == iota((B, B), 1), RIDGE, 0.0)
    scale = jnp.broadcast_to(scale[0:1, :], (B, B))
    for (i, k), n in PLACE_IN[chunk].items():
        block = flat[n * B : (n + 1) * B, :] * scale
        block = block - jnp.broadcast_to(mean_t[:, i : i + 1], (B, B)) * mean[k : k + 1, :]
        flat[n * B : (n + 1) * B, :] = block + eye if i == k else block


def center_rows(rows_refs, mean, k):
    out = []
    for ref in rows_refs:
        live = ref[:, 0:1] < 1e29
        out.append(jnp.where(live, ref[:, k * B : (k + 1) * B] - SHIFT - mean[k : k + 1, :], 0.0))
    return jnp.concatenate(out, axis=0)


def leaf(block, ones, inv, work):
    slots = [[] for _ in range(16)]
    for i, piece in enumerate(work):
        slots[i * 16 // len(work)].append(piece)

    def run(pieces):
        for piece in pieces:
            piece()

    inverse_factor(lambda g: block[8 * g : 8 * g + 8, :], ones[...], inv, [functools.partial(run, p) for p in slots])


def first_kernel(core_ref, *refs):
    parts_refs, rows_refs, (stat_ref, rows_l_ref, rows_r_ref, x_ref, z_ref) = refs[:4], refs[4:8], refs[8:13]
    flat, ones, inv, inv_r, diagonal, first_r, col0, col1, x, z_l = refs[13:]
    core = core_ref[0]
    gather_chunk(0, core, parts_refs, flat)
    scale = 1.0 / flat[STAT + 8 : STAT + 16, :]
    mean = flat[STAT : STAT + 8, :] * scale
    stat_ref[0:8, :] = mean
    stat_ref[8:16, :] = scale
    make_covariance(0, flat, mean, scale)
    ones[...] = jnp.ones((8, B), jnp.float32)

    def center(k):
        ref, n = (x, k) if k < 2 else (x_ref, k - 2)
        ref[n] = center_rows(rows_refs, stat_ref[...], k)

    leaf(flat[0:B], ones, inv, [functools.partial(center, k) for k in range(8)])
    inv_r[...] = right(inv[...])
    below = product(left(flat[B : 2 * B, :]), inv_r[...])
    first_r[...] = right(below)
    diagonal[...] = flat[8 * B : 9 * B, :] - product(left(below), first_r[...])

    def whiten(k):
        z = product(left(x[k]), inv_r[...])
        z_ref[k] = z
        z_l[...] = left(z)

    def parts(col, j, k):
        new = col[j * B : (j + 3) * B, :]
        rows_l_ref[j * B : (j + 3) * B, k * 6 * B : (k + 1) * 6 * B] = left(new)
        rows_r_ref[j * B : (j + 3) * B, k * 6 * B : (k + 1) * 6 * B] = right(new)

    def down(j, k):
        change = product(z_l[...], rows_r_ref[j * B : (j + 2) * B, k * 6 * B : (k + 1) * 6 * B])
        for i in range(2):
            x_ref[j + i] = x_ref[j + i] - change[:, i * B : (i + 1) * B]

    def solve(j):
        col0[j * B : (j + 3) * B, :] = product(left(flat[(2 + j) * B : (5 + j) * B, :]), inv_r[...])

    def apply(j):
        change = product(rows_l_ref[j * B : (j + 3) * B, : 6 * B], first_r[...])
        col1[j * B : (j + 3) * B, :] = flat[(9 + j) * B : (12 + j) * B, :] - change

    def down1():
        x[1] = x[1] - product(z_l[...], first_r[...])

    work = [functools.partial(solve, j) for j in (0, 3)]
    work += [functools.partial(parts, col0, j, 0) for j in (0, 3)]
    work += [functools.partial(apply, j) for j in (0, 3)]
    work += [functools.partial(whiten, 0), down1]
    work += [functools.partial(down, j, 0) for j in (0, 2, 4)]
    leaf(diagonal[...], ones, inv, work)
    inv_r[...] = right(inv[...])
    whiten(1)
    for j in (0, 3):
        col0[j * B : (j + 3) * B, :] = product(left(col1[j * B : (j + 3) * B, :]), inv_r[...])
        parts(col0, j, 1)
    for j in (0, 2, 4):
        down(j, 1)


def second_kernel(core_ref, *refs):
    parts_refs, (stat_ref, first_l, first_rr, x_ref, z_ref), out_refs = refs[:4], refs[4:9], refs[9:13]
    flat, ones, inv, inv_r, diagonal, panel, x, z_l, rows_l, rows_r, white = refs[13:]
    core = core_ref[0]
    at = PLACE_IN[1]
    gather_chunk(1, core, parts_refs, flat)
    make_covariance(1, flat, stat_ref[0:8, :], stat_ref[8:16, :])
    ones[...] = jnp.ones((8, B), jnp.float32)
    diagonal[...] = flat[0:B, :] - product(first_l[0:B, :], first_rr[0:B, :])

    def start_of(k):
        row = jnp.int32(0)
        for j in range(3, 8):
            row = jnp.where(k == j, at[j, j] * B, row)
        return pl.multiple_of(row, B)

    def update(left_ref, right_ref, skip, j, lo, hi):
        top = min(j + 2, 8)
        change = product(left_ref[(lo - skip) * B : (hi - skip) * B, :], right_ref[(j - skip) * B : (top - skip) * B, :])
        for c in range(j, top):
            first = max(lo, c)
            n, size = at[first, c] * B, (hi - first) * B
            flat[n : n + size, :] = flat[n : n + size, :] - change[(first - lo) * B :, (c - j) * B : (c - j + 1) * B]

    def spans(lo, hi):
        return [(i, min(i + 3, hi)) for i in range(lo, hi, 3)]

    def updates(left_ref, right_ref, skip, low):
        return [
            functools.partial(update, left_ref, right_ref, skip, j, *span) for j in range(low, 8, 2) for span in spans(j, 8)
        ]

    def advance(k):
        inv_r[...] = right(inv[...])
        below = product(left(flat[pl.ds(start_of(k) + B, B), :]), inv_r[...])
        panel[pl.ds(pl.multiple_of((k + 1) * B, B), B), :] = below
        diagonal[...] = flat[pl.ds(start_of(jnp.minimum(k + 1, 7)), B), :] - product(left(below), right(below))

    def take(j):
        x[j] = x_ref[j - 2]

    leaf(diagonal[...], ones, inv, updates(first_l, first_rr, 2, 2) + [functools.partial(take, j) for j in range(2, 8)])
    advance(2)

    @pl.loop(3, 8)
    def _(k):
        def solve(lo, hi):
            size = (hi - lo) * B
            column = flat[pl.ds(start_of(k - 1) + (2 + lo) * B, size), :]
            panel[pl.ds(pl.multiple_of((k + 1 + lo) * B, B), size), :] = product(left(column), inv_r[...])

        def whiten():
            z = product(left(x[k - 1]), inv_r[...])
            white[k - 1] = z
            z_l[...] = left(z)

        def parts(lo, hi):
            new = panel[lo * B : hi * B, :]
            rows_l[lo * B : hi * B, :] = left(new)
            rows_r[lo * B : hi * B, :] = right(new)

        def down(j):
            hi = min(j + 2, 8)
            change = product(z_l[...], rows_r[j * B : hi * B, :])
            for i in range(j, hi):
                x[i] = x[i] - change[:, (i - j) * B : (i - j + 1) * B]

        work = [functools.partial(solve, *span) for span in spans(0, 4)]
        work += [whiten]
        work += [functools.partial(parts, *span) for span in spans(3, 8)]
        work += updates(rows_l, rows_r, 0, 3)
        work += [functools.partial(down, j) for j in range(3, 8, 2)]
        leaf(diagonal[...], ones, inv, work)
        advance(k)

    white[7] = product(left(x[7]), inv_r[...])
    for k in range(8):
        for g in range(4):
            out_refs[g][:, k * B : (k + 1) * B] = (z_ref if k < 2 else white)[k, g * 64 : (g + 1) * 64, :]


def unpack_kernel(sel_ref, *refs):
    own_refs, other_refs, out_ref = refs[:4], refs[4:8], refs[8]
    sel = sel_ref[...]
    lane = iota((B, 256), 1).astype(jnp.float32)
    place = jnp.where(jnp.concatenate([sel, sel], axis=1) == lane, 1.0, 0.0)
    out_ref[...] = pick(place, jnp.concatenate([r[:32, :] for r in own_refs] + [r[32:, :] for r in other_refs], axis=0))


VMEM = pl.BlockSpec(memory_space=pltpu.VMEM)
SMEM = pl.BlockSpec(memory_space=pltpu.SMEM)


def f32(*shape):
    return jax.ShapeDtypeStruct(shape, jnp.float32)


def call(kernel, outs, args, scratch=(), mib=24, scalars=1, flops=1000000):
    return pl.pallas_call(
        kernel,
        out_shape=outs,
        in_specs=[SMEM] * scalars + [VMEM] * (len(args) - scalars),
        out_specs=jax.tree.map(lambda _: VMEM, outs),
        scratch_shapes=scratch,
        cost_estimate=pl.CostEstimate(flops=flops, bytes_accessed=4000000, transcendentals=0),
        compiler_params=pltpu.CompilerParams(vmem_limit_bytes=mib << 20),
    )(*args)


def whiten(embeddings, domain_ids, order):
    d, w = lax.axis_index("dom"), lax.axis_index("wide")
    core = (d % 2).reshape(1).astype(jnp.int32)
    home = ((w // 8) * 4 + (w % 4) // 2 * 2 + d // 4).reshape(1).astype(jnp.int32)

    def swap(x):
        return permute(x, lambda n: partner(n, 3))

    def exchange(arrays):
        return [permute(x, lambda n, turn=turn: toward(n, turn)) for turn, x in enumerate(arrays)]

    ids = domain_ids.reshape(1, B)
    where = jnp.concatenate([core, home])
    *packed, sel = call(
        pack_kernel,
        [f32(64, 1024)] * 4 + [f32(B, B)],
        (where, jnp.concatenate([ids, order]), swap(ids), embeddings, swap(embeddings)),
        mib=12,
    )
    rows = exchange(packed)

    def scratch(*shapes, dtype=jnp.float32):
        return [pltpu.VMEM(shape, dtype) for shape in shapes]

    def wide(*shapes):
        return scratch(*shapes, dtype=jnp.bfloat16)

    def gram(chunk):
        half = HALVES[chunk]
        return call(
            functools.partial(gram_kernel, chunk),
            [f32(half, B)] * 2,
            (core, *rows),
            scratch((256, 1024)) + wide((1024, 1536)) + scratch((2 * half, B)),
        )

    def across(x, turn, i):
        return permute(x, lambda n: partner(n, (turn + (2 if i else coords(n)[3])) % 3))

    grams = [gram(chunk) for chunk in range(2)]
    sums = []
    for chunk, (mine, other) in enumerate(grams):
        other = swap(other)
        sums.append([mine[lo:hi] + other[lo:hi] for lo, hi in zip(CUTS[chunk], CUTS[chunk][1:])])

    def doubled(x, turn, i):
        partners = across(x, turn, i)
        return x + partners

    for turn in range(3):
        sums = [[doubled(x, turn, i) for i, x in enumerate(parts)] for parts in sums]
    sums = [parts + [swap(x) for x in parts] for parts in sums]
    tile, tall = (B, B), (6 * B, B)

    def bf16(*shape):
        return jax.ShapeDtypeStruct(shape, jnp.bfloat16)

    state = call(
        first_kernel,
        [f32(16, B), bf16(6 * B, 12 * B), bf16(6 * B, 12 * B), f32(6, 256, B), f32(2, 256, B)],
        (core, *sums[0], *rows),
        scratch((STAT + 16, B), (8, B), tile)
        + wide((B, 6 * B))
        + scratch(tile)
        + wide((B, 6 * B))
        + scratch(tall, tall, (2, 256, B))
        + wide((256, 6 * B)),
        flops=6000000000,
    )
    white = call(
        second_kernel,
        [f32(64, 1024)] * 4,
        (core, *sums[1], *state),
        scratch((2 * HALVES[1] + 8 * B, B), (8, B), tile)
        + wide((B, 6 * B))
        + scratch(tile, (14 * B, B), (8, 256, B))
        + wide((256, 6 * B), (8 * B, 6 * B), (8 * B, 6 * B))
        + scratch((8, 256, B)),
        flops=20000000000,
    )
    white = exchange(white)
    return call(unpack_kernel, f32(B, 1024), (sel, *white, *[swap(x) for x in white]), mib=12, scalars=0)


def solution(mesh):
    placed = (P(AXES, None), P(AXES, None), P(AXES, None))
    return jax.shard_map(whiten, mesh=mesh, in_specs=placed, out_specs=P(AXES, None), check_vma=False)
```

```python
import functools

import jax
import jax.numpy as jnp
from jax import lax
from jax.experimental import pallas as pl
from jax.experimental.pallas import tpu as pltpu
from jax.sharding import PartitionSpec as P


RIDGE = 0.1
SHIFT = 1.0
EMPTY = 1e30
B = 128
AXES = ("dom", "wide")


def coords(n):
    d, w = divmod(n, 16)
    return [w // 4, w % 4, d // 2, d % 2]


def number(c):
    x, y, z, core = c
    return (z * 2 + core) * 16 + x * 4 + y


CARRIED = ((7, 0, 4, 2), (3, 5, 6, 1))


def toward(n, turn):
    c = coords(n)
    mask = CARRIED[c[3]][turn]
    for axis, bit in ((0, 4), (1, 2), (2, 1)):
        if mask & bit:
            c[axis] = 3 - c[axis]
    return number(c)


def partner(n, axis):
    c = coords(n)
    c[axis] ^= 1
    return number(c)


def permute(x, to):
    return lax.ppermute(x, AXES, [(n, to(n)) for n in range(128)])


def iota(shape, axis):
    return lax.broadcasted_iota(jnp.int32, shape, axis)


def split(x):
    high = x.astype(jnp.bfloat16)
    rest = x - high.astype(jnp.float32)
    middle = rest.astype(jnp.bfloat16)
    low = (rest - middle.astype(jnp.float32)).astype(jnp.bfloat16)
    return high, middle, low


def left(x):
    h, m, l = split(x)
    return jnp.concatenate([l, m, h, m, h, h], axis=1)


def right(x):
    h, m, l = split(x)
    return jnp.concatenate([h, m, l, h, m, h], axis=1)


def product(a, b):
    return lax.dot_general(a, b, (((1,), (1,)), ((), ())), preferred_element_type=jnp.float32)


def plain(a, b):
    return lax.dot_general(a, b, (((1,), (0,)), ((), ())), preferred_element_type=jnp.float32)


def pick(place, x):
    h, m, l = split(x)
    p = place.astype(jnp.bfloat16)
    return plain(jnp.concatenate([p, p, p], axis=1), jnp.concatenate([l, m, h], axis=0))


def group_and_rank(where_ref, ids):
    rows = ids.shape[1]
    turned = ids ^ where_ref[1]
    group = jnp.zeros_like(turned)
    for place, mask in enumerate(CARRIED[0] + CARRIED[1]):
        group = jnp.where(turned == mask, place, group)
    group = jnp.broadcast_to((group ^ (4 * where_ref[0])).astype(jnp.float32), (8, rows))
    onehot = jnp.where(group == iota((8, rows), 0).astype(jnp.float32), 1.0, 0.0)
    earlier = jnp.where(iota((rows, rows), 0) < iota((rows, rows), 1), 1.0, 0.0).astype(jnp.bfloat16)
    counted = plain(onehot.astype(jnp.bfloat16), earlier)
    return group[0:1, :], jnp.sum(counted * onehot, axis=0, keepdims=True)


def packed(slot, x):
    place = jnp.where(slot == iota((B, slot.shape[1]), 0).astype(jnp.float32), 1.0, 0.0)
    return jnp.where(jnp.sum(place, axis=1, keepdims=True) > 0.5, pick(place, x), EMPTY)


def pack_kernel(where_ref, small_ref, x_ref, out_ref, sel_ref):
    rows = x_ref.shape[0]
    group, rank = group_and_rank(where_ref, small_ref[0:1, :])
    slot = group * 32.0 + rank
    out_ref[...] = packed(slot, x_ref[...])
    home_slot = jnp.broadcast_to(slot, (rows, rows))
    want = jnp.broadcast_to(small_ref[1:2, :].astype(jnp.float32), (rows, rows)).T
    picked = jnp.where(want == iota((rows, rows), 1).astype(jnp.float32), home_slot, 0.0)
    sel_ref[...] = jnp.broadcast_to(jnp.sum(picked, axis=1, keepdims=True), (rows, rows))


def merge_kernel(where_ref, ids_ref, x_ref, own_ref, *out_refs):
    group, rank = group_and_rank(where_ref, ids_ref[...])
    theirs = packed(group * 32.0 + rank, x_ref[...])
    for g, ref in enumerate(out_refs):
        ref[:32, :] = own_ref[g * 32 : (g + 1) * 32, :]
        ref[32:, :] = theirs[g * 32 : (g + 1) * 32]


CHUNKS = ((0, 2), (2, 8))
PLACE_IN = [{p: n for n, p in enumerate((i, k) for k in range(*cols) for i in range(k, 8))} for cols in CHUNKS]
STAT = len(PLACE_IN[0]) * B
HALVES = ((STAT + 32) // 2, len(PLACE_IN[1]) * B // 2)
CUTS = ((0, 640, 976), (0, 896, 1344))


def rows_of(chunk, info_ref, which, part, place):
    start, end = CUTS[chunk][part], CUTS[chunk][part + 1]
    size = (end - start) // 2
    bit = info_ref[1 + which] if part == 0 else info_ref[3]
    return pl.ds(pl.multiple_of(which * HALVES[chunk] + start + (place ^ bit) * size, 8), size)


def gram_kernel(chunk, core_ref, *refs):
    rows_refs, (mine_ref, other_ref), (xs, xl, flat) = refs[:4], refs[4:6], refs[6:]
    for g in range(4):
        x = rows_refs[g][...]
        live = x[:, 0:1] < 1e29
        xs[g * 64 : (g + 1) * 64, :] = jnp.where(live, x - SHIFT, 0.0)
    first, end = CHUNKS[chunk]
    if chunk == 0:
        total = jnp.sum(xs[...], axis=0, keepdims=True)
        flat[STAT : STAT + 8, :] = jnp.concatenate([total[:, j * B : (j + 1) * B] for j in range(8)], axis=0)
        live = [jnp.where(ref[:, 0:B] < 1e29, 1.0, 0.0) for ref in rows_refs]
        count = jnp.sum(jnp.concatenate(live, axis=0), axis=0, keepdims=True)
        flat[STAT + 8 : STAT + 16, :] = jnp.broadcast_to(count, (8, B))
        flat[STAT + 16 : STAT + 32, :] = jnp.zeros((16, B), jnp.float32)
    xl[first * B :, :] = left(xs[:, first * B :].T)
    for k in range(first, end, 2):
        h, m, l = split(xs[:, k * B : (k + 2) * B])
        two = plain(xl[k * B :, :], jnp.concatenate([h, m, l, h, m, h], axis=0))
        for c in range(2):
            n = PLACE_IN[chunk][k + c, k + c] * B
            flat[n : n + (8 - k - c) * B, :] = two[c * B :, c * B : (c + 1) * B]
    for ref, which in ((mine_ref, core_ref[0]), (other_ref, 1 - core_ref[0])):
        for part in range(2):
            start, end = CUTS[chunk][part : part + 2]
            for place, row in enumerate((start, (start + end) // 2)):
                rows = rows_of(chunk, core_ref, which, part, place)
                ref[row : row + rows.size, :] = flat[rows, :]


def row_of(x, j):
    return jnp.broadcast_to(x[j : j + 1, :], x.shape)


def col_of(x, j):
    return jnp.broadcast_to(x[:, j : j + 1], x.shape)


def inverse_factor(block, one, out_ref, between):
    sub = iota((8, B), 0)
    lane = iota((8, B), 1)
    groups = B // 8
    s = [block(g) for g in range(groups)]
    t = [jnp.where(lane == sub + 8 * g, 1.0, 0.0) for g in range(groups)]

    even = sub % 2 == 0

    def eliminate(e0, e1, c, rows):
        v = jnp.zeros((8, B), jnp.float32)
        straight = crossed = jnp.zeros((8, B), jnp.float32)
        for j in range(0, 8, 2):
            top = {k: row_of(c[k], j) for k in range(j, 8)}
            low = {k: row_of(c[k], j + 1) for k in range(j + 1, 8)}
            p, q, r = top[j], top[j + 1], low[j + 1]
            inv = 1.0 / (p * r - q * q)
            pair = (sub == j) | (sub == j + 1)

            def multipliers(x, y):
                return (r * x - q * y) * inv, (p * y - q * x) * inv

            def sides(x):
                return row_of(x, j), row_of(x, j + 1)

            x, y = jnp.where(pair, 0.0, c[j]), jnp.where(pair, 0.0, c[j + 1])
            for k in range(j + 2, min(j + 4, 8)):
                both = x * (r * top[k] - q * low[k]) + y * (p * low[k] - q * top[k])
                c[k] = c[k] - both * inv
            m, n = multipliers(x, y)
            for k in range(j + 4, 8):
                c[k] = c[k] - m * top[k] - n * low[k]
            (b0, d0), (b1, d1) = sides(e0), sides(e1)
            e0 = e0 - m * b0 - n * d0
            e1 = e1 - m * b1 - n * d1
            over = q * (1.0 / p)
            v = jnp.where(sub == j, b1 * lax.rsqrt(p), v)
            v = jnp.where(sub == j + 1, (d1 - over * b1) * lax.rsqrt(r - over * q), v)
            straight = jnp.where(pair, jnp.where(even, r, p) * inv, straight)
            crossed = jnp.where(pair, q * inv, crossed)
            if rows is not None:
                f0, f1, d = rows
                m, n = multipliers(d[j], d[j + 1])
                f0 = f0 - m * b0 - n * d0
                f1 = f1 - m * b1 - n * d1
                for k in range(j + 2, 8):
                    d[k] = d[k] - m * top[k] - n * low[k]
                for k in range(8):
                    d[8 + k] = d[8 + k] - m * row_of(d[j], k) - n * row_of(d[j + 1], k)
                rows = f0, f1, d

        def scaled(e):
            other = jnp.where(even, pltpu.roll(e, 7, 0), pltpu.roll(e, 1, 0))
            return e * straight - other * crossed

        return v, scaled(e0), scaled(e1), rows

    def spread(x, first, count):
        return [col_of(x, first + j) * one for j in range(count)]

    def update(h, base, w0, w1):
        cols = [col_of(s[h], base + r) for r in range(8)]
        for r in range(8):
            s[h] = s[h] - cols[r] * w0[r]
            t[h] = t[h] - cols[r] * w1[r]

    for g in range(0, groups, 2):
        base = 8 * g
        near = range(g + 2, min(g + 4, groups))
        far = range(g + 4, groups)
        c = spread(s[g], base, 8)
        d = spread(s[g + 1], base, 16)
        v, p0, p1, (f0, f1, d) = eliminate(s[g], t[g], c, (s[g + 1], t[g + 1], d))
        out_ref[base : base + 8, :] = v
        if near:
            w0 = [row_of(p0, r) for r in range(8)]
            w1 = [row_of(p1, r) for r in range(8)]
        if far:
            below = jnp.concatenate([s[h] for h in far], axis=0)
            below = jnp.where(iota(below.shape, 1) >= base, below, 0.0)
            below = jnp.where(iota(below.shape, 1) < base + 16, below, 0.0)
        for h in near:
            update(h, base, w0, w1)
        between[g]()
        v, q0, q1, _ = eliminate(f0, f1, d[8:], None)
        out_ref[base + 8 : base + 16, :] = v
        if near:
            w0 = [row_of(q0, r) for r in range(8)]
            w1 = [row_of(q1, r) for r in range(8)]
            for h in near:
                update(h, base + 8, w0, w1)
        if far:
            fix = [col_of(p0, base + 8 + r) for r in range(8)]
            for r in range(8):
                p0 = p0 - fix[r] * w0[r]
                p1 = p1 - fix[r] * w1[r]
            parts = [jnp.concatenate([p0, p1], axis=1), jnp.concatenate([q0, q1], axis=1)]
            zero = jnp.zeros((8, 2 * B), jnp.float32)
            w = jnp.concatenate([parts[i - g] if g <= i < g + 2 else zero for i in range(groups)], axis=0)
            h, m, l = split(w)
            change = lax.dot_general(
                left(below), jnp.concatenate([h, m, l, h, m, h], axis=0), (((1,), (0,)), ((), ())), preferred_element_type=jnp.float32
            )
            for i, n in enumerate(far):
                s[n] = s[n] - change[8 * i : 8 * i + 8, :B]
                t[n] = t[n] - change[8 * i : 8 * i + 8, B:]
        between[g + 1]()


def gather_chunk(chunk, info_ref, refs, flat):
    for n, ref in enumerate(refs):
        flat[rows_of(chunk, info_ref, n // 4 ^ info_ref[0], n % 2, n // 2 % 2), :] = ref[...]


def make_covariance(chunk, flat, mean, scale):
    mean_t = jnp.concatenate([mean, jnp.zeros((B - 8, B), jnp.float32)], axis=0).T
    eye = jnp.where(iota((B, B), 0) == iota((B, B), 1), RIDGE, 0.0)
    scale = jnp.broadcast_to(scale[0:1, :], (B, B))
    for (i, k), n in PLACE_IN[chunk].items():
        block = flat[n * B : (n + 1) * B, :] * scale
        block = block - jnp.broadcast_to(mean_t[:, i : i + 1], (B, B)) * mean[k : k + 1, :]
        flat[n * B : (n + 1) * B, :] = block + eye if i == k else block


def center_rows(rows_refs, mean, k):
    out = []
    for ref in rows_refs:
        live = ref[:, 0:1] < 1e29
        out.append(jnp.where(live, ref[:, k * B : (k + 1) * B] - SHIFT - mean[k : k + 1, :], 0.0))
    return jnp.concatenate(out, axis=0)


def leaf(block, ones, inv, work):
    slots = [[] for _ in range(16)]
    for i, piece in enumerate(work):
        slots[i * 16 // len(work)].append(piece)

    def run(pieces):
        for piece in pieces:
            piece()

    inverse_factor(lambda g: block[8 * g : 8 * g + 8, :], ones[...], inv, [functools.partial(run, p) for p in slots])


def first_kernel(core_ref, *refs):
    parts_refs, rows_refs, (stat_ref, rows_l_ref, rows_r_ref, x_ref, z_ref) = refs[:8], refs[8:12], refs[12:17]
    flat, ones, inv, inv_r, diagonal, first_r, col0, col1, x, z_l = refs[17:]
    gather_chunk(0, core_ref, parts_refs, flat)
    scale = 1.0 / flat[STAT + 8 : STAT + 16, :]
    mean = flat[STAT : STAT + 8, :] * scale
    stat_ref[0:8, :] = mean
    stat_ref[8:16, :] = scale
    make_covariance(0, flat, mean, scale)
    ones[...] = jnp.ones((8, B), jnp.float32)

    def center(k):
        ref, n = (x, k) if k < 2 else (x_ref, k - 2)
        ref[n] = center_rows(rows_refs, stat_ref[...], k)

    leaf(flat[0:B], ones, inv, [functools.partial(center, k) for k in range(8)])
    inv_r[...] = right(inv[...])
    below = product(left(flat[B : 2 * B, :]), inv_r[...])
    first_r[...] = right(below)
    diagonal[...] = flat[8 * B : 9 * B, :] - product(left(below), first_r[...])

    def whiten(k):
        z = product(left(x[k]), inv_r[...])
        z_ref[k] = z
        z_l[...] = left(z)

    def parts(col, j, k):
        new = col[j * B : (j + 3) * B, :]
        rows_l_ref[j * B : (j + 3) * B, k * 6 * B : (k + 1) * 6 * B] = left(new)
        rows_r_ref[j * B : (j + 3) * B, k * 6 * B : (k + 1) * 6 * B] = right(new)

    def down(j, k):
        change = product(z_l[...], rows_r_ref[j * B : (j + 2) * B, k * 6 * B : (k + 1) * 6 * B])
        for i in range(2):
            x_ref[j + i] = x_ref[j + i] - change[:, i * B : (i + 1) * B]

    def solve(j):
        col0[j * B : (j + 3) * B, :] = product(left(flat[(2 + j) * B : (5 + j) * B, :]), inv_r[...])

    def apply(j):
        change = product(rows_l_ref[j * B : (j + 3) * B, : 6 * B], first_r[...])
        col1[j * B : (j + 3) * B, :] = flat[(9 + j) * B : (12 + j) * B, :] - change

    def down1():
        x[1] = x[1] - product(z_l[...], first_r[...])

    work = [functools.partial(solve, j) for j in (0, 3)]
    work += [functools.partial(parts, col0, j, 0) for j in (0, 3)]
    work += [functools.partial(apply, j) for j in (0, 3)]
    work += [functools.partial(whiten, 0), down1]
    work += [functools.partial(down, j, 0) for j in (0, 2, 4)]
    leaf(diagonal[...], ones, inv, work)
    inv_r[...] = right(inv[...])
    whiten(1)
    for j in (0, 3):
        col0[j * B : (j + 3) * B, :] = product(left(col1[j * B : (j + 3) * B, :]), inv_r[...])
        parts(col0, j, 1)
    for j in (0, 2, 4):
        down(j, 1)


def second_kernel(core_ref, *refs):
    parts_refs, (stat_ref, first_l, first_rr, x_ref, z_ref), out_refs = refs[:8], refs[8:13], refs[13:17]
    flat, ones, inv, inv_r, diagonal, panel, x, z_l, rows_l, rows_r, white = refs[17:]
    at = PLACE_IN[1]
    gather_chunk(1, core_ref, parts_refs, flat)
    make_covariance(1, flat, stat_ref[0:8, :], stat_ref[8:16, :])
    ones[...] = jnp.ones((8, B), jnp.float32)
    diagonal[...] = flat[0:B, :] - product(first_l[0:B, :], first_rr[0:B, :])

    def start_of(k):
        row = jnp.int32(0)
        for j in range(3, 8):
            row = jnp.where(k == j, at[j, j] * B, row)
        return pl.multiple_of(row, B)

    def update(left_ref, right_ref, skip, j, lo, hi):
        top = min(j + 2, 8)
        change = product(left_ref[(lo - skip) * B : (hi - skip) * B, :], right_ref[(j - skip) * B : (top - skip) * B, :])
        for c in range(j, top):
            first = max(lo, c)
            n, size = at[first, c] * B, (hi - first) * B
            flat[n : n + size, :] = flat[n : n + size, :] - change[(first - lo) * B :, (c - j) * B : (c - j + 1) * B]

    def spans(lo, hi):
        return [(i, min(i + 3, hi)) for i in range(lo, hi, 3)]

    def updates(left_ref, right_ref, skip, low):
        return [
            functools.partial(update, left_ref, right_ref, skip, j, *span) for j in range(low, 8, 2) for span in spans(j, 8)
        ]

    def advance(k):
        inv_r[...] = right(inv[...])
        below = product(left(flat[pl.ds(start_of(k) + B, B), :]), inv_r[...])
        panel[pl.ds(pl.multiple_of((k + 1) * B, B), B), :] = below
        diagonal[...] = flat[pl.ds(start_of(jnp.minimum(k + 1, 7)), B), :] - product(left(below), right(below))

    def take(j):
        x[j] = x_ref[j - 2]

    leaf(diagonal[...], ones, inv, updates(first_l, first_rr, 2, 2) + [functools.partial(take, j) for j in range(2, 8)])
    advance(2)

    @pl.loop(3, 8)
    def _(k):
        def solve(lo, hi):
            size = (hi - lo) * B
            column = flat[pl.ds(start_of(k - 1) + (2 + lo) * B, size), :]
            panel[pl.ds(pl.multiple_of((k + 1 + lo) * B, B), size), :] = product(left(column), inv_r[...])

        def whiten():
            z = product(left(x[k - 1]), inv_r[...])
            white[k - 1] = z
            z_l[...] = left(z)

        def parts(lo, hi):
            new = panel[lo * B : hi * B, :]
            rows_l[lo * B : hi * B, :] = left(new)
            rows_r[lo * B : hi * B, :] = right(new)

        def down(j):
            hi = min(j + 2, 8)
            change = product(z_l[...], rows_r[j * B : hi * B, :])
            for i in range(j, hi):
                x[i] = x[i] - change[:, (i - j) * B : (i - j + 1) * B]

        work = [functools.partial(solve, *span) for span in spans(0, 4)]
        work += [whiten]
        work += [functools.partial(parts, *span) for span in spans(3, 8)]
        work += updates(rows_l, rows_r, 0, 3)
        work += [functools.partial(down, j) for j in range(3, 8, 2)]
        leaf(diagonal[...], ones, inv, work)
        advance(k)

    white[7] = product(left(x[7]), inv_r[...])
    for k in range(8):
        for g in range(4):
            out_refs[g][:, k * B : (k + 1) * B] = (z_ref if k < 2 else white)[k, g * 64 : (g + 1) * 64, :]


def unpack_kernel(sel_ref, *refs):
    own_refs, other_refs, out_ref = refs[:4], refs[4:8], refs[8]
    sel = sel_ref[...]
    lane = iota((B, 256), 1).astype(jnp.float32)
    place = jnp.where(jnp.concatenate([sel, sel], axis=1) == lane, 1.0, 0.0)
    out_ref[...] = pick(place, jnp.concatenate([r[:32, :] for r in own_refs] + [r[32:, :] for r in other_refs], axis=0))


VMEM = pl.BlockSpec(memory_space=pltpu.VMEM)
SMEM = pl.BlockSpec(memory_space=pltpu.SMEM)


def f32(*shape):
    return jax.ShapeDtypeStruct(shape, jnp.float32)


def call(kernel, outs, args, scratch=(), mib=24, scalars=1, flops=1000000):
    return pl.pallas_call(
        kernel,
        out_shape=outs,
        in_specs=[SMEM] * scalars + [VMEM] * (len(args) - scalars),
        out_specs=jax.tree.map(lambda _: VMEM, outs),
        scratch_shapes=scratch,
        cost_estimate=pl.CostEstimate(flops=flops, bytes_accessed=4000000, transcendentals=0),
        compiler_params=pltpu.CompilerParams(vmem_limit_bytes=mib << 20),
    )(*args)


def whiten(embeddings, domain_ids, order):
    d, w = lax.axis_index("dom"), lax.axis_index("wide")
    core = (d % 2).reshape(1).astype(jnp.int32)
    home = ((w // 8) * 4 + (w % 4) // 2 * 2 + d // 4).reshape(1).astype(jnp.int32)

    def swap(x):
        return permute(x, lambda n: partner(n, 3))

    def exchange(arrays):
        return [permute(x, lambda n, turn=turn: toward(n, turn)) for turn, x in enumerate(arrays)]

    ids = domain_ids.reshape(1, B)
    where = jnp.concatenate([core, home])
    info = jnp.concatenate([core, jnp.stack([w // 4 % 2, w % 2, d // 2 % 2]).astype(jnp.int32)])
    their_rows = swap(embeddings)
    own, sel = call(
        pack_kernel,
        [f32(B, 1024), f32(B, B)],
        (where, jnp.concatenate([ids, order]), embeddings),
        mib=12,
        flops=1000000000,
    )
    rows = exchange(call(merge_kernel, [f32(64, 1024)] * 4, (where, swap(ids), their_rows, own), mib=12))

    def scratch(*shapes, dtype=jnp.float32):
        return [pltpu.VMEM(shape, dtype) for shape in shapes]

    def wide(*shapes):
        return scratch(*shapes, dtype=jnp.bfloat16)

    def gram(chunk):
        half = HALVES[chunk]
        return call(
            functools.partial(gram_kernel, chunk),
            [f32(half, B)] * 2,
            (info, *rows),
            scratch((256, 1024)) + wide((1024, 1536)) + scratch((2 * half, B)),
        )

    def across(x, turn, i):
        return permute(x, lambda n: partner(n, (turn + (2 if i else coords(n)[3])) % 3))

    grams = []
    for chunk in range(2):
        grams.append(gram(chunk))

    def doubled(mine, sent, turn, i):
        theirs = across(sent, turn, i)
        return mine + theirs

    kept, sent = [], []
    for chunk, (mine, other) in enumerate(grams):
        other = swap(other)
        cuts = [(lo, (lo + hi) // 2, hi) for lo, hi in zip(CUTS[chunk], CUTS[chunk][1:])]
        kept.append([mine[lo:mid] + other[lo:mid] for lo, mid, _ in cuts])
        sent.append([mine[mid:hi] + other[mid:hi] for _, mid, hi in cuts])
    for turn in range(3):
        kept = [
            [doubled(x, y, turn, i) for i, (x, y) in enumerate(zip(kept[chunk], sent[chunk]))]
            for chunk in range(2)
        ]
        sent = kept
    sums = []
    for chunk in range(2):
        parts = kept[chunk] + [across(x, 0, i) for i, x in enumerate(kept[chunk])]
        sums.append(parts + [swap(x) for x in parts])
    tile, tall = (B, B), (6 * B, B)

    def bf16(*shape):
        return jax.ShapeDtypeStruct(shape, jnp.bfloat16)

    state = call(
        first_kernel,
        [f32(16, B), bf16(6 * B, 12 * B), bf16(6 * B, 12 * B), f32(6, 256, B), f32(2, 256, B)],
        (info, *sums[0], *rows),
        scratch((STAT + 32, B), (8, B), tile)
        + wide((B, 6 * B))
        + scratch(tile)
        + wide((B, 6 * B))
        + scratch(tall, tall, (2, 256, B))
        + wide((256, 6 * B)),
        flops=6000000000,
    )
    white = call(
        second_kernel,
        [f32(64, 1024)] * 4,
        (info, *sums[1], *state),
        scratch((2 * HALVES[1] + 8 * B, B), (8, B), tile)
        + wide((B, 6 * B))
        + scratch(tile, (14 * B, B), (8, 256, B))
        + wide((256, 6 * B), (8 * B, 6 * B), (8 * B, 6 * B))
        + scratch((8, 256, B)),
        flops=20000000000,
    )
    white = exchange(white)
    return call(unpack_kernel, f32(B, 1024), (sel, *white, *[swap(x) for x in white]), mib=12, scalars=0)


def solution(mesh):
    placed = (P(AXES, None), P(AXES, None), P(AXES, None))
    return jax.shard_map(whiten, mesh=mesh, in_specs=placed, out_specs=P(AXES, None), check_vma=False)
```

```python
import functools

import jax
import jax.numpy as jnp
from jax import lax
from jax.experimental import pallas as pl
from jax.experimental.pallas import tpu as pltpu
from jax.sharding import PartitionSpec as P


RIDGE = 0.1
SHIFT = 1.0
EMPTY = 1e30
B = 128
AXES = ("dom", "wide")


def coords(n):
    d, w = divmod(n, 16)
    return [w // 4, w % 4, d // 2, d % 2]


def number(c):
    x, y, z, core = c
    return (z * 2 + core) * 16 + x * 4 + y


CARRIED = ((7, 0, 4, 2), (3, 5, 6, 1))


def toward(n, turn):
    c = coords(n)
    mask = CARRIED[c[3]][turn]
    for axis, bit in ((0, 4), (1, 2), (2, 1)):
        if mask & bit:
            c[axis] = 3 - c[axis]
    return number(c)


def partner(n, axis):
    c = coords(n)
    c[axis] ^= 1
    return number(c)


def permute(x, to):
    return lax.ppermute(x, AXES, [(n, to(n)) for n in range(128)])


def iota(shape, axis):
    return lax.broadcasted_iota(jnp.int32, shape, axis)


def split(x):
    high = x.astype(jnp.bfloat16)
    rest = x - high.astype(jnp.float32)
    middle = rest.astype(jnp.bfloat16)
    low = (rest - middle.astype(jnp.float32)).astype(jnp.bfloat16)
    return high, middle, low


def left(x):
    h, m, l = split(x)
    return jnp.concatenate([l, m, h, m, h, h], axis=1)


def right(x):
    h, m, l = split(x)
    return jnp.concatenate([h, m, l, h, m, h], axis=1)


def product(a, b):
    return lax.dot_general(a, b, (((1,), (1,)), ((), ())), preferred_element_type=jnp.float32)


def plain(a, b):
    return lax.dot_general(a, b, (((1,), (0,)), ((), ())), preferred_element_type=jnp.float32)


def pick(place, x):
    h, m, l = split(x)
    p = place.astype(jnp.bfloat16)
    return plain(jnp.concatenate([p, p, p], axis=1), jnp.concatenate([l, m, h], axis=0))


def group_and_rank(where_ref, ids):
    rows = ids.shape[1]
    turned = ids ^ where_ref[1]
    group = jnp.zeros_like(turned)
    for place, mask in enumerate(CARRIED[0] + CARRIED[1]):
        group = jnp.where(turned == mask, place, group)
    group = jnp.broadcast_to((group ^ (4 * where_ref[0])).astype(jnp.float32), (8, rows))
    onehot = jnp.where(group == iota((8, rows), 0).astype(jnp.float32), 1.0, 0.0)
    earlier = jnp.where(iota((rows, rows), 0) < iota((rows, rows), 1), 1.0, 0.0).astype(jnp.bfloat16)
    counted = plain(onehot.astype(jnp.bfloat16), earlier)
    return group[0:1, :], jnp.sum(counted * onehot, axis=0, keepdims=True)


def packed(slot, x):
    place = jnp.where(slot == iota((B, slot.shape[1]), 0).astype(jnp.float32), 1.0, 0.0)
    return jnp.where(jnp.sum(place, axis=1, keepdims=True) > 0.5, pick(place, x), EMPTY)


def pack_kernel(where_ref, small_ref, x_ref, out_ref, sel_ref):
    rows = x_ref.shape[0]
    group, rank = group_and_rank(where_ref, small_ref[0:1, :])
    slot = group * 32.0 + rank
    out_ref[...] = packed(slot, x_ref[...])
    home_slot = jnp.broadcast_to(slot, (rows, rows))
    want = jnp.broadcast_to(small_ref[1:2, :].astype(jnp.float32), (rows, rows)).T
    picked = jnp.where(want == iota((rows, rows), 1).astype(jnp.float32), home_slot, 0.0)
    sel_ref[...] = jnp.broadcast_to(jnp.sum(picked, axis=1, keepdims=True), (rows, rows))


def merge_kernel(where_ref, ids_ref, x_ref, own_ref, *out_refs):
    group, rank = group_and_rank(where_ref, ids_ref[...])
    theirs = packed(group * 32.0 + rank, x_ref[...])
    for g, ref in enumerate(out_refs):
        ref[:32, :] = own_ref[g * 32 : (g + 1) * 32, :]
        ref[32:, :] = theirs[g * 32 : (g + 1) * 32]


CHUNKS = ((0, 2), (2, 8))
PLACE_IN = [{p: n for n, p in enumerate((i, k) for k in range(*cols) for i in range(k, 8))} for cols in CHUNKS]
STAT = len(PLACE_IN[0]) * B
HALVES = ((STAT + 16) // 2, len(PLACE_IN[1]) * B // 2)
CUTS = ((0, 648, 968), (0, 896, 1344))


def gram_kernel(chunk, core_ref, *refs):
    rows_refs, (mine_ref, other_ref), (xs, xl, flat) = refs[:4], refs[4:6], refs[6:]
    for g in range(4):
        x = rows_refs[g][...]
        live = x[:, 0:1] < 1e29
        xs[g * 64 : (g + 1) * 64, :] = jnp.where(live, x - SHIFT, 0.0)
    first, end = CHUNKS[chunk]
    if chunk == 0:
        total = jnp.sum(xs[...], axis=0, keepdims=True)
        flat[STAT : STAT + 8, :] = jnp.concatenate([total[:, j * B : (j + 1) * B] for j in range(8)], axis=0)
        live = [jnp.where(ref[:, 0:B] < 1e29, 1.0, 0.0) for ref in rows_refs]
        count = jnp.sum(jnp.concatenate(live, axis=0), axis=0, keepdims=True)
        flat[STAT + 8 : STAT + 16, :] = jnp.broadcast_to(count, (8, B))
    xl[first * B :, :] = left(xs[:, first * B :].T)
    for k in range(first, end, 2):
        h, m, l = split(xs[:, k * B : (k + 2) * B])
        two = plain(xl[k * B :, :], jnp.concatenate([h, m, l, h, m, h], axis=0))
        for c in range(2):
            n = PLACE_IN[chunk][k + c, k + c] * B
            flat[n : n + (8 - k - c) * B, :] = two[c * B :, c * B : (c + 1) * B]
    half = HALVES[chunk]
    for ref, which in ((mine_ref, core_ref[0]), (other_ref, 1 - core_ref[0])):
        ref[...] = flat[pl.ds(pl.multiple_of(which * half, 8), half), :]


def row_of(x, j):
    return jnp.broadcast_to(x[j : j + 1, :], x.shape)


def col_of(x, j):
    return jnp.broadcast_to(x[:, j : j + 1], x.shape)


def inverse_factor(block, one, out_ref, between):
    sub = iota((8, B), 0)
    lane = iota((8, B), 1)
    groups = B // 8
    s = [block(g) for g in range(groups)]
    t = [jnp.where(lane == sub + 8 * g, 1.0, 0.0) for g in range(groups)]

    even = sub % 2 == 0

    def eliminate(e0, e1, c, rows):
        v = jnp.zeros((8, B), jnp.float32)
        straight = crossed = jnp.zeros((8, B), jnp.float32)
        for j in range(0, 8, 2):
            top = {k: row_of(c[k], j) for k in range(j, 8)}
            low = {k: row_of(c[k], j + 1) for k in range(j + 1, 8)}
            p, q, r = top[j], top[j + 1], low[j + 1]
            inv = 1.0 / (p * r - q * q)
            pair = (sub == j) | (sub == j + 1)

            def multipliers(x, y):
                return (r * x - q * y) * inv, (p * y - q * x) * inv

            def sides(x):
                return row_of(x, j), row_of(x, j + 1)

            x, y = jnp.where(pair, 0.0, c[j]), jnp.where(pair, 0.0, c[j + 1])
            for k in range(j + 2, min(j + 4, 8)):
                both = x * (r * top[k] - q * low[k]) + y * (p * low[k] - q * top[k])
                c[k] = c[k] - both * inv
            m, n = multipliers(x, y)
            for k in range(j + 4, 8):
                c[k] = c[k] - m * top[k] - n * low[k]
            (b0, d0), (b1, d1) = sides(e0), sides(e1)
            e0 = e0 - m * b0 - n * d0
            e1 = e1 - m * b1 - n * d1
            over = q * (1.0 / p)
            v = jnp.where(sub == j, b1 * lax.rsqrt(p), v)
            v = jnp.where(sub == j + 1, (d1 - over * b1) * lax.rsqrt(r - over * q), v)
            straight = jnp.where(pair, jnp.where(even, r, p) * inv, straight)
            crossed = jnp.where(pair, q * inv, crossed)
            if rows is not None:
                f0, f1, d = rows
                m, n = multipliers(d[j], d[j + 1])
                f0 = f0 - m * b0 - n * d0
                f1 = f1 - m * b1 - n * d1
                for k in range(j + 2, 8):
                    d[k] = d[k] - m * top[k] - n * low[k]
                for k in range(8):
                    d[8 + k] = d[8 + k] - m * row_of(d[j], k) - n * row_of(d[j + 1], k)
                rows = f0, f1, d

        def scaled(e):
            other = jnp.where(even, pltpu.roll(e, 7, 0), pltpu.roll(e, 1, 0))
            return e * straight - other * crossed

        return v, scaled(e0), scaled(e1), rows

    def spread(x, first, count):
        return [col_of(x, first + j) * one for j in range(count)]

    def update(h, base, w0, w1):
        cols = [col_of(s[h], base + r) for r in range(8)]
        for r in range(8):
            s[h] = s[h] - cols[r] * w0[r]
            t[h] = t[h] - cols[r] * w1[r]

    for g in range(0, groups, 2):
        base = 8 * g
        near = range(g + 2, min(g + 4, groups))
        far = range(g + 4, groups)
        c = spread(s[g], base, 8)
        d = spread(s[g + 1], base, 16)
        v, p0, p1, (f0, f1, d) = eliminate(s[g], t[g], c, (s[g + 1], t[g + 1], d))
        out_ref[base : base + 8, :] = v
        if near:
            w0 = [row_of(p0, r) for r in range(8)]
            w1 = [row_of(p1, r) for r in range(8)]
        if far:
            below = jnp.concatenate([s[h] for h in far], axis=0)
            below = jnp.where(iota(below.shape, 1) >= base, below, 0.0)
            below = jnp.where(iota(below.shape, 1) < base + 16, below, 0.0)
        for h in near:
            update(h, base, w0, w1)
        between[g]()
        v, q0, q1, _ = eliminate(f0, f1, d[8:], None)
        out_ref[base + 8 : base + 16, :] = v
        if near:
            w0 = [row_of(q0, r) for r in range(8)]
            w1 = [row_of(q1, r) for r in range(8)]
            for h in near:
                update(h, base + 8, w0, w1)
        if far:
            fix = [col_of(p0, base + 8 + r) for r in range(8)]
            for r in range(8):
                p0 = p0 - fix[r] * w0[r]
                p1 = p1 - fix[r] * w1[r]
            parts = [jnp.concatenate([p0, p1], axis=1), jnp.concatenate([q0, q1], axis=1)]
            zero = jnp.zeros((8, 2 * B), jnp.float32)
            w = jnp.concatenate([parts[i - g] if g <= i < g + 2 else zero for i in range(groups)], axis=0)
            h, m, l = split(w)
            change = lax.dot_general(
                left(below), jnp.concatenate([h, m, l, h, m, h], axis=0), (((1,), (0,)), ((), ())), preferred_element_type=jnp.float32
            )
            for i, n in enumerate(far):
                s[n] = s[n] - change[8 * i : 8 * i + 8, :B]
                t[n] = t[n] - change[8 * i : 8 * i + 8, B:]
        between[g + 1]()


def gather_chunk(chunk, core, refs, flat):
    for which, ref in enumerate(refs):
        start = (which // 2 ^ core) * HALVES[chunk] + CUTS[chunk][which % 2]
        flat[pl.ds(pl.multiple_of(start, 8), ref.shape[0]), :] = ref[...]


def make_covariance(chunk, flat, mean, scale):
    mean_t = jnp.concatenate([mean, jnp.zeros((B - 8, B), jnp.float32)], axis=0).T
    eye = jnp.where(iota((B, B), 0) == iota((B, B), 1), RIDGE, 0.0)
    scale = jnp.broadcast_to(scale[0:1, :], (B, B))
    for (i, k), n in PLACE_IN[chunk].items():
        block = flat[n * B : (n + 1) * B, :] * scale
        block = block - jnp.broadcast_to(mean_t[:, i : i + 1], (B, B)) * mean[k : k + 1, :]
        flat[n * B : (n + 1) * B, :] = block + eye if i == k else block


def center_rows(rows_refs, mean, k):
    out = []
    for ref in rows_refs:
        live = ref[:, 0:1] < 1e29
        out.append(jnp.where(live, ref[:, k * B : (k + 1) * B] - SHIFT - mean[k : k + 1, :], 0.0))
    return jnp.concatenate(out, axis=0)


def leaf(block, ones, inv, work):
    slots = [[] for _ in range(16)]
    for i, piece in enumerate(work):
        slots[i * 16 // len(work)].append(piece)

    def run(pieces):
        for piece in pieces:
            piece()

    inverse_factor(lambda g: block[8 * g : 8 * g + 8, :], ones[...], inv, [functools.partial(run, p) for p in slots])


def column0_kernel(core_ref, *refs):
    parts_refs, rows_refs, (flat, stat_ref, inv, x_ref), (ones,) = refs[:4], refs[4:8], refs[8:12], refs[12:]
    gather_chunk(0, core_ref[0], parts_refs, flat)
    scale = 1.0 / flat[STAT + 8 : STAT + 16, :]
    mean = flat[STAT : STAT + 8, :] * scale
    stat_ref[0:8, :] = mean
    stat_ref[8:16, :] = scale
    make_covariance(0, flat, mean, scale)
    ones[...] = jnp.ones((8, B), jnp.float32)

    def center(k):
        x_ref[k] = center_rows(rows_refs, stat_ref[...], k)

    leaf(flat[0:B], ones, inv, [functools.partial(center, k) for k in range(8)])


def column1_kernel(flat, inv0, x, rows_l_ref, rows_r_ref, x_ref, z_ref, ones, inv, inv_r, diagonal, first_r, col0, col1, x1, z_l):
    ones[...] = jnp.ones((8, B), jnp.float32)
    inv_r[...] = right(inv0[...])
    below = product(left(flat[B : 2 * B, :]), inv_r[...])
    first_r[...] = right(below)
    diagonal[...] = flat[8 * B : 9 * B, :] - product(left(below), first_r[...])

    def whiten(k):
        z = product(left(x1[...] if k else x[0]), inv_r[...])
        z_ref[k] = z
        z_l[...] = left(z)

    def parts(col, j, k):
        new = col[j * B : (j + 3) * B, :]
        rows_l_ref[j * B : (j + 3) * B, k * 6 * B : (k + 1) * 6 * B] = left(new)
        rows_r_ref[j * B : (j + 3) * B, k * 6 * B : (k + 1) * 6 * B] = right(new)

    def down(j, k):
        change = product(z_l[...], rows_r_ref[j * B : (j + 2) * B, k * 6 * B : (k + 1) * 6 * B])
        for i in range(2):
            old = x_ref[j + i] if k else x[j + i + 2]
            x_ref[j + i] = old - change[:, i * B : (i + 1) * B]

    def solve(j):
        col0[j * B : (j + 3) * B, :] = product(left(flat[(2 + j) * B : (5 + j) * B, :]), inv_r[...])

    def apply(j):
        change = product(rows_l_ref[j * B : (j + 3) * B, : 6 * B], first_r[...])
        col1[j * B : (j + 3) * B, :] = flat[(9 + j) * B : (12 + j) * B, :] - change

    def down1():
        x1[...] = x[1] - product(z_l[...], first_r[...])

    work = [functools.partial(solve, j) for j in (0, 3)]
    work += [functools.partial(parts, col0, j, 0) for j in (0, 3)]
    work += [functools.partial(apply, j) for j in (0, 3)]
    work += [functools.partial(whiten, 0), down1]
    work += [functools.partial(down, j, 0) for j in (0, 2, 4)]
    leaf(diagonal[...], ones, inv, work)
    inv_r[...] = right(inv[...])
    whiten(1)
    for j in (0, 3):
        col0[j * B : (j + 3) * B, :] = product(left(col1[j * B : (j + 3) * B, :]), inv_r[...])
        parts(col0, j, 1)
    for j in (0, 2, 4):
        down(j, 1)


def second_kernel(core_ref, *refs):
    parts_refs, (stat_ref, first_l, first_rr, x_ref, z_ref), out_refs = refs[:4], refs[4:9], refs[9:13]
    flat, ones, inv, inv_r, diagonal, panel, x, z_l, rows_l, rows_r, white = refs[13:]
    core = core_ref[0]
    at = PLACE_IN[1]
    gather_chunk(1, core, parts_refs, flat)
    make_covariance(1, flat, stat_ref[0:8, :], stat_ref[8:16, :])
    ones[...] = jnp.ones((8, B), jnp.float32)
    diagonal[...] = flat[0:B, :] - product(first_l[0:B, :], first_rr[0:B, :])

    def start_of(k):
        row = jnp.int32(0)
        for j in range(3, 8):
            row = jnp.where(k == j, at[j, j] * B, row)
        return pl.multiple_of(row, B)

    def update(left_ref, right_ref, skip, j, lo, hi):
        top = min(j + 2, 8)
        change = product(left_ref[(lo - skip) * B : (hi - skip) * B, :], right_ref[(j - skip) * B : (top - skip) * B, :])
        for c in range(j, top):
            first = max(lo, c)
            n, size = at[first, c] * B, (hi - first) * B
            flat[n : n + size, :] = flat[n : n + size, :] - change[(first - lo) * B :, (c - j) * B : (c - j + 1) * B]

    def spans(lo, hi):
        return [(i, min(i + 3, hi)) for i in range(lo, hi, 3)]

    def updates(left_ref, right_ref, skip, low):
        return [
            functools.partial(update, left_ref, right_ref, skip, j, *span) for j in range(low, 8, 2) for span in spans(j, 8)
        ]

    def advance(k):
        inv_r[...] = right(inv[...])
        below = product(left(flat[pl.ds(start_of(k) + B, B), :]), inv_r[...])
        panel[pl.ds(pl.multiple_of((k + 1) * B, B), B), :] = below
        diagonal[...] = flat[pl.ds(start_of(jnp.minimum(k + 1, 7)), B), :] - product(left(below), right(below))

    def take(j):
        x[j] = x_ref[j - 2]

    leaf(diagonal[...], ones, inv, updates(first_l, first_rr, 2, 2) + [functools.partial(take, j) for j in range(2, 8)])
    advance(2)

    def step(low, k):
        def solve(lo, hi):
            size = (hi - lo) * B
            column = flat[pl.ds(start_of(k - 1) + (2 + lo) * B, size), :]
            panel[pl.ds(pl.multiple_of((k + 1 + lo) * B, B), size), :] = product(left(column), inv_r[...])

        def whiten():
            z = product(left(x[k - 1]), inv_r[...])
            white[k - 1] = z
            z_l[...] = left(z)

        def parts(lo, hi):
            new = panel[lo * B : hi * B, :]
            rows_l[lo * B : hi * B, :] = left(new)
            rows_r[lo * B : hi * B, :] = right(new)

        def down(j):
            hi = min(j + 2, 8)
            change = product(z_l[...], rows_r[j * B : hi * B, :])
            for i in range(j, hi):
                x[i] = x[i] - change[:, (i - j) * B : (i - j + 1) * B]

        work = [functools.partial(solve, *span) for span in spans(0, 7 - low)]
        work += [whiten]
        work += [functools.partial(parts, *span) for span in spans(low, 8)]
        work += updates(rows_l, rows_r, 0, low)
        work += [functools.partial(down, j) for j in range(low, 8, 2)]
        leaf(diagonal[...], ones, inv, work)
        advance(k)

    for low, end in ((3, 5), (5, 8)):
        pl.loop(low, end)(functools.partial(step, low))
    white[7] = product(left(x[7]), inv_r[...])
    for k in range(8):
        for g in range(4):
            out_refs[g][:, k * B : (k + 1) * B] = (z_ref if k < 2 else white)[k, g * 64 : (g + 1) * 64, :]


def unpack_kernel(sel_ref, *refs):
    own_refs, other_refs, out_ref = refs[:4], refs[4:8], refs[8]
    sel = sel_ref[...]
    lane = iota((B, 256), 1).astype(jnp.float32)
    place = jnp.where(jnp.concatenate([sel, sel], axis=1) == lane, 1.0, 0.0)
    out_ref[...] = pick(place, jnp.concatenate([r[:32, :] for r in own_refs] + [r[32:, :] for r in other_refs], axis=0))


VMEM = pl.BlockSpec(memory_space=pltpu.VMEM)
SMEM = pl.BlockSpec(memory_space=pltpu.SMEM)


def f32(*shape):
    return jax.ShapeDtypeStruct(shape, jnp.float32)


def call(kernel, outs, args, scratch=(), mib=24, scalars=1, flops=1000000):
    return pl.pallas_call(
        kernel,
        out_shape=outs,
        in_specs=[SMEM] * scalars + [VMEM] * (len(args) - scalars),
        out_specs=jax.tree.map(lambda _: VMEM, outs),
        scratch_shapes=scratch,
        cost_estimate=pl.CostEstimate(flops=flops, bytes_accessed=4000000, transcendentals=0),
        compiler_params=pltpu.CompilerParams(vmem_limit_bytes=mib << 20),
    )(*args)


def whiten(embeddings, domain_ids, order):
    d, w = lax.axis_index("dom"), lax.axis_index("wide")
    core = (d % 2).reshape(1).astype(jnp.int32)
    home = ((w // 8) * 4 + (w % 4) // 2 * 2 + d // 4).reshape(1).astype(jnp.int32)

    def swap(x):
        return permute(x, lambda n: partner(n, 3))

    def exchange(arrays):
        return [permute(x, lambda n, turn=turn: toward(n, turn)) for turn, x in enumerate(arrays)]

    ids = domain_ids.reshape(1, B)
    where = jnp.concatenate([core, home])
    their_rows = swap(embeddings)
    own, sel = call(
        pack_kernel,
        [f32(B, 1024), f32(B, B)],
        (where, jnp.concatenate([ids, order]), embeddings),
        mib=12,
        flops=1000000000,
    )
    rows = exchange(call(merge_kernel, [f32(64, 1024)] * 4, (where, swap(ids), their_rows, own), mib=12))

    def scratch(*shapes, dtype=jnp.float32):
        return [pltpu.VMEM(shape, dtype) for shape in shapes]

    def wide(*shapes):
        return scratch(*shapes, dtype=jnp.bfloat16)

    def gram(chunk):
        half = HALVES[chunk]
        return call(
            functools.partial(gram_kernel, chunk),
            [f32(half, B)] * 2,
            (core, *rows),
            scratch((256, 1024)) + wide((1024, 1536)) + scratch((2 * half, B)),
        )

    def across(x, turn, i):
        return permute(x, lambda n: partner(n, (turn + (2 if i else coords(n)[3])) % 3))

    grams = []
    for chunk in range(2):
        grams.append(gram(chunk))

    sums = []
    for chunk, (mine, other) in enumerate(grams):
        other = swap(other)
        sums.append([mine[lo:hi] + other[lo:hi] for lo, hi in zip(CUTS[chunk], CUTS[chunk][1:])])

    def doubled(x, turn, i):
        partners = across(x, turn, i)
        return x + partners

    for turn in range(3):
        sums = [[doubled(x, turn, i) for i, x in enumerate(parts)] for parts in sums]
    for parts in sums:
        for i in range(2):
            parts.append(swap(parts[i]))
    tile, tall = (B, B), (6 * B, B)

    def bf16(*shape):
        return jax.ShapeDtypeStruct(shape, jnp.bfloat16)

    flat, stat, inv, x = call(
        column0_kernel,
        [f32(STAT + 16, B), f32(16, B), f32(*tile), f32(8, 256, B)],
        (core, *sums[0], *rows),
        scratch((8, B)),
        flops=3000000000,
    )
    state = call(
        column1_kernel,
        [bf16(6 * B, 12 * B), bf16(6 * B, 12 * B), f32(6, 256, B), f32(2, 256, B)],
        (flat, inv, x),
        scratch((8, B), tile)
        + wide((B, 6 * B))
        + scratch(tile)
        + wide((B, 6 * B))
        + scratch(tall, tall, (256, B))
        + wide((256, 6 * B)),
        scalars=0,
        flops=3000000000,
    )
    white = call(
        second_kernel,
        [f32(64, 1024)] * 4,
        (core, *sums[1], stat, *state),
        scratch((2 * HALVES[1] + 8 * B, B), (8, B), tile)
        + wide((B, 6 * B))
        + scratch(tile, (14 * B, B), (8, 256, B))
        + wide((256, 6 * B), (8 * B, 6 * B), (8 * B, 6 * B))
        + scratch((8, 256, B)),
        flops=20000000000,
    )
    white = exchange(white)
    return call(unpack_kernel, f32(B, 1024), (sel, *white, *[swap(x) for x in white]), mib=12, scalars=0)


def solution(mesh):
    placed = (P(AXES, None), P(AXES, None), P(AXES, None))
    return jax.shard_map(whiten, mesh=mesh, in_specs=placed, out_specs=P(AXES, None), check_vma=False)
```

```python
import functools

import jax
import jax.numpy as jnp
from jax import lax
from jax.experimental import pallas as pl
from jax.experimental.pallas import tpu as pltpu
from jax.sharding import PartitionSpec as P


RIDGE = 0.1
SHIFT = 1.0
EMPTY = 1e30
B = 128
AXES = ("dom", "wide")


def coords(n):
    d, w = divmod(n, 16)
    return [w // 4, w % 4, d // 2, d % 2]


def number(c):
    x, y, z, core = c
    return (z * 2 + core) * 16 + x * 4 + y


CARRIED = ((7, 0, 4, 2), (3, 5, 6, 1))


def toward(n, turn):
    c = coords(n)
    mask = CARRIED[c[3]][turn]
    for axis, bit in ((0, 4), (1, 2), (2, 1)):
        if mask & bit:
            c[axis] = 3 - c[axis]
    return number(c)


def partner(n, axis):
    c = coords(n)
    c[axis] ^= 1
    return number(c)


def permute(x, to):
    return lax.ppermute(x, AXES, [(n, to(n)) for n in range(128)])


def iota(shape, axis):
    return lax.broadcasted_iota(jnp.int32, shape, axis)


def split(x):
    high = x.astype(jnp.bfloat16)
    rest = x - high.astype(jnp.float32)
    middle = rest.astype(jnp.bfloat16)
    low = (rest - middle.astype(jnp.float32)).astype(jnp.bfloat16)
    return high, middle, low


def left(x):
    h, m, l = split(x)
    return jnp.concatenate([l, m, h, m, h, h], axis=1)


def right(x):
    h, m, l = split(x)
    return jnp.concatenate([h, m, l, h, m, h], axis=1)


def product(a, b):
    return lax.dot_general(a, b, (((1,), (1,)), ((), ())), preferred_element_type=jnp.float32)


def plain(a, b):
    return lax.dot_general(a, b, (((1,), (0,)), ((), ())), preferred_element_type=jnp.float32)


def pick(place, x):
    h, m, l = split(x)
    p = place.astype(jnp.bfloat16)
    return plain(jnp.concatenate([p, p, p], axis=1), jnp.concatenate([l, m, h], axis=0))


def group_and_rank(where_ref, ids):
    rows = ids.shape[1]
    turned = ids ^ where_ref[1]
    group = jnp.zeros_like(turned)
    for place, mask in enumerate(CARRIED[0] + CARRIED[1]):
        group = jnp.where(turned == mask, place, group)
    group = jnp.broadcast_to((group ^ (4 * where_ref[0])).astype(jnp.float32), (8, rows))
    onehot = jnp.where(group == iota((8, rows), 0).astype(jnp.float32), 1.0, 0.0)
    earlier = jnp.where(iota((rows, rows), 0) < iota((rows, rows), 1), 1.0, 0.0).astype(jnp.bfloat16)
    counted = plain(onehot.astype(jnp.bfloat16), earlier)
    return group[0:1, :], jnp.sum(counted * onehot, axis=0, keepdims=True)


def packed(slot, x):
    place = jnp.where(slot == iota((B, slot.shape[1]), 0).astype(jnp.float32), 1.0, 0.0)
    return jnp.where(jnp.sum(place, axis=1, keepdims=True) > 0.5, pick(place, x), EMPTY)


def pack_kernel(where_ref, small_ref, x_ref, out_ref, sel_ref):
    rows = x_ref.shape[0]
    group, rank = group_and_rank(where_ref, small_ref[0:1, :])
    slot = group * 32.0 + rank
    out_ref[...] = packed(slot, x_ref[...])
    home_slot = jnp.broadcast_to(slot, (rows, rows))
    want = jnp.broadcast_to(small_ref[1:2, :].astype(jnp.float32), (rows, rows)).T
    picked = jnp.where(want == iota((rows, rows), 1).astype(jnp.float32), home_slot, 0.0)
    sel_ref[...] = jnp.broadcast_to(jnp.sum(picked, axis=1, keepdims=True), (rows, rows))


def merge_kernel(where_ref, ids_ref, x_ref, own_ref, *out_refs):
    group, rank = group_and_rank(where_ref, ids_ref[...])
    theirs = packed(group * 32.0 + rank, x_ref[...])
    for g, ref in enumerate(out_refs):
        ref[:32, :] = own_ref[g * 32 : (g + 1) * 32, :]
        ref[32:, :] = theirs[g * 32 : (g + 1) * 32]


CHUNKS = ((0, 2), (2, 8))
PLACE_IN = [{p: n for n, p in enumerate((i, k) for k in range(*cols) for i in range(k, 8))} for cols in CHUNKS]
STAT = len(PLACE_IN[0]) * B
HALVES = ((STAT + 16) // 2, len(PLACE_IN[1]) * B // 2)
CUTS = ((0, 648, 968), (0, 896, 1344))


def rows_of(chunk, info_ref, which, part, place):
    start, end = CUTS[chunk][part], CUTS[chunk][part + 1]
    first, size = which * HALVES[chunk] + start, end - start
    if chunk == 1:
        size //= 2
        bit = info_ref[1 + which] if part == 0 else info_ref[3]
        first += (place ^ bit) * size
    return pl.ds(pl.multiple_of(first, 8), size)


def gram_kernel(chunk, core_ref, *refs):
    rows_refs, (mine_ref, other_ref), (xs, xl, flat) = refs[:4], refs[4:6], refs[6:]
    for g in range(4):
        x = rows_refs[g][...]
        live = x[:, 0:1] < 1e29
        xs[g * 64 : (g + 1) * 64, :] = jnp.where(live, x - SHIFT, 0.0)
    first, end = CHUNKS[chunk]
    if chunk == 0:
        total = jnp.sum(xs[...], axis=0, keepdims=True)
        flat[STAT : STAT + 8, :] = jnp.concatenate([total[:, j * B : (j + 1) * B] for j in range(8)], axis=0)
        live = [jnp.where(ref[:, 0:B] < 1e29, 1.0, 0.0) for ref in rows_refs]
        count = jnp.sum(jnp.concatenate(live, axis=0), axis=0, keepdims=True)
        flat[STAT + 8 : STAT + 16, :] = jnp.broadcast_to(count, (8, B))
    xl[first * B :, :] = left(xs[:, first * B :].T)
    for k in range(first, end, 2):
        h, m, l = split(xs[:, k * B : (k + 2) * B])
        two = plain(xl[k * B :, :], jnp.concatenate([h, m, l, h, m, h], axis=0))
        for c in range(2):
            n = PLACE_IN[chunk][k + c, k + c] * B
            flat[n : n + (8 - k - c) * B, :] = two[c * B :, c * B : (c + 1) * B]
    for ref, which in ((mine_ref, core_ref[0]), (other_ref, 1 - core_ref[0])):
        row = 0
        for part in range(2):
            for place in range(1 + chunk):
                rows = rows_of(chunk, core_ref, which, part, place)
                ref[row : row + rows.size, :] = flat[rows, :]
                row += rows.size


def row_of(x, j):
    return jnp.broadcast_to(x[j : j + 1, :], x.shape)


def col_of(x, j):
    return jnp.broadcast_to(x[:, j : j + 1], x.shape)


def inverse_factor(block, one, out_ref, between):
    sub = iota((8, B), 0)
    lane = iota((8, B), 1)
    groups = B // 8
    s = [block(g) for g in range(groups)]
    t = [jnp.where(lane == sub + 8 * g, 1.0, 0.0) for g in range(groups)]

    even = sub % 2 == 0

    def eliminate(e0, e1, c, rows):
        v = jnp.zeros((8, B), jnp.float32)
        straight = crossed = jnp.zeros((8, B), jnp.float32)
        for j in range(0, 8, 2):
            top = {k: row_of(c[k], j) for k in range(j, 8)}
            low = {k: row_of(c[k], j + 1) for k in range(j + 1, 8)}
            p, q, r = top[j], top[j + 1], low[j + 1]
            inv = 1.0 / (p * r - q * q)
            pair = (sub == j) | (sub == j + 1)

            def multipliers(x, y):
                return (r * x - q * y) * inv, (p * y - q * x) * inv

            def sides(x):
                return row_of(x, j), row_of(x, j + 1)

            x, y = jnp.where(pair, 0.0, c[j]), jnp.where(pair, 0.0, c[j + 1])
            for k in range(j + 2, min(j + 4, 8)):
                both = x * (r * top[k] - q * low[k]) + y * (p * low[k] - q * top[k])
                c[k] = c[k] - both * inv
            m, n = multipliers(x, y)
            for k in range(j + 4, 8):
                c[k] = c[k] - m * top[k] - n * low[k]
            (b0, d0), (b1, d1) = sides(e0), sides(e1)
            e0 = e0 - m * b0 - n * d0
            e1 = e1 - m * b1 - n * d1
            over = q * (1.0 / p)
            v = jnp.where(sub == j, b1 * lax.rsqrt(p), v)
            v = jnp.where(sub == j + 1, (d1 - over * b1) * lax.rsqrt(r - over * q), v)
            straight = jnp.where(pair, jnp.where(even, r, p) * inv, straight)
            crossed = jnp.where(pair, q * inv, crossed)
            if rows is not None:
                f0, f1, d = rows
                m, n = multipliers(d[j], d[j + 1])
                f0 = f0 - m * b0 - n * d0
                f1 = f1 - m * b1 - n * d1
                for k in range(j + 2, 8):
                    d[k] = d[k] - m * top[k] - n * low[k]
                for k in range(8):
                    d[8 + k] = d[8 + k] - m * row_of(d[j], k) - n * row_of(d[j + 1], k)
                rows = f0, f1, d

        def scaled(e):
            other = jnp.where(even, pltpu.roll(e, 7, 0), pltpu.roll(e, 1, 0))
            return e * straight - other * crossed

        return v, scaled(e0), scaled(e1), rows

    def spread(x, first, count):
        return [col_of(x, first + j) * one for j in range(count)]

    def update(h, base, w0, w1):
        cols = [col_of(s[h], base + r) for r in range(8)]
        for r in range(8):
            s[h] = s[h] - cols[r] * w0[r]
            t[h] = t[h] - cols[r] * w1[r]

    for g in range(0, groups, 2):
        base = 8 * g
        near = range(g + 2, min(g + 4, groups))
        far = range(g + 4, groups)
        c = spread(s[g], base, 8)
        d = spread(s[g + 1], base, 16)
        v, p0, p1, (f0, f1, d) = eliminate(s[g], t[g], c, (s[g + 1], t[g + 1], d))
        out_ref[base : base + 8, :] = v
        if near:
            w0 = [row_of(p0, r) for r in range(8)]
            w1 = [row_of(p1, r) for r in range(8)]
        if far:
            below = jnp.concatenate([s[h] for h in far], axis=0)
            below = jnp.where(iota(below.shape, 1) >= base, below, 0.0)
            below = jnp.where(iota(below.shape, 1) < base + 16, below, 0.0)
        for h in near:
            update(h, base, w0, w1)
        between[g]()
        v, q0, q1, _ = eliminate(f0, f1, d[8:], None)
        out_ref[base + 8 : base + 16, :] = v
        if near:
            w0 = [row_of(q0, r) for r in range(8)]
            w1 = [row_of(q1, r) for r in range(8)]
            for h in near:
                update(h, base + 8, w0, w1)
        if far:
            fix = [col_of(p0, base + 8 + r) for r in range(8)]
            for r in range(8):
                p0 = p0 - fix[r] * w0[r]
                p1 = p1 - fix[r] * w1[r]
            parts = [jnp.concatenate([p0, p1], axis=1), jnp.concatenate([q0, q1], axis=1)]
            zero = jnp.zeros((8, 2 * B), jnp.float32)
            w = jnp.concatenate([parts[i - g] if g <= i < g + 2 else zero for i in range(groups)], axis=0)
            h, m, l = split(w)
            change = lax.dot_general(
                left(below), jnp.concatenate([h, m, l, h, m, h], axis=0), (((1,), (0,)), ((), ())), preferred_element_type=jnp.float32
            )
            for i, n in enumerate(far):
                s[n] = s[n] - change[8 * i : 8 * i + 8, :B]
                t[n] = t[n] - change[8 * i : 8 * i + 8, B:]
        between[g + 1]()


def gather_chunk(chunk, info_ref, refs, flat):
    for n, ref in enumerate(refs):
        flat[rows_of(chunk, info_ref, n // (len(refs) // 2) ^ info_ref[0], n % 2, n // 2 % 2), :] = ref[...]


def make_covariance(chunk, flat, mean, scale):
    mean_t = jnp.concatenate([mean, jnp.zeros((B - 8, B), jnp.float32)], axis=0).T
    eye = jnp.where(iota((B, B), 0) == iota((B, B), 1), RIDGE, 0.0)
    scale = jnp.broadcast_to(scale[0:1, :], (B, B))
    for (i, k), n in PLACE_IN[chunk].items():
        block = flat[n * B : (n + 1) * B, :] * scale
        block = block - jnp.broadcast_to(mean_t[:, i : i + 1], (B, B)) * mean[k : k + 1, :]
        flat[n * B : (n + 1) * B, :] = block + eye if i == k else block


def center_rows(rows_refs, mean, k):
    out = []
    for ref in rows_refs:
        live = ref[:, 0:1] < 1e29
        out.append(jnp.where(live, ref[:, k * B : (k + 1) * B] - SHIFT - mean[k : k + 1, :], 0.0))
    return jnp.concatenate(out, axis=0)


def leaf(block, ones, inv, work):
    slots = [[] for _ in range(16)]
    for i, piece in enumerate(work):
        slots[i * 16 // len(work)].append(piece)

    def run(pieces):
        for piece in pieces:
            piece()

    inverse_factor(lambda g: block[8 * g : 8 * g + 8, :], ones[...], inv, [functools.partial(run, p) for p in slots])


def column0_kernel(core_ref, *refs):
    parts_refs, rows_refs, (flat, stat_ref, inv, x_ref), (ones,) = refs[:4], refs[4:8], refs[8:12], refs[12:]
    gather_chunk(0, core_ref, parts_refs, flat)
    scale = 1.0 / flat[STAT + 8 : STAT + 16, :]
    mean = flat[STAT : STAT + 8, :] * scale
    stat_ref[0:8, :] = mean
    stat_ref[8:16, :] = scale
    make_covariance(0, flat, mean, scale)
    ones[...] = jnp.ones((8, B), jnp.float32)

    def center(k):
        x_ref[k] = center_rows(rows_refs, stat_ref[...], k)

    leaf(flat[0:B], ones, inv, [functools.partial(center, k) for k in range(8)])


def column1_kernel(flat, inv0, x, rows_l_ref, rows_r_ref, x_ref, z_ref, ones, inv, inv_r, diagonal, first_r, col0, col1, x1, z_l):
    ones[...] = jnp.ones((8, B), jnp.float32)
    inv_r[...] = right(inv0[...])
    below = product(left(flat[B : 2 * B, :]), inv_r[...])
    first_r[...] = right(below)
    diagonal[...] = flat[8 * B : 9 * B, :] - product(left(below), first_r[...])

    def whiten(k):
        z = product(left(x1[...] if k else x[0]), inv_r[...])
        z_ref[k] = z
        z_l[...] = left(z)

    def parts(col, j, k):
        new = col[j * B : (j + 3) * B, :]
        rows_l_ref[j * B : (j + 3) * B, k * 6 * B : (k + 1) * 6 * B] = left(new)
        rows_r_ref[j * B : (j + 3) * B, k * 6 * B : (k + 1) * 6 * B] = right(new)

    def down(j, k):
        change = product(z_l[...], rows_r_ref[j * B : (j + 2) * B, k * 6 * B : (k + 1) * 6 * B])
        for i in range(2):
            old = x_ref[j + i] if k else x[j + i + 2]
            x_ref[j + i] = old - change[:, i * B : (i + 1) * B]

    def solve(j):
        col0[j * B : (j + 3) * B, :] = product(left(flat[(2 + j) * B : (5 + j) * B, :]), inv_r[...])

    def apply(j):
        change = product(rows_l_ref[j * B : (j + 3) * B, : 6 * B], first_r[...])
        col1[j * B : (j + 3) * B, :] = flat[(9 + j) * B : (12 + j) * B, :] - change

    def down1():
        x1[...] = x[1] - product(z_l[...], first_r[...])

    work = [functools.partial(solve, j) for j in (0, 3)]
    work += [functools.partial(parts, col0, j, 0) for j in (0, 3)]
    work += [functools.partial(apply, j) for j in (0, 3)]
    work += [functools.partial(whiten, 0), down1]
    work += [functools.partial(down, j, 0) for j in (0, 2, 4)]
    leaf(diagonal[...], ones, inv, work)
    inv_r[...] = right(inv[...])
    whiten(1)
    for j in (0, 3):
        col0[j * B : (j + 3) * B, :] = product(left(col1[j * B : (j + 3) * B, :]), inv_r[...])
        parts(col0, j, 1)
    for j in (0, 2, 4):
        down(j, 1)


def second_kernel(core_ref, *refs):
    parts_refs, (stat_ref, first_l, first_rr, x_ref, z_ref), out_refs = refs[:8], refs[8:13], refs[13:17]
    flat, ones, inv, inv_r, diagonal, panel, x, z_l, rows_l, rows_r, white = refs[17:]
    at = PLACE_IN[1]
    gather_chunk(1, core_ref, parts_refs, flat)
    make_covariance(1, flat, stat_ref[0:8, :], stat_ref[8:16, :])
    ones[...] = jnp.ones((8, B), jnp.float32)
    diagonal[...] = flat[0:B, :] - product(first_l[0:B, :], first_rr[0:B, :])

    def start_of(k):
        row = jnp.int32(0)
        for j in range(3, 8):
            row = jnp.where(k == j, at[j, j] * B, row)
        return pl.multiple_of(row, B)

    def update(left_ref, right_ref, skip, j, lo, hi):
        top = min(j + 2, 8)
        change = product(left_ref[(lo - skip) * B : (hi - skip) * B, :], right_ref[(j - skip) * B : (top - skip) * B, :])
        for c in range(j, top):
            first = max(lo, c)
            n, size = at[first, c] * B, (hi - first) * B
            flat[n : n + size, :] = flat[n : n + size, :] - change[(first - lo) * B :, (c - j) * B : (c - j + 1) * B]

    def spans(lo, hi):
        return [(i, min(i + 3, hi)) for i in range(lo, hi, 3)]

    def updates(left_ref, right_ref, skip, low):
        return [
            functools.partial(update, left_ref, right_ref, skip, j, *span) for j in range(low, 8, 2) for span in spans(j, 8)
        ]

    def advance(k):
        inv_r[...] = right(inv[...])
        below = product(left(flat[pl.ds(start_of(k) + B, B), :]), inv_r[...])
        panel[pl.ds(pl.multiple_of((k + 1) * B, B), B), :] = below
        diagonal[...] = flat[pl.ds(start_of(jnp.minimum(k + 1, 7)), B), :] - product(left(below), right(below))

    def take(j):
        x[j] = x_ref[j - 2]

    leaf(diagonal[...], ones, inv, updates(first_l, first_rr, 2, 2) + [functools.partial(take, j) for j in range(2, 8)])
    advance(2)

    def step(low, k):
        def solve(lo, hi):
            size = (hi - lo) * B
            column = flat[pl.ds(start_of(k - 1) + (2 + lo) * B, size), :]
            panel[pl.ds(pl.multiple_of((k + 1 + lo) * B, B), size), :] = product(left(column), inv_r[...])

        def whiten():
            z = product(left(x[k - 1]), inv_r[...])
            white[k - 1] = z
            z_l[...] = left(z)

        def parts(lo, hi):
            new = panel[lo * B : hi * B, :]
            rows_l[lo * B : hi * B, :] = left(new)
            rows_r[lo * B : hi * B, :] = right(new)

        def down(j):
            hi = min(j + 2, 8)
            change = product(z_l[...], rows_r[j * B : hi * B, :])
            for i in range(j, hi):
                x[i] = x[i] - change[:, (i - j) * B : (i - j + 1) * B]

        work = [functools.partial(solve, *span) for span in spans(0, 7 - low)]
        work += [whiten]
        work += [functools.partial(parts, *span) for span in spans(low, 8)]
        work += updates(rows_l, rows_r, 0, low)
        work += [functools.partial(down, j) for j in range(low, 8, 2)]
        leaf(diagonal[...], ones, inv, work)
        advance(k)

    for low, end in ((3, 5), (5, 8)):
        pl.loop(low, end)(functools.partial(step, low))
    white[7] = product(left(x[7]), inv_r[...])
    for k in range(8):
        for g in range(4):
            out_refs[g][:, k * B : (k + 1) * B] = (z_ref if k < 2 else white)[k, g * 64 : (g + 1) * 64, :]


def unpack_kernel(sel_ref, *refs):
    own_refs, other_refs, out_ref = refs[:4], refs[4:8], refs[8]
    sel = sel_ref[...]
    lane = iota((B, 256), 1).astype(jnp.float32)
    place = jnp.where(jnp.concatenate([sel, sel], axis=1) == lane, 1.0, 0.0)
    out_ref[...] = pick(place, jnp.concatenate([r[:32, :] for r in own_refs] + [r[32:, :] for r in other_refs], axis=0))


VMEM = pl.BlockSpec(memory_space=pltpu.VMEM)
SMEM = pl.BlockSpec(memory_space=pltpu.SMEM)


def f32(*shape):
    return jax.ShapeDtypeStruct(shape, jnp.float32)


def call(kernel, outs, args, scratch=(), mib=24, scalars=1, flops=1000000):
    return pl.pallas_call(
        kernel,
        out_shape=outs,
        in_specs=[SMEM] * scalars + [VMEM] * (len(args) - scalars),
        out_specs=jax.tree.map(lambda _: VMEM, outs),
        scratch_shapes=scratch,
        cost_estimate=pl.CostEstimate(flops=flops, bytes_accessed=4000000, transcendentals=0),
        compiler_params=pltpu.CompilerParams(vmem_limit_bytes=mib << 20),
    )(*args)


def whiten(embeddings, domain_ids, order):
    d, w = lax.axis_index("dom"), lax.axis_index("wide")
    core = (d % 2).reshape(1).astype(jnp.int32)
    home = ((w // 8) * 4 + (w % 4) // 2 * 2 + d // 4).reshape(1).astype(jnp.int32)

    def swap(x):
        return permute(x, lambda n: partner(n, 3))

    def exchange(arrays):
        return [permute(x, lambda n, turn=turn: toward(n, turn)) for turn, x in enumerate(arrays)]

    ids = domain_ids.reshape(1, B)
    where = jnp.concatenate([core, home])
    info = jnp.concatenate([core, jnp.stack([w // 4 % 2, w % 2, d // 2 % 2]).astype(jnp.int32)])
    their_rows = swap(embeddings)
    own, sel = call(
        pack_kernel,
        [f32(B, 1024), f32(B, B)],
        (where, jnp.concatenate([ids, order]), embeddings),
        mib=12,
        flops=1000000000,
    )
    rows = exchange(call(merge_kernel, [f32(64, 1024)] * 4, (where, swap(ids), their_rows, own), mib=12))

    def scratch(*shapes, dtype=jnp.float32):
        return [pltpu.VMEM(shape, dtype) for shape in shapes]

    def wide(*shapes):
        return scratch(*shapes, dtype=jnp.bfloat16)

    def gram(chunk):
        half = HALVES[chunk]
        return call(
            functools.partial(gram_kernel, chunk),
            [f32(half, B)] * 2,
            (info, *rows),
            scratch((256, 1024)) + wide((1024, 1536)) + scratch((2 * half, B)),
        )

    def across(x, turn, i):
        return permute(x, lambda n: partner(n, (turn + (2 if i else coords(n)[3])) % 3))

    grams = []
    for chunk in range(2):
        grams.append(gram(chunk))

    def doubled(mine, sent, turn, i):
        theirs = across(sent, turn, i)
        return mine + theirs

    sums, sent = [], []
    for chunk, (mine, other) in enumerate(grams):
        other = swap(other)
        spans = list(zip(CUTS[chunk], CUTS[chunk][1:]))
        kept = [(lo, (lo + hi) // 2 if chunk else hi) for lo, hi in spans]
        sums.append([mine[lo:hi] + other[lo:hi] for lo, hi in kept])
        sent.append([mine[lo:hi] + other[lo:hi] for (_, lo), (_, hi) in zip(kept, spans)] if chunk else sums[0])
    for turn in range(3):
        sums = [[doubled(sums[chunk][i], sent[chunk][i], turn, i) for i in range(2)] for chunk in range(2)]
        sent = sums
    sums[1] = sums[1] + [across(x, 0, i) for i, x in enumerate(sums[1])]
    for parts in sums:
        for x in parts[:]:
            parts.append(swap(x))
    tile, tall = (B, B), (6 * B, B)

    def bf16(*shape):
        return jax.ShapeDtypeStruct(shape, jnp.bfloat16)

    flat, stat, inv, x = call(
        column0_kernel,
        [f32(STAT + 16, B), f32(16, B), f32(*tile), f32(8, 256, B)],
        (info, *sums[0], *rows),
        scratch((8, B)),
        flops=3000000000,
    )
    state = call(
        column1_kernel,
        [bf16(6 * B, 12 * B), bf16(6 * B, 12 * B), f32(6, 256, B), f32(2, 256, B)],
        (flat, inv, x),
        scratch((8, B), tile)
        + wide((B, 6 * B))
        + scratch(tile)
        + wide((B, 6 * B))
        + scratch(tall, tall, (256, B))
        + wide((256, 6 * B)),
        scalars=0,
        flops=3000000000,
    )
    white = call(
        second_kernel,
        [f32(64, 1024)] * 4,
        (info, *sums[1], stat, *state),
        scratch((2 * HALVES[1] + 8 * B, B), (8, B), tile)
        + wide((B, 6 * B))
        + scratch(tile, (14 * B, B), (8, 256, B))
        + wide((256, 6 * B), (8 * B, 6 * B), (8 * B, 6 * B))
        + scratch((8, 256, B)),
        flops=20000000000,
    )
    white = exchange(white)
    return call(unpack_kernel, f32(B, 1024), (sel, *white, *[swap(x) for x in white]), mib=12, scalars=0)


def solution(mesh):
    placed = (P(AXES, None), P(AXES, None), P(AXES, None))
    return jax.shard_map(whiten, mesh=mesh, in_specs=placed, out_specs=P(AXES, None), check_vma=False)
```

```python
import functools

import jax
import jax.numpy as jnp
from jax import lax
from jax.experimental import pallas as pl
from jax.experimental.pallas import tpu as pltpu
from jax.sharding import PartitionSpec as P


RIDGE = 0.1
SHIFT = 1.0
EMPTY = 1e30
B = 128
AXES = ("dom", "wide")


def coords(n):
    d, w = divmod(n, 16)
    return [w // 4, w % 4, d // 2, d % 2]


def number(c):
    x, y, z, core = c
    return (z * 2 + core) * 16 + x * 4 + y


CARRIED = ((7, 0, 4, 2), (3, 5, 6, 1))


def toward(n, turn):
    c = coords(n)
    mask = CARRIED[c[3]][turn]
    for axis, bit in ((0, 4), (1, 2), (2, 1)):
        if mask & bit:
            c[axis] = 3 - c[axis]
    return number(c)


def partner(n, axis):
    c = coords(n)
    c[axis] ^= 1
    return number(c)


def permute(x, to):
    return lax.ppermute(x, AXES, [(n, to(n)) for n in range(128)])


def core_of(place_ref):
    return place_ref[0] & 1


def bit_of(place_ref, axis):
    return (place_ref[0] >> (1 + axis)) & 1


def home_of(place_ref):
    return place_ref[0] >> 4


def iota(shape, axis):
    return lax.broadcasted_iota(jnp.int32, shape, axis)


def split(x):
    high = x.astype(jnp.bfloat16)
    rest = x - high.astype(jnp.float32)
    middle = rest.astype(jnp.bfloat16)
    low = (rest - middle.astype(jnp.float32)).astype(jnp.bfloat16)
    return high, middle, low


def left(x):
    h, m, l = split(x)
    return jnp.concatenate([l, m, h, m, h, h], axis=1)


def right(x):
    h, m, l = split(x)
    return jnp.concatenate([h, m, l, h, m, h], axis=1)


def product(a, b):
    return lax.dot_general(a, b, (((1,), (1,)), ((), ())), preferred_element_type=jnp.float32)


def plain(a, b):
    return lax.dot_general(a, b, (((1,), (0,)), ((), ())), preferred_element_type=jnp.float32)


def pick(place, x):
    h, m, l = split(x)
    p = place.astype(jnp.bfloat16)
    return plain(jnp.concatenate([p, p, p], axis=1), jnp.concatenate([l, m, h], axis=0))


def group_and_rank(where_ref, ids):
    rows = ids.shape[1]
    turned = ids ^ home_of(where_ref)
    group = jnp.zeros_like(turned)
    for place, mask in enumerate(CARRIED[0] + CARRIED[1]):
        group = jnp.where(turned == mask, place, group)
    group = jnp.broadcast_to((group ^ (4 * core_of(where_ref))).astype(jnp.float32), (8, rows))
    onehot = jnp.where(group == iota((8, rows), 0).astype(jnp.float32), 1.0, 0.0)
    earlier = jnp.where(iota((rows, rows), 0) < iota((rows, rows), 1), 1.0, 0.0).astype(jnp.bfloat16)
    counted = plain(onehot.astype(jnp.bfloat16), earlier)
    return group[0:1, :], jnp.sum(counted * onehot, axis=0, keepdims=True)


def packed(slot, x):
    place = jnp.where(slot == iota((B, slot.shape[1]), 0).astype(jnp.float32), 1.0, 0.0)
    return jnp.where(jnp.sum(place, axis=1, keepdims=True) > 0.5, pick(place, x), EMPTY)


def pack_kernel(where_ref, small_ref, x_ref, out_ref, sel_ref):
    rows = x_ref.shape[0]
    group, rank = group_and_rank(where_ref, small_ref[0:1, :])
    slot = group * 32.0 + rank
    out_ref[...] = packed(slot, x_ref[...])
    home_slot = jnp.broadcast_to(slot, (rows, rows))
    want = jnp.broadcast_to(small_ref[1:2, :].astype(jnp.float32), (rows, rows)).T
    picked = jnp.where(want == iota((rows, rows), 1).astype(jnp.float32), home_slot, 0.0)
    sel_ref[...] = jnp.broadcast_to(jnp.sum(picked, axis=1, keepdims=True), (rows, rows))


def merge_kernel(where_ref, ids_ref, x_ref, own_ref, *out_refs):
    group, rank = group_and_rank(where_ref, ids_ref[...])
    theirs = packed(group * 32.0 + rank, x_ref[...])
    for g, ref in enumerate(out_refs):
        ref[:32, :] = own_ref[g * 32 : (g + 1) * 32, :]
        ref[32:, :] = theirs[g * 32 : (g + 1) * 32]


CHUNKS = ((0, 2), (2, 8))
PLACE_IN = [{p: n for n, p in enumerate((i, k) for k in range(*cols) for i in range(k, 8))} for cols in CHUNKS]
STAT = len(PLACE_IN[0]) * B
HALVES = ((STAT + 16) // 2, len(PLACE_IN[1]) * B // 2)
CUTS = ((0, 648, 968), (0, 896, 1344))


def rows_of(chunk, info_ref, which, part, place):
    start, end = CUTS[chunk][part], CUTS[chunk][part + 1]
    first, size = which * HALVES[chunk] + start, end - start
    if chunk == 1:
        size //= 2
        bit = bit_of(info_ref, which if part == 0 else 2)
        first += (place ^ bit) * size
    return pl.ds(pl.multiple_of(first, 8), size)


def gram_kernel(chunk, core_ref, *refs):
    rows_refs, (mine_ref, other_ref), (xs, xl, flat) = refs[:4], refs[4:6], refs[6:]
    for g in range(4):
        x = rows_refs[g][...]
        live = x[:, 0:1] < 1e29
        xs[g * 64 : (g + 1) * 64, :] = jnp.where(live, x - SHIFT, 0.0)
    first, end = CHUNKS[chunk]
    if chunk == 0:
        total = jnp.sum(xs[...], axis=0, keepdims=True)
        flat[STAT : STAT + 8, :] = jnp.concatenate([total[:, j * B : (j + 1) * B] for j in range(8)], axis=0)
        live = [jnp.where(ref[:, 0:B] < 1e29, 1.0, 0.0) for ref in rows_refs]
        count = jnp.sum(jnp.concatenate(live, axis=0), axis=0, keepdims=True)
        flat[STAT + 8 : STAT + 16, :] = jnp.broadcast_to(count, (8, B))
    xl[first * B :, :] = left(xs[:, first * B :].T)
    for k in range(first, end, 2):
        h, m, l = split(xs[:, k * B : (k + 2) * B])
        two = plain(xl[k * B :, :], jnp.concatenate([h, m, l, h, m, h], axis=0))
        for c in range(2):
            n = PLACE_IN[chunk][k + c, k + c] * B
            flat[n : n + (8 - k - c) * B, :] = two[c * B :, c * B : (c + 1) * B]
    for ref, which in ((mine_ref, core_of(core_ref)), (other_ref, 1 - core_of(core_ref))):
        row = 0
        for part in range(2):
            for place in range(1 + chunk):
                rows = rows_of(chunk, core_ref, which, part, place)
                ref[row : row + rows.size, :] = flat[rows, :]
                row += rows.size


def row_of(x, j):
    return jnp.broadcast_to(x[j : j + 1, :], x.shape)


def col_of(x, j):
    return jnp.broadcast_to(x[:, j : j + 1], x.shape)


def inverse_factor(block, one, out_ref, between):
    sub = iota((8, B), 0)
    lane = iota((8, B), 1)
    groups = B // 8
    s = [block(g) for g in range(groups)]
    t = [jnp.where(lane == sub + 8 * g, 1.0, 0.0) for g in range(groups)]

    even = sub % 2 == 0

    def eliminate(e0, e1, c, rows):
        v = jnp.zeros((8, B), jnp.float32)
        straight = crossed = jnp.zeros((8, B), jnp.float32)
        for j in range(0, 8, 2):
            top = {k: row_of(c[k], j) for k in range(j, 8)}
            low = {k: row_of(c[k], j + 1) for k in range(j + 1, 8)}
            p, q, r = top[j], top[j + 1], low[j + 1]
            inv = 1.0 / (p * r - q * q)
            pair = (sub == j) | (sub == j + 1)

            def multipliers(x, y):
                return (r * x - q * y) * inv, (p * y - q * x) * inv

            def sides(x):
                return row_of(x, j), row_of(x, j + 1)

            x, y = jnp.where(pair, 0.0, c[j]), jnp.where(pair, 0.0, c[j + 1])
            for k in range(j + 2, min(j + 4, 8)):
                both = x * (r * top[k] - q * low[k]) + y * (p * low[k] - q * top[k])
                c[k] = c[k] - both * inv
            m, n = multipliers(x, y)
            for k in range(j + 4, 8):
                c[k] = c[k] - m * top[k] - n * low[k]
            (b0, d0), (b1, d1) = sides(e0), sides(e1)
            e0 = e0 - m * b0 - n * d0
            e1 = e1 - m * b1 - n * d1
            over = q * (1.0 / p)
            v = jnp.where(sub == j, b1 * lax.rsqrt(p), v)
            v = jnp.where(sub == j + 1, (d1 - over * b1) * lax.rsqrt(r - over * q), v)
            straight = jnp.where(pair, jnp.where(even, r, p) * inv, straight)
            crossed = jnp.where(pair, q * inv, crossed)
            if rows is not None:
                f0, f1, d = rows
                m, n = multipliers(d[j], d[j + 1])
                f0 = f0 - m * b0 - n * d0
                f1 = f1 - m * b1 - n * d1
                for k in range(j + 2, 8):
                    d[k] = d[k] - m * top[k] - n * low[k]
                for k in range(8):
                    d[8 + k] = d[8 + k] - m * row_of(d[j], k) - n * row_of(d[j + 1], k)
                rows = f0, f1, d

        def scaled(e):
            other = jnp.where(even, pltpu.roll(e, 7, 0), pltpu.roll(e, 1, 0))
            return e * straight - other * crossed

        return v, scaled(e0), scaled(e1), rows

    def spread(x, first, count):
        return [col_of(x, first + j) * one for j in range(count)]

    def update(h, base, w0, w1):
        cols = [col_of(s[h], base + r) for r in range(8)]
        for r in range(8):
            s[h] = s[h] - cols[r] * w0[r]
            t[h] = t[h] - cols[r] * w1[r]

    for g in range(0, groups, 2):
        base = 8 * g
        near = range(g + 2, min(g + 4, groups))
        far = range(g + 4, groups)
        c = spread(s[g], base, 8)
        d = spread(s[g + 1], base, 16)
        v, p0, p1, (f0, f1, d) = eliminate(s[g], t[g], c, (s[g + 1], t[g + 1], d))
        out_ref[base : base + 8, :] = v
        if near:
            w0 = [row_of(p0, r) for r in range(8)]
            w1 = [row_of(p1, r) for r in range(8)]
        if far:
            below = jnp.concatenate([s[h] for h in far], axis=0)
            below = jnp.where(iota(below.shape, 1) >= base, below, 0.0)
            below = jnp.where(iota(below.shape, 1) < base + 16, below, 0.0)
        for h in near:
            update(h, base, w0, w1)
        between[g]()
        v, q0, q1, _ = eliminate(f0, f1, d[8:], None)
        out_ref[base + 8 : base + 16, :] = v
        if near:
            w0 = [row_of(q0, r) for r in range(8)]
            w1 = [row_of(q1, r) for r in range(8)]
            for h in near:
                update(h, base + 8, w0, w1)
        if far:
            fix = [col_of(p0, base + 8 + r) for r in range(8)]
            for r in range(8):
                p0 = p0 - fix[r] * w0[r]
                p1 = p1 - fix[r] * w1[r]
            parts = [jnp.concatenate([p0, p1], axis=1), jnp.concatenate([q0, q1], axis=1)]
            zero = jnp.zeros((8, 2 * B), jnp.float32)
            w = jnp.concatenate([parts[i - g] if g <= i < g + 2 else zero for i in range(groups)], axis=0)
            h, m, l = split(w)
            change = lax.dot_general(
                left(below), jnp.concatenate([h, m, l, h, m, h], axis=0), (((1,), (0,)), ((), ())), preferred_element_type=jnp.float32
            )
            for i, n in enumerate(far):
                s[n] = s[n] - change[8 * i : 8 * i + 8, :B]
                t[n] = t[n] - change[8 * i : 8 * i + 8, B:]
        between[g + 1]()


def gather_chunk(chunk, info_ref, refs, flat):
    for n, ref in enumerate(refs):
        flat[rows_of(chunk, info_ref, n // (len(refs) // 2) ^ core_of(info_ref), n % 2, n // 2 % 2), :] = ref[...]


def make_covariance(chunk, flat, mean, scale):
    mean_t = jnp.concatenate([mean, jnp.zeros((B - 8, B), jnp.float32)], axis=0).T
    eye = jnp.where(iota((B, B), 0) == iota((B, B), 1), RIDGE, 0.0)
    scale = jnp.broadcast_to(scale[0:1, :], (B, B))
    for (i, k), n in PLACE_IN[chunk].items():
        block = flat[n * B : (n + 1) * B, :] * scale
        block = block - jnp.broadcast_to(mean_t[:, i : i + 1], (B, B)) * mean[k : k + 1, :]
        flat[n * B : (n + 1) * B, :] = block + eye if i == k else block


def center_rows(rows_refs, mean, k):
    out = []
    for ref in rows_refs:
        live = ref[:, 0:1] < 1e29
        out.append(jnp.where(live, ref[:, k * B : (k + 1) * B] - SHIFT - mean[k : k + 1, :], 0.0))
    return jnp.concatenate(out, axis=0)


def leaf(block, ones, inv, work):
    slots = [[] for _ in range(16)]
    for i, piece in enumerate(work):
        slots[i * 16 // len(work)].append(piece)

    def run(pieces):
        for piece in pieces:
            piece()

    inverse_factor(lambda g: block[8 * g : 8 * g + 8, :], ones[...], inv, [functools.partial(run, p) for p in slots])


def column0_kernel(core_ref, *refs):
    parts_refs, rows_refs, (flat, stat_ref, inv, x_ref), (ones,) = refs[:4], refs[4:8], refs[8:12], refs[12:]
    gather_chunk(0, core_ref, parts_refs, flat)
    scale = 1.0 / flat[STAT + 8 : STAT + 16, :]
    mean = flat[STAT : STAT + 8, :] * scale
    stat_ref[0:8, :] = mean
    stat_ref[8:16, :] = scale
    make_covariance(0, flat, mean, scale)
    ones[...] = jnp.ones((8, B), jnp.float32)

    def center(k):
        x_ref[k] = center_rows(rows_refs, stat_ref[...], k)

    leaf(flat[0:B], ones, inv, [functools.partial(center, k) for k in range(8)])


def column1_kernel(flat, inv0, x, rows_l_ref, rows_r_ref, x_ref, z_ref, ones, inv, inv_r, diagonal, first_r, col0, col1, x1, z_l):
    ones[...] = jnp.ones((8, B), jnp.float32)
    inv_r[...] = right(inv0[...])
    below = product(left(flat[B : 2 * B, :]), inv_r[...])
    first_r[...] = right(below)
    diagonal[...] = flat[8 * B : 9 * B, :] - product(left(below), first_r[...])

    def whiten(k):
        z = product(left(x1[...] if k else x[0]), inv_r[...])
        z_ref[k] = z
        z_l[...] = left(z)

    def parts(col, j, k):
        new = col[j * B : (j + 3) * B, :]
        rows_l_ref[j * B : (j + 3) * B, k * 6 * B : (k + 1) * 6 * B] = left(new)
        rows_r_ref[j * B : (j + 3) * B, k * 6 * B : (k + 1) * 6 * B] = right(new)

    def down(j, k):
        change = product(z_l[...], rows_r_ref[j * B : (j + 2) * B, k * 6 * B : (k + 1) * 6 * B])
        for i in range(2):
            old = x_ref[j + i] if k else x[j + i + 2]
            x_ref[j + i] = old - change[:, i * B : (i + 1) * B]

    def solve(j):
        col0[j * B : (j + 3) * B, :] = product(left(flat[(2 + j) * B : (5 + j) * B, :]), inv_r[...])

    def apply(j):
        change = product(rows_l_ref[j * B : (j + 3) * B, : 6 * B], first_r[...])
        col1[j * B : (j + 3) * B, :] = flat[(9 + j) * B : (12 + j) * B, :] - change

    def down1():
        x1[...] = x[1] - product(z_l[...], first_r[...])

    work = [functools.partial(solve, j) for j in (0, 3)]
    work += [functools.partial(parts, col0, j, 0) for j in (0, 3)]
    work += [functools.partial(apply, j) for j in (0, 3)]
    work += [functools.partial(whiten, 0), down1]
    work += [functools.partial(down, j, 0) for j in (0, 2, 4)]
    leaf(diagonal[...], ones, inv, work)
    inv_r[...] = right(inv[...])
    whiten(1)
    for j in (0, 3):
        col0[j * B : (j + 3) * B, :] = product(left(col1[j * B : (j + 3) * B, :]), inv_r[...])
        parts(col0, j, 1)
    for j in (0, 2, 4):
        down(j, 1)


def second_kernel(core_ref, *refs):
    parts_refs, (stat_ref, first_l, first_rr, x_ref, z_ref), out_refs = refs[:8], refs[8:13], refs[13:17]
    flat, ones, inv, inv_r, diagonal, panel, x, z_l, rows_l, rows_r, white = refs[17:]
    at = PLACE_IN[1]
    gather_chunk(1, core_ref, parts_refs, flat)
    make_covariance(1, flat, stat_ref[0:8, :], stat_ref[8:16, :])
    ones[...] = jnp.ones((8, B), jnp.float32)
    diagonal[...] = flat[0:B, :] - product(first_l[0:B, :], first_rr[0:B, :])

    def start_of(k):
        row = jnp.int32(0)
        for j in range(3, 8):
            row = jnp.where(k == j, at[j, j] * B, row)
        return pl.multiple_of(row, B)

    def update(left_ref, right_ref, skip, j, lo, hi):
        top = min(j + 2, 8)
        change = product(left_ref[(lo - skip) * B : (hi - skip) * B, :], right_ref[(j - skip) * B : (top - skip) * B, :])
        for c in range(j, top):
            first = max(lo, c)
            n, size = at[first, c] * B, (hi - first) * B
            flat[n : n + size, :] = flat[n : n + size, :] - change[(first - lo) * B :, (c - j) * B : (c - j + 1) * B]

    def spans(lo, hi):
        return [(i, min(i + 3, hi)) for i in range(lo, hi, 3)]

    def updates(left_ref, right_ref, skip, low):
        return [
            functools.partial(update, left_ref, right_ref, skip, j, *span) for j in range(low, 8, 2) for span in spans(j, 8)
        ]

    def advance(k):
        inv_r[...] = right(inv[...])
        below = product(left(flat[pl.ds(start_of(k) + B, B), :]), inv_r[...])
        panel[pl.ds(pl.multiple_of((k + 1) * B, B), B), :] = below
        diagonal[...] = flat[pl.ds(start_of(jnp.minimum(k + 1, 7)), B), :] - product(left(below), right(below))

    def take(j):
        x[j] = x_ref[j - 2]

    leaf(diagonal[...], ones, inv, updates(first_l, first_rr, 2, 2) + [functools.partial(take, j) for j in range(2, 8)])
    advance(2)

    def step(low, k):
        def solve(lo, hi):
            size = (hi - lo) * B
            column = flat[pl.ds(start_of(k - 1) + (2 + lo) * B, size), :]
            panel[pl.ds(pl.multiple_of((k + 1 + lo) * B, B), size), :] = product(left(column), inv_r[...])

        def whiten():
            z = product(left(x[k - 1]), inv_r[...])
            white[k - 1] = z
            z_l[...] = left(z)

        def parts(lo, hi):
            new = panel[lo * B : hi * B, :]
            rows_l[lo * B : hi * B, :] = left(new)
            rows_r[lo * B : hi * B, :] = right(new)

        def down(j):
            hi = min(j + 2, 8)
            change = product(z_l[...], rows_r[j * B : hi * B, :])
            for i in range(j, hi):
                x[i] = x[i] - change[:, (i - j) * B : (i - j + 1) * B]

        work = [functools.partial(solve, *span) for span in spans(0, 7 - low)]
        work += [whiten]
        work += [functools.partial(parts, *span) for span in spans(low, 8)]
        work += updates(rows_l, rows_r, 0, low)
        work += [functools.partial(down, j) for j in range(low, 8, 2)]
        leaf(diagonal[...], ones, inv, work)
        advance(k)

    for low, end in ((3, 5), (5, 8)):
        pl.loop(low, end)(functools.partial(step, low))
    white[7] = product(left(x[7]), inv_r[...])
    for k in range(8):
        for g in range(4):
            out_refs[g][:, k * B : (k + 1) * B] = (z_ref if k < 2 else white)[k, g * 64 : (g + 1) * 64, :]


def unpack_kernel(sel_ref, *refs):
    own_refs, other_refs, out_ref = refs[:4], refs[4:8], refs[8]
    sel = sel_ref[...]
    lane = iota((B, 256), 1).astype(jnp.float32)
    place = jnp.where(jnp.concatenate([sel, sel], axis=1) == lane, 1.0, 0.0)
    out_ref[...] = pick(place, jnp.concatenate([r[:32, :] for r in own_refs] + [r[32:, :] for r in other_refs], axis=0))


VMEM = pl.BlockSpec(memory_space=pltpu.VMEM)
SMEM = pl.BlockSpec(memory_space=pltpu.SMEM)


def f32(*shape):
    return jax.ShapeDtypeStruct(shape, jnp.float32)


def call(kernel, outs, args, scratch=(), mib=24, scalars=1, flops=1000000):
    return pl.pallas_call(
        kernel,
        out_shape=outs,
        in_specs=[SMEM] * scalars + [VMEM] * (len(args) - scalars),
        out_specs=jax.tree.map(lambda _: VMEM, outs),
        scratch_shapes=scratch,
        cost_estimate=pl.CostEstimate(flops=flops, bytes_accessed=4000000, transcendentals=0),
        compiler_params=pltpu.CompilerParams(vmem_limit_bytes=mib << 20),
    )(*args)


def whiten(embeddings, domain_ids, order):
    d, w = lax.axis_index("dom"), lax.axis_index("wide")
    home = (w // 8) * 4 + (w % 4) // 2 * 2 + d // 4
    info = (d % 2 + w // 4 % 2 * 2 + w % 2 * 4 + d // 2 % 2 * 8 + home * 16).reshape(1).astype(jnp.int32)

    def swap(x):
        return permute(x, lambda n: partner(n, 3))

    def exchange(arrays):
        return [permute(x, lambda n, turn=turn: toward(n, turn)) for turn, x in enumerate(arrays)]

    ids = domain_ids.reshape(1, B)
    their_rows = swap(embeddings)
    own, sel = call(
        pack_kernel,
        [f32(B, 1024), f32(B, B)],
        (info, jnp.concatenate([ids, order]), embeddings),
        mib=12,
        flops=1000000000,
    )
    rows = exchange(call(merge_kernel, [f32(64, 1024)] * 4, (info, swap(ids), their_rows, own), mib=12))

    def scratch(*shapes, dtype=jnp.float32):
        return [pltpu.VMEM(shape, dtype) for shape in shapes]

    def wide(*shapes):
        return scratch(*shapes, dtype=jnp.bfloat16)

    def gram(chunk):
        half = HALVES[chunk]
        return call(
            functools.partial(gram_kernel, chunk),
            [f32(half, B)] * 2,
            (info, *rows),
            scratch((256, 1024)) + wide((1024, 1536)) + scratch((2 * half, B)),
        )

    def across(x, turn, i):
        return permute(x, lambda n: partner(n, (turn + (2 if i else coords(n)[3])) % 3))

    grams = []
    for chunk in range(2):
        grams.append(gram(chunk))

    def doubled(mine, sent, turn, i):
        theirs = across(sent, turn, i)
        return mine + theirs

    sums, sent = [], []
    for chunk, (mine, other) in enumerate(grams):
        other = swap(other)
        spans = list(zip(CUTS[chunk], CUTS[chunk][1:]))
        kept = [(lo, (lo + hi) // 2 if chunk else hi) for lo, hi in spans]
        sums.append([mine[lo:hi] + other[lo:hi] for lo, hi in kept])
        sent.append([mine[lo:hi] + other[lo:hi] for (_, lo), (_, hi) in zip(kept, spans)] if chunk else sums[0])
    for turn in range(3):
        sums = [[doubled(sums[chunk][i], sent[chunk][i], turn, i) for i in range(2)] for chunk in range(2)]
        sent = sums
    sums[1] = sums[1] + [across(x, 0, i) for i, x in enumerate(sums[1])]
    for parts in sums:
        for x in parts[:]:
            parts.append(swap(x))
    tile, tall = (B, B), (6 * B, B)

    def bf16(*shape):
        return jax.ShapeDtypeStruct(shape, jnp.bfloat16)

    flat, stat, inv, x = call(
        column0_kernel,
        [f32(STAT + 16, B), f32(16, B), f32(*tile), f32(8, 256, B)],
        (info, *sums[0], *rows),
        scratch((8, B)),
        flops=3000000000,
    )
    state = call(
        column1_kernel,
        [bf16(6 * B, 12 * B), bf16(6 * B, 12 * B), f32(6, 256, B), f32(2, 256, B)],
        (flat, inv, x),
        scratch((8, B), tile)
        + wide((B, 6 * B))
        + scratch(tile)
        + wide((B, 6 * B))
        + scratch(tall, tall, (256, B))
        + wide((256, 6 * B)),
        scalars=0,
        flops=3000000000,
    )
    white = call(
        second_kernel,
        [f32(64, 1024)] * 4,
        (info, *sums[1], stat, *state),
        scratch((2 * HALVES[1] + 8 * B, B), (8, B), tile)
        + wide((B, 6 * B))
        + scratch(tile, (14 * B, B), (8, 256, B))
        + wide((256, 6 * B), (8 * B, 6 * B), (8 * B, 6 * B))
        + scratch((8, 256, B)),
        flops=20000000000,
    )
    white = exchange(white)
    return call(unpack_kernel, f32(B, 1024), (sel, *white, *[swap(x) for x in white]), mib=12, scalars=0)


def solution(mesh):
    placed = (P(AXES, None), P(AXES, None), P(AXES, None))
    return jax.shard_map(whiten, mesh=mesh, in_specs=placed, out_specs=P(AXES, None), check_vma=False)
```

```python
import functools

import jax
import jax.numpy as jnp
from jax import lax
from jax.experimental import pallas as pl
from jax.experimental.pallas import tpu as pltpu
from jax.sharding import PartitionSpec as P


RIDGE = 0.1
SHIFT = 1.0
EMPTY = 1e30
B = 128
AXES = ("dom", "wide")


def coords(n):
    d, w = divmod(n, 16)
    return [w // 4, w % 4, d // 2, d % 2]


def number(c):
    x, y, z, core = c
    return (z * 2 + core) * 16 + x * 4 + y


CARRIED = ((7, 0, 4, 2), (3, 5, 6, 1))


def toward(n, turn):
    c = coords(n)
    mask = CARRIED[c[3]][turn]
    for axis, bit in ((0, 4), (1, 2), (2, 1)):
        if mask & bit:
            c[axis] = 3 - c[axis]
    return number(c)


def partner(n, axis):
    c = coords(n)
    c[axis] ^= 1
    return number(c)


def permute(x, to):
    return lax.ppermute(x, AXES, [(n, to(n)) for n in range(128)])


def core_of(place_ref):
    return place_ref[0] & 1


def bit_of(place_ref, axis):
    return (place_ref[0] >> (1 + axis)) & 1


def home_of(place_ref):
    return place_ref[0] >> 4


def iota(shape, axis):
    return lax.broadcasted_iota(jnp.int32, shape, axis)


def split(x):
    high = x.astype(jnp.bfloat16)
    rest = x - high.astype(jnp.float32)
    middle = rest.astype(jnp.bfloat16)
    low = (rest - middle.astype(jnp.float32)).astype(jnp.bfloat16)
    return high, middle, low


def left(x):
    h, m, l = split(x)
    return jnp.concatenate([l, m, h, m, h, h], axis=1)


def right(x):
    h, m, l = split(x)
    return jnp.concatenate([h, m, l, h, m, h], axis=1)


def product(a, b):
    return lax.dot_general(a, b, (((1,), (1,)), ((), ())), preferred_element_type=jnp.float32)


def plain(a, b):
    return lax.dot_general(a, b, (((1,), (0,)), ((), ())), preferred_element_type=jnp.float32)


def pick(place, x):
    h, m, l = split(x)
    p = place.astype(jnp.bfloat16)
    return plain(jnp.concatenate([p, p, p], axis=1), jnp.concatenate([l, m, h], axis=0))


def group_and_rank(where_ref, ids):
    rows = ids.shape[1]
    turned = ids ^ home_of(where_ref)
    group = jnp.zeros_like(turned)
    for place, mask in enumerate(CARRIED[0] + CARRIED[1]):
        group = jnp.where(turned == mask, place, group)
    group = jnp.broadcast_to((group ^ (4 * core_of(where_ref))).astype(jnp.float32), (8, rows))
    onehot = jnp.where(group == iota((8, rows), 0).astype(jnp.float32), 1.0, 0.0)
    earlier = jnp.where(iota((rows, rows), 0) < iota((rows, rows), 1), 1.0, 0.0).astype(jnp.bfloat16)
    counted = plain(onehot.astype(jnp.bfloat16), earlier)
    return group[0:1, :], jnp.sum(counted * onehot, axis=0, keepdims=True)


def packed(slot, x):
    place = jnp.where(slot == iota((B, slot.shape[1]), 0).astype(jnp.float32), 1.0, 0.0)
    return jnp.where(jnp.sum(place, axis=1, keepdims=True) > 0.5, pick(place, x), EMPTY)


def pack_kernel(where_ref, small_ref, x_ref, out_ref, sel_ref):
    rows = x_ref.shape[0]
    group, rank = group_and_rank(where_ref, small_ref[0:1, :])
    slot = group * 32.0 + rank
    out_ref[...] = packed(slot, x_ref[...])
    home_slot = jnp.broadcast_to(slot, (rows, rows))
    want = jnp.broadcast_to(small_ref[1:2, :].astype(jnp.float32), (rows, rows)).T
    picked = jnp.where(want == iota((rows, rows), 1).astype(jnp.float32), home_slot, 0.0)
    sel_ref[...] = jnp.broadcast_to(jnp.sum(picked, axis=1, keepdims=True), (rows, rows))


def merge_kernel(where_ref, ids_ref, x_ref, own_ref, *out_refs):
    group, rank = group_and_rank(where_ref, ids_ref[...])
    theirs = packed(group * 32.0 + rank, x_ref[...])
    for g, ref in enumerate(out_refs):
        ref[:32, :] = own_ref[g * 32 : (g + 1) * 32, :]
        ref[32:, :] = theirs[g * 32 : (g + 1) * 32]


CHUNKS = ((0, 2), (2, 8))
PLACE_IN = [{p: n for n, p in enumerate((i, k) for k in range(*cols) for i in range(k, 8))} for cols in CHUNKS]
STAT = len(PLACE_IN[0]) * B
HALVES = ((STAT + 16) // 2, len(PLACE_IN[1]) * B // 2)
CUTS = ((0, 648, 968), (0, 896, 1344))


def rows_of(chunk, info_ref, which, part, place):
    start, end = CUTS[chunk][part], CUTS[chunk][part + 1]
    first, size = which * HALVES[chunk] + start, end - start
    if chunk == 1:
        size //= 2
        bit = bit_of(info_ref, which if part == 0 else 2)
        first += (place ^ bit) * size
    return pl.ds(pl.multiple_of(first, 8), size)


def gram_kernel(chunk, core_ref, *refs):
    rows_refs, (mine_ref, other_ref), (xs, xl, flat) = refs[:4], refs[4:6], refs[6:]
    for g in range(4):
        x = rows_refs[g][...]
        live = x[:, 0:1] < 1e29
        xs[g * 64 : (g + 1) * 64, :] = jnp.where(live, x - SHIFT, 0.0)
    first, end = CHUNKS[chunk]
    if chunk == 0:
        total = jnp.sum(xs[...], axis=0, keepdims=True)
        flat[STAT : STAT + 8, :] = jnp.concatenate([total[:, j * B : (j + 1) * B] for j in range(8)], axis=0)
        live = [jnp.where(ref[:, 0:B] < 1e29, 1.0, 0.0) for ref in rows_refs]
        count = jnp.sum(jnp.concatenate(live, axis=0), axis=0, keepdims=True)
        flat[STAT + 8 : STAT + 16, :] = jnp.broadcast_to(count, (8, B))
    xl[first * B :, :] = left(xs[:, first * B :].T)
    for k in range(first, end, 2):
        h, m, l = split(xs[:, k * B : (k + 2) * B])
        two = plain(xl[k * B :, :], jnp.concatenate([h, m, l, h, m, h], axis=0))
        for c in range(2):
            n = PLACE_IN[chunk][k + c, k + c] * B
            flat[n : n + (8 - k - c) * B, :] = two[c * B :, c * B : (c + 1) * B]
    for ref, which in ((mine_ref, core_of(core_ref)), (other_ref, 1 - core_of(core_ref))):
        row = 0
        for part in range(2):
            for place in range(1 + chunk):
                rows = rows_of(chunk, core_ref, which, part, place)
                ref[row : row + rows.size, :] = flat[rows, :]
                row += rows.size


def row_of(x, j):
    return jnp.broadcast_to(x[j : j + 1, :], x.shape)


def col_of(x, j):
    return jnp.broadcast_to(x[:, j : j + 1], x.shape)


def inverse_factor(block, one, out_ref, between):
    sub = iota((8, B), 0)
    lane = iota((8, B), 1)
    groups = B // 8
    s = [block(g) for g in range(groups)]
    t = [jnp.where(lane == sub + 8 * g, 1.0, 0.0) for g in range(groups)]

    even = sub % 2 == 0

    def eliminate(e0, e1, c, rows):
        v = jnp.zeros((8, B), jnp.float32)
        straight = crossed = jnp.zeros((8, B), jnp.float32)
        for j in range(0, 8, 2):
            top = {k: row_of(c[k], j) for k in range(j, 8)}
            low = {k: row_of(c[k], j + 1) for k in range(j + 1, 8)}
            p, q, r = top[j], top[j + 1], low[j + 1]
            inv = 1.0 / (p * r - q * q)
            pair = (sub == j) | (sub == j + 1)

            def multipliers(x, y):
                return (r * x - q * y) * inv, (p * y - q * x) * inv

            def sides(x):
                return row_of(x, j), row_of(x, j + 1)

            x, y = jnp.where(pair, 0.0, c[j]), jnp.where(pair, 0.0, c[j + 1])
            for k in range(j + 2, min(j + 4, 8)):
                both = x * (r * top[k] - q * low[k]) + y * (p * low[k] - q * top[k])
                c[k] = c[k] - both * inv
            m, n = multipliers(x, y)
            for k in range(j + 4, 8):
                c[k] = c[k] - m * top[k] - n * low[k]
            (b0, d0), (b1, d1) = sides(e0), sides(e1)
            e0 = e0 - m * b0 - n * d0
            e1 = e1 - m * b1 - n * d1
            over = q * (1.0 / p)
            v = jnp.where(sub == j, b1 * lax.rsqrt(p), v)
            v = jnp.where(sub == j + 1, (d1 - over * b1) * lax.rsqrt(r - over * q), v)
            straight = jnp.where(pair, jnp.where(even, r, p) * inv, straight)
            crossed = jnp.where(pair, q * inv, crossed)
            if rows is not None:
                f0, f1, d = rows
                m, n = multipliers(d[j], d[j + 1])
                f0 = f0 - m * b0 - n * d0
                f1 = f1 - m * b1 - n * d1
                for k in range(j + 2, 8):
                    d[k] = d[k] - m * top[k] - n * low[k]
                for k in range(8):
                    d[8 + k] = d[8 + k] - m * row_of(d[j], k) - n * row_of(d[j + 1], k)
                rows = f0, f1, d

        def scaled(e):
            other = jnp.where(even, pltpu.roll(e, 7, 0), pltpu.roll(e, 1, 0))
            return e * straight - other * crossed

        return v, scaled(e0), scaled(e1), rows

    def spread(x, first, count):
        return [col_of(x, first + j) * one for j in range(count)]

    def update(h, base, w0, w1):
        cols = [col_of(s[h], base + r) for r in range(8)]
        for r in range(8):
            s[h] = s[h] - cols[r] * w0[r]
            t[h] = t[h] - cols[r] * w1[r]

    for g in range(0, groups, 2):
        base = 8 * g
        near = range(g + 2, min(g + 4, groups))
        far = range(g + 4, groups)
        c = spread(s[g], base, 8)
        d = spread(s[g + 1], base, 16)
        v, p0, p1, (f0, f1, d) = eliminate(s[g], t[g], c, (s[g + 1], t[g + 1], d))
        out_ref[base : base + 8, :] = v
        if near:
            w0 = [row_of(p0, r) for r in range(8)]
            w1 = [row_of(p1, r) for r in range(8)]
        if far:
            below = jnp.concatenate([s[h] for h in far], axis=0)
            below = jnp.where(iota(below.shape, 1) >= base, below, 0.0)
            below = jnp.where(iota(below.shape, 1) < base + 16, below, 0.0)
        for h in near:
            update(h, base, w0, w1)
        between[g]()
        v, q0, q1, _ = eliminate(f0, f1, d[8:], None)
        out_ref[base + 8 : base + 16, :] = v
        if near:
            w0 = [row_of(q0, r) for r in range(8)]
            w1 = [row_of(q1, r) for r in range(8)]
            for h in near:
                update(h, base + 8, w0, w1)
        if far:
            fix = [col_of(p0, base + 8 + r) for r in range(8)]
            for r in range(8):
                p0 = p0 - fix[r] * w0[r]
                p1 = p1 - fix[r] * w1[r]
            parts = [jnp.concatenate([p0, p1], axis=1), jnp.concatenate([q0, q1], axis=1)]
            zero = jnp.zeros((8, 2 * B), jnp.float32)
            w = jnp.concatenate([parts[i - g] if g <= i < g + 2 else zero for i in range(groups)], axis=0)
            h, m, l = split(w)
            change = lax.dot_general(
                left(below), jnp.concatenate([h, m, l, h, m, h], axis=0), (((1,), (0,)), ((), ())), preferred_element_type=jnp.float32
            )
            for i, n in enumerate(far):
                s[n] = s[n] - change[8 * i : 8 * i + 8, :B]
                t[n] = t[n] - change[8 * i : 8 * i + 8, B:]
        between[g + 1]()


def gather_chunk(chunk, info_ref, refs, flat):
    for n, ref in enumerate(refs):
        flat[rows_of(chunk, info_ref, n // (len(refs) // 2) ^ core_of(info_ref), n % 2, n // 2 % 2), :] = ref[...]


def covariance_steps(chunk, flat, mean, scale):
    mean_t = jnp.concatenate([mean, jnp.zeros((B - 8, B), jnp.float32)], axis=0).T
    eye = jnp.where(iota((B, B), 0) == iota((B, B), 1), RIDGE, 0.0)
    scale = jnp.broadcast_to(scale[0:1, :], (B, B))

    def step(n, i, k):
        block = flat[n * B : (n + 1) * B, :] * scale
        block = block - jnp.broadcast_to(mean_t[:, i : i + 1], (B, B)) * mean[k : k + 1, :]
        flat[n * B : (n + 1) * B, :] = block + eye if i == k else block

    return [functools.partial(step, n, i, k) for (i, k), n in PLACE_IN[chunk].items()]


def center_rows(rows_refs, mean, k):
    out = []
    for ref in rows_refs:
        live = ref[:, 0:1] < 1e29
        out.append(jnp.where(live, ref[:, k * B : (k + 1) * B] - SHIFT - mean[k : k + 1, :], 0.0))
    return jnp.concatenate(out, axis=0)


def leaf(block, ones, inv, work):
    slots = [[] for _ in range(16)]
    for i, piece in enumerate(work):
        slots[i * 16 // len(work)].append(piece)

    def run(pieces):
        for piece in pieces:
            piece()

    inverse_factor(lambda g: block[8 * g : 8 * g + 8, :], ones[...], inv, [functools.partial(run, p) for p in slots])


def column0_kernel(core_ref, *refs):
    parts_refs, rows_refs, (flat, stat_ref, inv, x_ref), (ones,) = refs[:4], refs[4:8], refs[8:12], refs[12:]
    gather_chunk(0, core_ref, parts_refs, flat)
    scale = 1.0 / flat[STAT + 8 : STAT + 16, :]
    mean = flat[STAT : STAT + 8, :] * scale
    stat_ref[0:8, :] = mean
    stat_ref[8:16, :] = scale
    first, *rest = covariance_steps(0, flat, mean, scale)
    first()
    ones[...] = jnp.ones((8, B), jnp.float32)

    def center(k):
        x_ref[k] = center_rows(rows_refs, stat_ref[...], k)

    leaf(flat[0:B], ones, inv, rest + [functools.partial(center, k) for k in range(8)])


def column1_kernel(flat, inv0, x, rows_l_ref, rows_r_ref, x_ref, z_ref, ones, inv, inv_r, diagonal, first_r, col0, col1, x1, z_l):
    ones[...] = jnp.ones((8, B), jnp.float32)
    inv_r[...] = right(inv0[...])
    below = product(left(flat[B : 2 * B, :]), inv_r[...])
    first_r[...] = right(below)
    diagonal[...] = flat[8 * B : 9 * B, :] - product(left(below), first_r[...])

    def whiten(k):
        z = product(left(x1[...] if k else x[0]), inv_r[...])
        z_ref[k] = z
        z_l[...] = left(z)

    def parts(col, j, k):
        new = col[j * B : (j + 3) * B, :]
        rows_l_ref[j * B : (j + 3) * B, k * 6 * B : (k + 1) * 6 * B] = left(new)
        rows_r_ref[j * B : (j + 3) * B, k * 6 * B : (k + 1) * 6 * B] = right(new)

    def down(j, k):
        change = product(z_l[...], rows_r_ref[j * B : (j + 2) * B, k * 6 * B : (k + 1) * 6 * B])
        for i in range(2):
            old = x_ref[j + i] if k else x[j + i + 2]
            x_ref[j + i] = old - change[:, i * B : (i + 1) * B]

    def solve(j):
        col0[j * B : (j + 3) * B, :] = product(left(flat[(2 + j) * B : (5 + j) * B, :]), inv_r[...])

    def apply(j):
        change = product(rows_l_ref[j * B : (j + 3) * B, : 6 * B], first_r[...])
        col1[j * B : (j + 3) * B, :] = flat[(9 + j) * B : (12 + j) * B, :] - change

    def down1():
        x1[...] = x[1] - product(z_l[...], first_r[...])

    work = [functools.partial(solve, j) for j in (0, 3)]
    work += [functools.partial(parts, col0, j, 0) for j in (0, 3)]
    work += [functools.partial(apply, j) for j in (0, 3)]
    work += [functools.partial(whiten, 0), down1]
    work += [functools.partial(down, j, 0) for j in (0, 2, 4)]
    leaf(diagonal[...], ones, inv, work)
    inv_r[...] = right(inv[...])
    whiten(1)
    for j in (0, 3):
        col0[j * B : (j + 3) * B, :] = product(left(col1[j * B : (j + 3) * B, :]), inv_r[...])
        parts(col0, j, 1)
    for j in (0, 2, 4):
        down(j, 1)


def second_kernel(core_ref, *refs):
    parts_refs, (stat_ref, first_l, first_rr, x_ref, z_ref), out_refs = refs[:8], refs[8:13], refs[13:17]
    flat, ones, inv, inv_r, diagonal, panel, x, z_l, rows_l, rows_r, white = refs[17:]
    at = PLACE_IN[1]
    gather_chunk(1, core_ref, parts_refs, flat)
    for make in covariance_steps(1, flat, stat_ref[0:8, :], stat_ref[8:16, :]):
        make()
    ones[...] = jnp.ones((8, B), jnp.float32)
    diagonal[...] = flat[0:B, :] - product(first_l[0:B, :], first_rr[0:B, :])

    def start_of(k):
        row = jnp.int32(0)
        for j in range(3, 8):
            row = jnp.where(k == j, at[j, j] * B, row)
        return pl.multiple_of(row, B)

    def update(left_ref, right_ref, skip, j, lo, hi):
        top = min(j + 2, 8)
        change = product(left_ref[(lo - skip) * B : (hi - skip) * B, :], right_ref[(j - skip) * B : (top - skip) * B, :])
        for c in range(j, top):
            first = max(lo, c)
            n, size = at[first, c] * B, (hi - first) * B
            flat[n : n + size, :] = flat[n : n + size, :] - change[(first - lo) * B :, (c - j) * B : (c - j + 1) * B]

    def spans(lo, hi):
        return [(i, min(i + 3, hi)) for i in range(lo, hi, 3)]

    def updates(left_ref, right_ref, skip, low):
        return [
            functools.partial(update, left_ref, right_ref, skip, j, *span) for j in range(low, 8, 2) for span in spans(j, 8)
        ]

    def advance(k):
        inv_r[...] = right(inv[...])
        below = product(left(flat[pl.ds(start_of(k) + B, B), :]), inv_r[...])
        panel[pl.ds(pl.multiple_of((k + 1) * B, B), B), :] = below
        diagonal[...] = flat[pl.ds(start_of(jnp.minimum(k + 1, 7)), B), :] - product(left(below), right(below))

    def take(j):
        x[j] = x_ref[j - 2]

    leaf(diagonal[...], ones, inv, updates(first_l, first_rr, 2, 2) + [functools.partial(take, j) for j in range(2, 8)])
    advance(2)

    def step(low, k):
        def solve(lo, hi):
            size = (hi - lo) * B
            column = flat[pl.ds(start_of(k - 1) + (2 + lo) * B, size), :]
            panel[pl.ds(pl.multiple_of((k + 1 + lo) * B, B), size), :] = product(left(column), inv_r[...])

        def whiten():
            z = product(left(x[k - 1]), inv_r[...])
            white[k - 1] = z
            z_l[...] = left(z)

        def parts(lo, hi):
            new = panel[lo * B : hi * B, :]
            rows_l[lo * B : hi * B, :] = left(new)
            rows_r[lo * B : hi * B, :] = right(new)

        def down(j):
            hi = min(j + 2, 8)
            change = product(z_l[...], rows_r[j * B : hi * B, :])
            for i in range(j, hi):
                x[i] = x[i] - change[:, (i - j) * B : (i - j + 1) * B]

        work = [functools.partial(solve, *span) for span in spans(0, 7 - low)]
        work += [whiten]
        work += [functools.partial(parts, *span) for span in spans(low, 8)]
        work += updates(rows_l, rows_r, 0, low)
        work += [functools.partial(down, j) for j in range(low, 8, 2)]
        leaf(diagonal[...], ones, inv, work)
        advance(k)

    for low, end in ((3, 5), (5, 8)):
        pl.loop(low, end)(functools.partial(step, low))
    white[7] = product(left(x[7]), inv_r[...])
    for k in range(8):
        for g in range(4):
            out_refs[g][:, k * B : (k + 1) * B] = (z_ref if k < 2 else white)[k, g * 64 : (g + 1) * 64, :]


def unpack_kernel(sel_ref, *refs):
    own_refs, other_refs, out_ref = refs[:4], refs[4:8], refs[8]
    sel = sel_ref[...]
    lane = iota((B, 256), 1).astype(jnp.float32)
    place = jnp.where(jnp.concatenate([sel, sel], axis=1) == lane, 1.0, 0.0)
    out_ref[...] = pick(place, jnp.concatenate([r[:32, :] for r in own_refs] + [r[32:, :] for r in other_refs], axis=0))


VMEM = pl.BlockSpec(memory_space=pltpu.VMEM)
SMEM = pl.BlockSpec(memory_space=pltpu.SMEM)


def f32(*shape):
    return jax.ShapeDtypeStruct(shape, jnp.float32)


def call(kernel, outs, args, scratch=(), mib=24, scalars=1, flops=1000000):
    return pl.pallas_call(
        kernel,
        out_shape=outs,
        in_specs=[SMEM] * scalars + [VMEM] * (len(args) - scalars),
        out_specs=jax.tree.map(lambda _: VMEM, outs),
        scratch_shapes=scratch,
        cost_estimate=pl.CostEstimate(flops=flops, bytes_accessed=4000000, transcendentals=0),
        compiler_params=pltpu.CompilerParams(vmem_limit_bytes=mib << 20),
    )(*args)


def whiten(embeddings, domain_ids, order):
    d, w = lax.axis_index("dom"), lax.axis_index("wide")
    home = (w // 8) * 4 + (w % 4) // 2 * 2 + d // 4
    info = (d % 2 + w // 4 % 2 * 2 + w % 2 * 4 + d // 2 % 2 * 8 + home * 16).reshape(1).astype(jnp.int32)

    def swap(x):
        return permute(x, lambda n: partner(n, 3))

    def exchange(arrays):
        return [permute(x, lambda n, turn=turn: toward(n, turn)) for turn, x in enumerate(arrays)]

    ids = domain_ids.reshape(1, B)
    their_rows = swap(embeddings)
    own, sel = call(
        pack_kernel,
        [f32(B, 1024), f32(B, B)],
        (info, jnp.concatenate([ids, order]), embeddings),
        mib=12,
        flops=1000000000,
    )
    rows = exchange(call(merge_kernel, [f32(64, 1024)] * 4, (info, swap(ids), their_rows, own), mib=12))

    def scratch(*shapes, dtype=jnp.float32):
        return [pltpu.VMEM(shape, dtype) for shape in shapes]

    def wide(*shapes):
        return scratch(*shapes, dtype=jnp.bfloat16)

    def gram(chunk):
        half = HALVES[chunk]
        return call(
            functools.partial(gram_kernel, chunk),
            [f32(half, B)] * 2,
            (info, *rows),
            scratch((256, 1024)) + wide((1024, 1536)) + scratch((2 * half, B)),
        )

    def across(x, turn, i):
        return permute(x, lambda n: partner(n, (turn + (2 if i else coords(n)[3])) % 3))

    grams = []
    for chunk in range(2):
        grams.append(gram(chunk))

    def doubled(mine, sent, turn, i):
        theirs = across(sent, turn, i)
        return mine + theirs

    sums, sent = [], []
    for chunk, (mine, other) in enumerate(grams):
        other = swap(other)
        spans = list(zip(CUTS[chunk], CUTS[chunk][1:]))
        kept = [(lo, (lo + hi) // 2 if chunk else hi) for lo, hi in spans]
        sums.append([mine[lo:hi] + other[lo:hi] for lo, hi in kept])
        sent.append([mine[lo:hi] + other[lo:hi] for (_, lo), (_, hi) in zip(kept, spans)] if chunk else sums[0])
    for turn in range(3):
        sums = [[doubled(sums[chunk][i], sent[chunk][i], turn, i) for i in range(2)] for chunk in range(2)]
        sent = sums
    sums[1] = sums[1] + [across(x, 0, i) for i, x in enumerate(sums[1])]
    for parts in sums:
        for x in parts[:]:
            parts.append(swap(x))
    tile, tall = (B, B), (6 * B, B)

    def bf16(*shape):
        return jax.ShapeDtypeStruct(shape, jnp.bfloat16)

    flat, stat, inv, x = call(
        column0_kernel,
        [f32(STAT + 16, B), f32(16, B), f32(*tile), f32(8, 256, B)],
        (info, *sums[0], *rows),
        scratch((8, B)),
        flops=3000000000,
    )
    state = call(
        column1_kernel,
        [bf16(6 * B, 12 * B), bf16(6 * B, 12 * B), f32(6, 256, B), f32(2, 256, B)],
        (flat, inv, x),
        scratch((8, B), tile)
        + wide((B, 6 * B))
        + scratch(tile)
        + wide((B, 6 * B))
        + scratch(tall, tall, (256, B))
        + wide((256, 6 * B)),
        scalars=0,
        flops=3000000000,
    )
    white = call(
        second_kernel,
        [f32(64, 1024)] * 4,
        (info, *sums[1], stat, *state),
        scratch((2 * HALVES[1] + 8 * B, B), (8, B), tile)
        + wide((B, 6 * B))
        + scratch(tile, (14 * B, B), (8, 256, B))
        + wide((256, 6 * B), (8 * B, 6 * B), (8 * B, 6 * B))
        + scratch((8, 256, B)),
        flops=20000000000,
    )
    white = exchange(white)
    return call(unpack_kernel, f32(B, 1024), (sel, *white, *[swap(x) for x in white]), mib=12, scalars=0)


def solution(mesh):
    placed = (P(AXES, None), P(AXES, None), P(AXES, None))
    return jax.shard_map(whiten, mesh=mesh, in_specs=placed, out_specs=P(AXES, None), check_vma=False)
```
